128 devices in a mesh: gx: 4 (over y), gy: 32 (over z, x, core).
Axes of the slice: x: 4, y: 4, z: 4, core: 2. Of those that a mesh axis runs over, the one named last changes fastest.
Arguments:
- positions: float32 [3, 2097152], P(None, ('gx', 'gy')), may hold values from -6 to 6
- normals: float32 [3, 2097152], P(None, ('gx', 'gy')), may hold values from -6 to 6
- areas: float32 [2097152], P(('gx', 'gy')), may hold values from 0.5 to 2
- pair_first: int32 [16384], P(('gx', 'gy')), may hold values from 0 to 8191, as said below
- pair_second: int32 [16384], P(('gx', 'gy')), may hold values from 0 to 8191, as said below
- pair_count: int32 [128], P(('gx', 'gy')), may hold values from 32 to 128, as said below
Outputs:
- gradient: float32 [3, 2097152], P(None, ('gx', 'gy'))
The draws below stay inside these ranges and needn't reach their ends.
Inputs may be any that keep to these rules, and one draw needn't show every extreme that they name: `pair_first`: slot s holds a first cluster owned by device s // 128, that is in s // 128 * 64 to (s // 128 + 1) * 64 - 1. `pair_second`: the second cluster of slot s lies on a device at most 2 away from s // 128: its index // 64 differs from s // 128 by at most 2. Dead slots hold such pairs too. `pair_count`: some device has all 128 slots live in every draw.
All inputs are finite; a program needn't handle non-finite values.
Results may differ from the reference program's by a relative error of at most 0.0001.
Values sent between devices are 32-bit elements; how exact they have to be, the bound alone decides.
A program may use at most 64 MiB of HBM per device.

```python
import math
import jax
import jax.numpy as jnp
from jax import lax

C = 256
CL_DEV = 64
PAIR_CAP = 128
REACH = 2
BLOCK = 4
NC = 8192
FACES = 2097152


def draw_pair_first(key, part):
    devices = NC // CL_DEV
    total = devices * PAIR_CAP
    owner = jnp.arange(total, dtype=jnp.int32) // PAIR_CAP
    local = jax.random.randint(jax.random.fold_in(key, 11), (total,), 0, CL_DEV, dtype=jnp.int32)
    return (owner * CL_DEV + local).astype(jnp.int32)


def draw_pair_second(key, part):
    devices = NC // CL_DEV
    total = devices * PAIR_CAP
    owner = jnp.arange(total, dtype=jnp.int32) // PAIR_CAP
    offset = jax.random.randint(jax.random.fold_in(key, 23), (total,), -REACH, REACH + 1, dtype=jnp.int32)
    target = jnp.clip(owner + offset, 0, devices - 1)
    local = jax.random.randint(jax.random.fold_in(key, 37), (total,), 0, CL_DEV, dtype=jnp.int32)
    return (target * CL_DEV + local).astype(jnp.int32)


def draw_pair_count(key, part):
    devices = NC // CL_DEV
    level = jax.random.randint(jax.random.fold_in(key, 41), (devices,), 0, 8, dtype=jnp.int32)
    fullest = jax.random.randint(jax.random.fold_in(key, 53), (), 0, devices, dtype=jnp.int32)
    level = jnp.where(jnp.arange(devices, dtype=jnp.int32) == fullest, 7, level)
    lowest = PAIR_CAP // 4
    return (lowest + (PAIR_CAP - lowest) * level * level // 49).astype(jnp.int32)


def block_levels(key, extent, split, low, high):
    level = 1.0
    for axis_at, shards_of in split:
        draws = jax.random.uniform(jax.random.fold_in(jax.random.fold_in(key, 6), axis_at), (shards_of,), jnp.float32, low / len(split), high / len(split))
        level = level * jnp.repeat(jnp.exp(draws), extent[axis_at] // shards_of).reshape((-1,) + (1,) * (len(extent) - 1 - axis_at))
    return level


def gaussian(rng, shape, spread, bound, cuts=(), held_as=jnp.bfloat16):
    array = jax.random.normal(rng, shape, jnp.float32) * spread
    if len(cuts) > 0:
        array = block_levels(rng, shape, cuts, -0.22, 0.18) * array
    return jnp.clip(array, min=-bound, max=bound).astype(held_as)


def setup_inputs(seed: int = 0) -> dict:
    key_of = jax.random.split(jax.random.key(seed), 7)
    positions = gaussian(key_of[0], (3, FACES), 1.0, 6.0, ((1, 128),), jnp.float32)
    normals = gaussian(key_of[1], (3, FACES), 1.0, 6.0, ((1, 128),), jnp.float32)
    areas = jnp.clip(jnp.exp(math.log(2.0) - 1.3862944 * jax.random.uniform(key_of[2], (FACES,), jnp.float32) ** block_levels(key_of[2], (FACES,), ((0, 128),), -0.2, 0.2)), 0.5, 2.0)
    pair_first = draw_pair_first(jax.random.fold_in(key_of[6], 71), 0)
    pair_second = draw_pair_second(jax.random.fold_in(key_of[6], 71), 0)
    pair_count = draw_pair_count(jax.random.fold_in(key_of[6], 71), 0)
    return {"positions": positions, "normals": normals, "areas": areas, "pair_first": pair_first, "pair_second": pair_second, "pair_count": pair_count}


def tile_terms(pos_f, nor_f, area_f, pos_g, nor_g, area_g):
    delta = [pos_f[:, k, :, None] - pos_g[:, k, None, :] for k in range(3)]
    radius = delta[0] * delta[0] + delta[1] * delta[1] + delta[2] * delta[2] + 1.0
    inverse = 1.0 / radius
    weight = area_f[:, :, None] * area_g[:, None, :] * inverse * inverse * inverse
    along_f = nor_f[:, 0, :, None] * delta[0] + nor_f[:, 1, :, None] * delta[1] + nor_f[:, 2, :, None] * delta[2]
    along_g = nor_g[:, 0, None, :] * delta[0] + nor_g[:, 1, None, :] * delta[1] + nor_g[:, 2, None, :] * delta[2]
    linear_f = 2.0 * weight * along_f
    linear_g = 2.0 * weight * along_g
    radial = -6.0 * weight * inverse * (along_f * along_f + along_g * along_g)
    grad_first = []
    grad_second = []
    for k in range(3):
        comp = linear_f * nor_f[:, k, :, None] + linear_g * nor_g[:, k, None, :] + radial * delta[k]
        grad_first.append(jnp.sum(comp, axis=2))
        grad_second.append(-jnp.sum(comp, axis=1))
    return jnp.stack(grad_first, axis=1), jnp.stack(grad_second, axis=1)


def reference(positions, normals, areas, pair_first, pair_second, pair_count):
    pos = positions.reshape(3, NC, C).transpose(1, 0, 2)
    nor = normals.reshape(3, NC, C).transpose(1, 0, 2)
    area = areas.reshape(NC, C)
    total = pair_first.shape[0]
    slots = jnp.arange(total, dtype=jnp.int32)
    owners = slots // PAIR_CAP
    live = ((slots % PAIR_CAP) < pair_count[owners]).astype(jnp.float32)
    firsts = pair_first.reshape(total // BLOCK, BLOCK)
    seconds = pair_second.reshape(total // BLOCK, BLOCK)
    lives = live.reshape(total // BLOCK, BLOCK)

    def step(grad, inputs):
        first, second, alive = inputs
        grad_first, grad_second = tile_terms(pos[first], nor[first], area[first], pos[second], nor[second], area[second])
        grad = grad.at[first].add(grad_first * alive[:, None, None])
        grad = grad.at[second].add(grad_second * alive[:, None, None])
        return grad, None

    start = jnp.zeros((NC, 3, C), jnp.float32)
    grad, unused = lax.scan(step, start, (firsts, seconds, lives))
    return grad.transpose(1, 0, 2).reshape(3, NC * C)
```

```python
import jax
import jax.numpy as jnp
from jax import lax
from jax.experimental import pallas as pl
from jax.experimental.pallas import tpu as pltpu
from jax.sharding import PartitionSpec as P

C = 256
REACH = 2
F32 = jnp.float32
BF = jnp.bfloat16


def split3(t):
    a = t.astype(BF).astype(F32)
    r = t - a
    b = r.astype(BF).astype(F32)
    return a, b, r - b


def split2(t):
    a = t.astype(BF).astype(F32)
    return a, t - a


def wide(v):
    return jnp.broadcast_to(v, (8, C))


def prep(f, g, alive, lhs_ref, rhs_ref, wf_ref, wg_ref, keep_ref):
    row = lax.broadcasted_iota(jnp.int32, (8, C), 0)
    isp = row < 3
    isn = (row >= 3) & (row < 6)
    ctr = jnp.where(isp, wide(jnp.sum(f, axis=1, keepdims=True) * (1.0 / C)), 0.0)
    f = f - ctr
    g = g - ctr

    def dots(t):
        p = jnp.where(isp, t, 0.0)
        n = jnp.where(isp, pltpu.roll(t, 5, 0), 0.0)
        return p, n, wide(jnp.sum(p * p, axis=0, keepdims=True)), wide(jnp.sum(p * n, axis=0, keepdims=True))

    pf, nf, sf, cf = dots(f)
    pg, ng, sg, cg = dots(g)
    one = jnp.ones((8, C), F32)
    zero = jnp.zeros((8, C), F32)
    a0, a1, a2 = split3(jnp.where(row < 6, f, jnp.where(row == 6, sf + 1.0, cf)))
    lhs_ref[...] = jnp.concatenate([a0, a0, a0, a1, a1, a2, one, zero], axis=0).T.astype(BF)
    tr = jnp.where(isp, -2.0 * g, jnp.where(row == 6, 1.0, 0.0))
    ts = jnp.where(isn, -pltpu.roll(g, 3, 0), jnp.where(row == 7, 1.0, 0.0))

    def rows3(u):
        return jnp.where(row == 0, u[0], jnp.where(row == 1, u[1], jnp.where(row == 2, u[2], 0.0)))

    lasts = (rows3(split3(sg)), zero, rows3(split3(-cg)))
    for j, t in enumerate((tr, ts, ng)):
        u0, u1, u2 = split3(t)
        rhs_ref[:, j * C : (j + 1) * C] = jnp.concatenate([u0, u1, u2, u0, u1, u0, lasts[j], zero], axis=0).astype(BF)
    af = wide(f[6:7, :])
    ag = wide(g[6:7, :])
    af2 = af * (2.0 * alive)
    ag2 = ag * (2.0 * alive)

    def put(ref, vs):
        for j, v in enumerate(vs):
            ref[j] = jnp.concatenate(split2(v), axis=0).astype(BF)

    put(wf_ref, (nf * af2, jnp.where(row == 3, af2, 0.0), (-3.0 * pf + jnp.where(row == 4, 3.0, 0.0)) * af2))
    put(wg_ref, (jnp.where(row == 3, ag2, 0.0), ng * ag2, (3.0 * pg - jnp.where(row == 4, 3.0, 0.0)) * ag2))
    for i, v in enumerate((nf, pf, af, ng, pg, ag)):
        keep_ref[i] = v


def forward(lhs_ref, rhs_ref, l_ref, rows):
    for i in range(C // rows):
        sl = slice(i * rows, (i + 1) * rows)
        left = lhs_ref[sl, :]
        r2, sf, sg = (jnp.dot(left, rhs_ref[:, j * C : (j + 1) * C], preferred_element_type=F32) for j in range(3))
        inv = 1.0 / r2
        inv3 = inv * inv * inv
        lf = inv3 * sf
        lg = inv3 * sg
        rad = inv * (lf * sf + lg * sg)
        for j, v in enumerate((lf, lg, rad)):
            h = v.astype(BF)
            l_ref[j, sl, :] = h
            l_ref[j + 3, sl, :] = (v - h.astype(F32)).astype(BF)


def sums(l_ref, wf_ref, wg_ref, keep_ref):
    cs = None
    rs = None
    for j in range(6):
        tile = l_ref[j]
        a = lax.dot_general(wf_ref[j % 3], tile, (((1,), (0,)), ((), ())), preferred_element_type=F32)
        b = lax.dot_general(wg_ref[j % 3], tile, (((1,), (1,)), ((), ())), preferred_element_type=F32)
        cs = a if cs is None else cs + a
        rs = b if rs is None else rs + b
    cs = cs[0:8] + cs[8:16]
    rs = rs[0:8] + rs[8:16]
    nf, pf, af, ng, pg, ag = (keep_ref[i] for i in range(6))
    gf = af * (rs + nf * wide(rs[3:4]) + pf * wide(rs[4:5]))
    gg = -ag * (cs + ng * wide(cs[3:4]) + pg * wide(cs[4:5]))
    return gf, gg


def near_field(first, second, count, geos):
    nwin = len(geos)
    faces = geos[0].shape[1]

    def kernel(first, second, count, *refs):
        geo = refs[:nwin]
        outs = refs[nwin : 2 * nwin]
        r = list(refs[2 * nwin :])
        win = r.pop(0)
        acc = r.pop(0)
        bufs = [[r.pop(0) for _ in range(6)] for _ in range(2)]
        sem = r.pop(0)
        copies = [
            pltpu.make_async_copy(geo[k], win.at[:, pl.ds(k * faces, faces)], sem.at[k]) for k in range(nwin)
        ]
        for c in copies:
            c.start()
        acc[...] = jnp.zeros_like(acc)
        for c in copies:
            c.wait()
        n = count[0]

        def ds(c):
            return pl.ds(pl.multiple_of(c * C, C), C)

        def step(i, carry):
            for u in range(2):
                p = 2 * i + u
                prep(win[:, ds(first[p])], win[:, ds(second[p])], jnp.where(p < n, 1.0, 0.0).astype(F32), *bufs[u][:5])
            for u in range(2):
                forward(bufs[u][0], bufs[u][1], bufs[u][5], 32)
            for u in range(2):
                p = 2 * i + u
                gf, gg = sums(bufs[u][5], bufs[u][2], bufs[u][3], bufs[u][4])
                acc[:, ds(first[p])] += gf
                acc[:, ds(second[p])] += gg
            return carry

        lax.fori_loop(0, (n + 1) // 2, step, 0)
        for k in range(nwin):
            outs[k][...] = acc[0:3, k * faces : (k + 1) * faces]

    buf = [
        pltpu.VMEM((C, 64), BF),
        pltpu.VMEM((64, 3 * C), BF),
        pltpu.VMEM((3, 16, C), BF),
        pltpu.VMEM((3, 16, C), BF),
        pltpu.VMEM((6, 8, C), F32),
        pltpu.VMEM((6, C, C), BF),
    ]
    return pl.pallas_call(
        kernel,
        out_shape=[jax.ShapeDtypeStruct((3, faces), F32)] * nwin,
        in_specs=[pl.BlockSpec(memory_space=pltpu.SMEM)] * 3 + [pl.BlockSpec(memory_space=pl.ANY)] * nwin,
        out_specs=[pl.BlockSpec(memory_space=pltpu.VMEM)] * nwin,
        scratch_shapes=[pltpu.VMEM((8, nwin * faces), F32)] * 2 + buf + buf + [pltpu.SemaphoreType.DMA((nwin,))],
        compiler_params=pltpu.CompilerParams(vmem_limit_bytes=40 * 2**20),
    )(first, second, count, *geos)


def shifted(value, axis, by):
    size = 1
    for a in axis:
        size *= lax.axis_size(a)
    return lax.ppermute(value, axis, [(i, i + by) for i in range(size) if 0 <= i + by < size])


def body(positions, normals, areas, pair_first, pair_second, pair_count):
    faces = areas.shape[0]
    clusters = faces // C
    axis = ("gx", "gy")
    geometry = jnp.concatenate([positions, normals, areas[None, :], jnp.zeros((1, faces), F32)], axis=0)
    geos = [geometry if k == 0 else shifted(geometry, axis, -k) for k in range(-REACH, REACH + 1)]
    base = (lax.axis_index(axis) - REACH) * clusters
    outs = near_field(pair_first - base, pair_second - base, pair_count, geos)
    owned = outs[REACH]
    for k in range(-REACH, REACH + 1):
        if k != 0:
            owned = owned + shifted(outs[k + REACH], axis, k)
    return owned


def solution(mesh):
    flat = P(("gx", "gy"))
    deep = P(None, ("gx", "gy"))
    return jax.shard_map(
        body, mesh=mesh, in_specs=(deep, deep, flat, flat, flat, flat), out_specs=deep, check_vma=False
    )
```

```python
import jax
import jax.numpy as jnp
from jax import lax
from jax.experimental import pallas as pl
from jax.experimental.pallas import tpu as pltpu
from jax.sharding import PartitionSpec as P

C = 256
REACH = 2
F32 = jnp.float32
BF = jnp.bfloat16


def split3(t):
    a = t.astype(BF).astype(F32)
    r = t - a
    b = r.astype(BF).astype(F32)
    return a, b, r - b


def split2(t):
    a = t.astype(BF).astype(F32)
    return a, t - a


def wide(v):
    return jnp.broadcast_to(v, (8, C))


def prep(f, g, alive, lhs_ref, rhs_ref, wf_ref, wg_ref, keep_ref):
    row = lax.broadcasted_iota(jnp.int32, (8, C), 0)
    isp = row < 3
    isn = (row >= 3) & (row < 6)
    ctr = jnp.where(isp, wide(jnp.sum(f, axis=1, keepdims=True) * (1.0 / C)), 0.0)
    f = f - ctr
    g = g - ctr

    def dots(t):
        p = jnp.where(isp, t, 0.0)
        n = jnp.where(isp, pltpu.roll(t, 5, 0), 0.0)
        return p, n, wide(jnp.sum(p * p, axis=0, keepdims=True)), wide(jnp.sum(p * n, axis=0, keepdims=True))

    pf, nf, sf, cf = dots(f)
    pg, ng, sg, cg = dots(g)
    one = jnp.ones((8, C), F32)
    zero = jnp.zeros((8, C), F32)
    a0, a1, a2 = split3(jnp.where(row < 6, f, jnp.where(row == 6, sf + 1.0, cf)))
    lhs_ref[...] = jnp.concatenate([a0, a0, a0, a1, a1, a2, one, zero], axis=0).T.astype(BF)
    tr = jnp.where(isp, -2.0 * g, jnp.where(row == 6, 1.0, 0.0))
    ts = jnp.where(isn, -pltpu.roll(g, 3, 0), jnp.where(row == 7, 1.0, 0.0))

    def rows3(u):
        return jnp.where(row == 0, u[0], jnp.where(row == 1, u[1], jnp.where(row == 2, u[2], 0.0)))

    lasts = (rows3(split3(sg)), zero, rows3(split3(-cg)))
    for j, t in enumerate((tr, ts, ng)):
        u0, u1, u2 = split3(t)
        rhs_ref[:, j * C : (j + 1) * C] = jnp.concatenate([u0, u1, u2, u0, u1, u0, lasts[j], zero], axis=0).astype(BF)
    af = wide(f[6:7, :])
    ag = wide(g[6:7, :])
    af2 = af * (2.0 * alive)
    ag2 = ag * (2.0 * alive)

    def put(ref, vs):
        for j, v in enumerate(vs):
            ref[j] = jnp.concatenate(split2(v), axis=0).astype(BF)

    put(wf_ref, (nf * af2, jnp.where(row == 3, af2, 0.0), (-3.0 * pf + jnp.where(row == 4, 3.0, 0.0)) * af2))
    put(wg_ref, (jnp.where(row == 3, ag2, 0.0), ng * ag2, (3.0 * pg - jnp.where(row == 4, 3.0, 0.0)) * ag2))
    for i, v in enumerate((nf, pf, af, ng, pg, ag)):
        keep_ref[i] = v


def forward(lhs_ref, rhs_ref, l_ref, rows):
    for i in range(C // rows):
        sl = slice(i * rows, (i + 1) * rows)
        left = lhs_ref[sl, :]
        r2, sf, sg = (jnp.dot(left, rhs_ref[:, j * C : (j + 1) * C], preferred_element_type=F32) for j in range(3))
        inv = 1.0 / r2
        inv3 = inv * inv * inv
        lf = inv3 * sf
        lg = inv3 * sg
        rad = inv * (lf * sf + lg * sg)
        for j, v in enumerate((lf, lg, rad)):
            h = v.astype(BF)
            l_ref[j, sl, :] = h
            l_ref[j + 3, sl, :] = (v - h.astype(F32)).astype(BF)


def sums(l_ref, wf_ref, wg_ref, keep_ref):
    cs = None
    rs = None
    for j in range(6):
        tile = l_ref[j]
        a = lax.dot_general(wf_ref[j % 3], tile, (((1,), (0,)), ((), ())), preferred_element_type=F32)
        b = lax.dot_general(wg_ref[j % 3], tile, (((1,), (1,)), ((), ())), preferred_element_type=F32)
        cs = a if cs is None else cs + a
        rs = b if rs is None else rs + b
    cs = cs[0:8] + cs[8:16]
    rs = rs[0:8] + rs[8:16]
    nf, pf, af, ng, pg, ag = (keep_ref[i] for i in range(6))
    gf = af * (rs + nf * wide(rs[3:4]) + pf * wide(rs[4:5]))
    gg = -ag * (cs + ng * wide(cs[3:4]) + pg * wide(cs[4:5]))
    return gf, gg


def near_field(first, second, count, geos):
    nwin = len(geos)
    faces = geos[0].shape[1]

    def kernel(first, second, count, *refs):
        geo = refs[:nwin]
        outs = refs[nwin : 2 * nwin]
        r = list(refs[2 * nwin :])
        win = r.pop(0)
        acc = r.pop(0)
        bufs = [[r.pop(0) for _ in range(6)] for _ in range(2)]
        sem = r.pop(0)
        copies = [
            pltpu.make_async_copy(geo[k], win.at[:, pl.ds(k * faces, faces)], sem.at[k]) for k in range(nwin)
        ]
        for c in copies:
            c.start()
        acc[...] = jnp.zeros_like(acc)
        for c in copies:
            c.wait()
        n = count[0]

        def ds(c):
            return pl.ds(pl.multiple_of(c * C, C), C)

        def step(i, carry):
            for u in range(2):
                p = 2 * i + u
                prep(win[:, ds(first[p])], win[:, ds(second[p])], jnp.where(p < n, 1.0, 0.0).astype(F32), *bufs[u][:5])
            for u in range(2):
                forward(bufs[u][0], bufs[u][1], bufs[u][5], 32)
            for u in range(2):
                p = 2 * i + u
                gf, gg = sums(bufs[u][5], bufs[u][2], bufs[u][3], bufs[u][4])
                acc[:, ds(first[p])] += gf
                acc[:, ds(second[p])] += gg
            return carry

        lax.fori_loop(0, (n + 1) // 2, step, 0)
        for k in range(nwin):
            outs[k][...] = acc[0:3, k * faces : (k + 1) * faces]

    buf = [
        pltpu.VMEM((C, 64), BF),
        pltpu.VMEM((64, 3 * C), BF),
        pltpu.VMEM((3, 16, C), BF),
        pltpu.VMEM((3, 16, C), BF),
        pltpu.VMEM((6, 8, C), F32),
        pltpu.VMEM((6, C, C), BF),
    ]
    return pl.pallas_call(
        kernel,
        out_shape=[jax.ShapeDtypeStruct((3, faces), F32)] * nwin,
        in_specs=[pl.BlockSpec(memory_space=pltpu.SMEM)] * 3 + [pl.BlockSpec(memory_space=pl.ANY)] * nwin,
        out_specs=[pl.BlockSpec(memory_space=pltpu.VMEM)] * nwin,
        scratch_shapes=[pltpu.VMEM((8, nwin * faces), F32)] * 2 + buf + buf + [pltpu.SemaphoreType.DMA((nwin,))],
        compiler_params=pltpu.CompilerParams(vmem_limit_bytes=40 * 2**20),
    )(first, second, count, *geos)


MESH = pl.DeviceIdType.MESH


def place(flat):
    inner = lax.axis_size("gy")
    total = lax.axis_size("gx") * inner
    flat = (flat + total) % total
    return (flat // inner, flat % inner)


def greet(devices):
    barrier = pltpu.get_barrier_semaphore()
    for d in devices:
        pl.semaphore_signal(barrier, inc=1, device_id=d, device_id_type=MESH)
    pl.semaphore_wait(barrier, len(devices))


def gather(geometry, rows, chunks):
    faces = geometry.shape[1]
    part = faces // chunks

    def kernel(own, low, far, sib, high, send, recv):
        me = lax.axis_index("gx") * lax.axis_size("gy") + lax.axis_index("gy")
        odd = me % 2
        up, down, other = place(me + 2), place(me - 2), place(me + 1 - 2 * odd)
        greet((up, down, other))

        def move(kind, i, src, dst, device):
            sl = (pl.ds(0, rows), pl.ds(i * part, part))
            return pltpu.make_async_remote_copy(
                src_ref=src.at[sl],
                dst_ref=dst.at[sl],
                send_sem=send.at[kind, i],
                recv_sem=recv.at[kind, i],
                device_id=device,
                device_id_type=MESH,
            )

        for i in range(chunks):
            move(0, i, own, low, up).start()
            move(1, i, own, high, down).start()
        for i in range(chunks):
            move(2, i, own, sib, other).start()
        for i in range(chunks):
            move(0, i, own, low, up).wait_recv()
            move(1, i, own, high, down).wait_recv()

            @pl.when(odd == 0)
            def _():
                move(3, i, high, far, other).start()

            @pl.when(odd == 1)
            def _():
                move(3, i, low, far, other).start()

        for i in range(chunks):
            move(2, i, own, sib, other).wait_recv()
            move(3, i, own, far, other).wait_recv()
        for i in range(chunks):
            move(0, i, own, low, up).wait_send()
            move(1, i, own, high, down).wait_send()
            move(2, i, own, sib, other).wait_send()
            move(3, i, own, far, other).wait_send()

    return pl.pallas_call(
        kernel,
        out_shape=[jax.ShapeDtypeStruct((8, faces), F32)] * 4,
        in_specs=[pl.BlockSpec(memory_space=pl.ANY)],
        out_specs=[pl.BlockSpec(memory_space=pl.ANY)] * 4,
        scratch_shapes=[pltpu.SemaphoreType.DMA((4, chunks)), pltpu.SemaphoreType.DMA((4, chunks))],
        compiler_params=pltpu.CompilerParams(collective_id=0, has_side_effects=True),
    )(geometry)


def give_back(own, low, far, sib, high):
    faces = own.shape[1]

    def kernel(own, low, far, sib, high, out, box, send, recv):
        me = lax.axis_index("gx") * lax.axis_size("gy") + lax.axis_index("gy")
        odd = me % 2
        targets = (place(me - 2), place(me - 1 + 2 * odd), place(me + 1 - 2 * odd), place(me + 2))
        greet(targets)
        copies = [
            pltpu.make_async_remote_copy(
                src_ref=src,
                dst_ref=box.at[k],
                send_sem=send.at[k],
                recv_sem=recv.at[k],
                device_id=device,
                device_id_type=MESH,
            )
            for k, (src, device) in enumerate(zip((low, far, sib, high), targets, strict=True))
        ]
        for k in (0, 3, 1, 2):
            copies[k].start()
        total = own[...]
        for k in (2, 1, 0, 3):
            copies[k].wait_recv()
        out[...] = total + ((box[0] + box[3]) + (box[1] + box[2]))
        for c in copies:
            c.wait_send()

    return pl.pallas_call(
        kernel,
        out_shape=jax.ShapeDtypeStruct((3, faces), F32),
        in_specs=[pl.BlockSpec(memory_space=pltpu.VMEM)] * 5,
        out_specs=pl.BlockSpec(memory_space=pltpu.VMEM),
        scratch_shapes=[
            pltpu.VMEM((4, 3, faces), F32),
            pltpu.SemaphoreType.DMA((4,)),
            pltpu.SemaphoreType.DMA((4,)),
        ],
        compiler_params=pltpu.CompilerParams(collective_id=1, has_side_effects=True),
    )(own, low, far, sib, high)


def body(positions, normals, areas, pair_first, pair_second, pair_count):
    faces = areas.shape[0]
    clusters = faces // C
    me = lax.axis_index(("gx", "gy"))
    geometry = jnp.concatenate([positions, normals, areas[None, :], jnp.zeros((1, faces), F32)], axis=0)
    low, far, sib, high = gather(geometry, 8, 4)
    first = pair_first - (me - REACH) * clusters
    reach = pair_second // clusters - me
    slot = REACH + jnp.where(jnp.abs(reach) == 1, reach * (1 - 2 * (me % 2)), reach)
    second = slot * clusters + pair_second % clusters
    outs = near_field(first, second, pair_count, [low, far, geometry, sib, high])
    return give_back(outs[2], outs[0], outs[1], outs[3], outs[4])


def solution(mesh):
    flat = P(("gx", "gy"))
    deep = P(None, ("gx", "gy"))
    return jax.shard_map(
        body, mesh=mesh, in_specs=(deep, deep, flat, flat, flat, flat), out_specs=deep, check_vma=False
    )
```

```python
import jax
import jax.numpy as jnp
from jax import lax
from jax.experimental import pallas as pl
from jax.experimental.pallas import tpu as pltpu
from jax.sharding import PartitionSpec as P

C = 256
REACH = 2
F32 = jnp.float32
BF = jnp.bfloat16
MESH = pl.DeviceIdType.MESH
VMEM_LIMIT = 60 * 2**20


def split3(t):
    a = t.astype(BF).astype(F32)
    r = t - a
    b = r.astype(BF).astype(F32)
    return a, b, r - b


def split2(t):
    a = t.astype(BF).astype(F32)
    return a, t - a


def wide(v):
    return jnp.broadcast_to(v, (8, C))


def row_index():
    return lax.broadcasted_iota(jnp.int32, (8, C), 0)


def prep(f, g, lhs_ref, rhs_ref, w_ref, keep_ref):
    row = row_index()
    isp = row < 3

    def at(k, v):
        return jnp.where(row == k, v, 0.0)

    af = wide(f[6:7, :])
    ag = wide(g[6:7, :])
    ctr = jnp.where(isp, wide(jnp.sum(f, axis=1, keepdims=True) * (1.0 / C)), 0.0)

    def parts(t):
        p = jnp.where(isp, t - ctr, 0.0)
        n = jnp.where(isp, pltpu.roll(t, 5, 0), 0.0)
        return p, n, wide(jnp.sum(p * p, axis=0, keepdims=True)), wide(jnp.sum(p * n, axis=0, keepdims=True))

    pf, nf, sf, cf = parts(f)
    pg, ng, sg, cg = parts(g)
    iaf = 1.0 / af
    iag = 1.0 / ag

    def left(t):
        u0, u1, u2 = split3(t)
        return jnp.concatenate([u0, u0, u0, u1, u1, u2], axis=0).T.astype(BF)

    def right(t):
        u0, u1, u2 = split3(t)
        return jnp.concatenate([u0, u1, u2, u0, u1, u0], axis=0).astype(BF)

    lhs_ref[0] = left(pf + at(3, sf + 1.0) + at(4, 1.0))
    lhs_ref[1] = left(af * (nf + at(3, cf) + pltpu.roll(pf, 4, 0) + at(7, 1.0)))
    rhs_ref[0] = right(-2.0 * pg + at(3, 1.0) + at(4, sg))
    rhs_ref[1] = right(ag * (at(3, 1.0) - pg))
    rhs_ref[2] = right(ag * (pltpu.roll(ng, 4, 0) - at(7, cg)))
    sums = (2.0 * nf, iaf * (at(6, 6.0) - 6.0 * pltpu.roll(pf, 3, 0)), iag * (6.0 * pg - at(3, 6.0)))
    for j, v in enumerate(sums):
        w_ref[j] = jnp.concatenate(split2(v), axis=0).astype(BF)
    for i, v in enumerate((nf, pf, iaf, ng, pg, iag)):
        keep_ref[i] = v


def terms(base, rows, sub, n, cs, lhs_ref, rhs_ref, l_ref, x_ref):
    def half(v):
        return v[:, :128] + v[:, 128:]

    big = slice(base, base + rows)
    left = lhs_ref[1, big, :]
    all_r2 = jnp.dot(lhs_ref[0, big, :], rhs_ref[0], preferred_element_type=F32)
    all_sf = jnp.dot(left, rhs_ref[1], preferred_element_type=F32)
    all_sg = jnp.dot(left, rhs_ref[2], preferred_element_type=F32)
    for s in range(0, rows, sub):
        sl = slice(base + s, base + s + sub)
        q = slice(s, s + sub)
        inv = 1.0 / all_r2[q]
        sf = all_sf[q]
        sg = all_sg[q]
        inv3 = inv * inv * inv
        lf = inv3 * sf
        lg = inv3 * sg
        rad = inv * (lf * sf + lg * sg)
        for j, v in ((0, lf), (2, rad)):
            h = v.astype(BF)
            l_ref[j, sl, :] = h
            l_ref[j + 1, sl, :] = (v - h.astype(F32)).astype(BF)
        for t in range(0, sub, 8):
            o = slice(t, t + 8)
            so = slice(base + s + t, base + s + t + 8)
            cs = cs + lg[o]
            x_ref[3, so, :] = half(lf[o])
            for k in range(3):
                x_ref[k, so, :] = half(lg[o] * n[k])
    return cs


def along(w, tile):
    return lax.dot_general(w, tile, (((1,), (0,)), ((), ())), preferred_element_type=F32)


def across(w, tile):
    return lax.dot_general(w, tile, (((1,), (1,)), ((), ())), preferred_element_type=F32)


def stage(h, now, before, ws, ks, load, save, rows=64, sub=16):
    lhs, rhs, w, keep, tiles, x, csr = now
    w_b, keep_b, tiles_b, x_b, csr_b = before[2:]
    ws[...] = w_b[...]
    ks[...] = keep_b[...]
    normal = [wide(keep[3, k : k + 1, :]) for k in range(3)]
    cs = jnp.zeros((8, C), F32)
    xs = [[None, None] for _ in range(4)]
    col = []
    rsum = []
    count = C // rows
    for c in range(count):
        cs = terms(c * rows, rows, sub, normal, cs, lhs, rhs, tiles, x)
        for e in range(c * 8 // count, (c + 1) * 8 // count):
            k, s = e // 2, e % 2
            xs[k][s] = jnp.sum(x_b[k, s * 128 : (s + 1) * 128, :].T, axis=0, keepdims=True)
            if e < 4:
                col.append(along(ws[e // 2], tiles_b[e]))
            elif e < 6:
                rsum.append(across(ws[2], tiles_b[e - 2]))
        if c == count // 2 - 1:
            prep(*load(h + 1), *before[:4])
    csr_old = csr_b[...]
    csr[...] = cs
    row = row_index()
    ct = (col[0] + col[1]) + (col[2] + col[3])
    rt = rsum[0] + rsum[1]
    ct = ct[0:8] + ct[8:16]
    rt = rt[0:8] + rt[8:16]
    nf, pf, iaf, ng, pg, iag = (ks[i] for i in range(6))
    xv = [wide(jnp.concatenate(v, axis=1)) for v in xs]
    lean = jnp.where(row == 0, xv[0], jnp.where(row == 1, xv[1], xv[2]))
    gf = 2.0 * (nf * xv[3] + lean) + iaf * (rt + pf * wide(rt[3:4]))
    csum = wide(jnp.sum(csr_old, axis=0, keepdims=True))
    gg = -(ct + ng * (2.0 * csum) + iag * (pltpu.roll(ct, 5, 0) + pg * wide(ct[6:7])))
    save(h - 1, gf, gg)


STAGE = [
    pltpu.VMEM((2, C, 48), BF),
    pltpu.VMEM((3, 48, C), BF),
    pltpu.VMEM((3, 16, C), BF),
    pltpu.VMEM((6, 8, C), F32),
    pltpu.VMEM((4, C, C), BF),
    pltpu.VMEM((4, C, 128), F32),
    pltpu.VMEM((8, C), F32),
]
KEPT = [pltpu.VMEM((3, 16, C), BF), pltpu.VMEM((6, 8, C), F32)]


def lanes(c):
    return pl.ds(pl.multiple_of(c * C, C), C)


def near_field(first, second, count, geos):
    nwin = len(geos)
    faces = geos[0].shape[1]
    slots = first.shape[0]

    def kernel(first, second, count, *refs):
        geo = refs[:nwin]
        outs = refs[nwin : 2 * nwin]
        win, acc = refs[2 * nwin : 2 * nwin + 2]
        even = refs[2 * nwin + 2 : 2 * nwin + 9]
        odd = refs[2 * nwin + 9 : 2 * nwin + 16]
        ws, ks, sem = refs[2 * nwin + 16 :]
        copies = [
            pltpu.make_async_copy(geo[k], win.at[:, pl.ds(k * faces, faces)], sem.at[k]) for k in range(nwin)
        ]
        for c in copies:
            c.start()
        acc[...] = jnp.zeros_like(acc)
        for c in copies:
            c.wait()
        n = count[0]

        def load(h):
            q = jnp.minimum(h, slots - 1)
            return win[:, lanes(first[q])], win[:, lanes(second[q])]

        def save(h, gf, gg):
            live = (h >= 0) & (h < n)
            q = jnp.clip(h, 0, slots - 1)
            fi = lanes(first[q])
            si = lanes(second[q])
            acc[:, fi] += jnp.where(live, gf, 0.0)
            acc[:, si] += jnp.where(live, gg, 0.0)

        prep(*load(0), *even[:4])

        def step(i, carry):
            stage(2 * i, even, odd, ws, ks, load, save)
            stage(2 * i + 1, odd, even, ws, ks, load, save)
            return carry

        lax.fori_loop(0, (n + 2) // 2, step, 0)
        for k in range(nwin):
            outs[k][...] = acc[0:3, k * faces : (k + 1) * faces]

    return pl.pallas_call(
        kernel,
        out_shape=[jax.ShapeDtypeStruct((3, faces), F32)] * nwin,
        in_specs=[pl.BlockSpec(memory_space=pltpu.SMEM)] * 3 + [pl.BlockSpec(memory_space=pl.ANY)] * nwin,
        out_specs=[pl.BlockSpec(memory_space=pltpu.VMEM)] * nwin,
        scratch_shapes=[pltpu.VMEM((8, nwin * faces), F32)] * 2
        + STAGE
        + STAGE
        + KEPT
        + [pltpu.SemaphoreType.DMA((nwin,))],
        compiler_params=pltpu.CompilerParams(vmem_limit_bytes=VMEM_LIMIT),
    )(first, second, count, *geos)


def place(flat):
    inner = lax.axis_size("gy")
    total = lax.axis_size("gx") * inner
    flat = (flat + total) % total
    return (flat // inner, flat % inner)


def greet(devices):
    barrier = pltpu.get_barrier_semaphore()
    for d in devices:
        pl.semaphore_signal(barrier, inc=1, device_id=d, device_id_type=MESH)
    pl.semaphore_wait(barrier, len(devices))


def gather(geometry, rows, chunks):
    faces = geometry.shape[1]
    part = faces // chunks

    def kernel(own, low, far, sib, high, send, recv):
        me = lax.axis_index("gx") * lax.axis_size("gy") + lax.axis_index("gy")
        odd = me % 2
        up, down, other = place(me + 2), place(me - 2), place(me + 1 - 2 * odd)
        greet((up, down, other))

        def move(kind, i, src, dst, device):
            sl = (pl.ds(0, rows), pl.ds(i * part, part))
            return pltpu.make_async_remote_copy(
                src_ref=src.at[sl],
                dst_ref=dst.at[sl],
                send_sem=send.at[kind, i],
                recv_sem=recv.at[kind, i],
                device_id=device,
                device_id_type=MESH,
            )

        for i in range(chunks):
            move(0, i, own, low, up).start()
            move(1, i, own, high, down).start()
        for i in range(chunks):
            move(2, i, own, sib, other).start()
        for i in range(chunks):
            move(0, i, own, low, up).wait_recv()
            move(1, i, own, high, down).wait_recv()

            @pl.when(odd == 0)
            def _():
                move(3, i, high, far, other).start()

            @pl.when(odd == 1)
            def _():
                move(3, i, low, far, other).start()

        for i in range(chunks):
            move(2, i, own, sib, other).wait_recv()
            move(3, i, own, far, other).wait_recv()
        for i in range(chunks):
            move(0, i, own, low, up).wait_send()
            move(1, i, own, high, down).wait_send()
            move(2, i, own, sib, other).wait_send()
            move(3, i, own, far, other).wait_send()

    return pl.pallas_call(
        kernel,
        out_shape=[jax.ShapeDtypeStruct((8, faces), F32)] * 4,
        in_specs=[pl.BlockSpec(memory_space=pl.ANY)],
        out_specs=[pl.BlockSpec(memory_space=pl.ANY)] * 4,
        scratch_shapes=[pltpu.SemaphoreType.DMA((4, chunks)), pltpu.SemaphoreType.DMA((4, chunks))],
        compiler_params=pltpu.CompilerParams(
            collective_id=0, has_side_effects=True, vmem_limit_bytes=VMEM_LIMIT
        ),
    )(geometry)


def give_back(low, far, sib, high):
    faces = low.shape[1]

    def kernel(low, far, sib, high, *refs):
        boxes = refs[:4]
        send, recv = refs[4:]
        me = lax.axis_index("gx") * lax.axis_size("gy") + lax.axis_index("gy")
        odd = me % 2
        targets = (place(me - 2), place(me - 1 + 2 * odd), place(me + 1 - 2 * odd), place(me + 2))
        greet(targets)
        copies = [
            pltpu.make_async_remote_copy(
                src_ref=src,
                dst_ref=boxes[k],
                send_sem=send.at[k],
                recv_sem=recv.at[k],
                device_id=device,
                device_id_type=MESH,
            )
            for k, (src, device) in enumerate(zip((low, far, sib, high), targets, strict=True))
        ]
        for k in (0, 3, 1, 2):
            copies[k].start()
        for c in copies:
            c.wait()

    return pl.pallas_call(
        kernel,
        out_shape=[jax.ShapeDtypeStruct((3, faces), F32)] * 4,
        in_specs=[pl.BlockSpec(memory_space=pl.ANY)] * 4,
        out_specs=[pl.BlockSpec(memory_space=pl.ANY)] * 4,
        scratch_shapes=[pltpu.SemaphoreType.DMA((4,)), pltpu.SemaphoreType.DMA((4,))],
        compiler_params=pltpu.CompilerParams(
            collective_id=1, has_side_effects=True, vmem_limit_bytes=VMEM_LIMIT
        ),
    )(low, far, sib, high)


def body(positions, normals, areas, pair_first, pair_second, pair_count):
    faces = areas.shape[0]
    clusters = faces // C
    me = lax.axis_index(("gx", "gy"))
    geometry = jnp.concatenate([positions, normals, areas[None, :], jnp.zeros((1, faces), F32)], axis=0)
    low, far, sib, high = gather(geometry, 7, 4)
    first = pair_first - (me - REACH) * clusters
    reach = pair_second // clusters - me
    slot = REACH + jnp.where(jnp.abs(reach) == 1, reach * (1 - 2 * (me % 2)), reach)
    second = slot * clusters + pair_second % clusters
    outs = near_field(first, second, pair_count, [low, far, geometry, sib, high])
    boxes = give_back(outs[0], outs[1], outs[3], outs[4])
    return outs[2] + ((boxes[0] + boxes[3]) + (boxes[1] + boxes[2]))


def solution(mesh):
    flat = P(("gx", "gy"))
    deep = P(None, ("gx", "gy"))
    return jax.shard_map(
        body, mesh=mesh, in_specs=(deep, deep, flat, flat, flat, flat), out_specs=deep, check_vma=False
    )
```

```python
import jax
import jax.numpy as jnp
from jax import lax
from jax.experimental import pallas as pl
from jax.experimental.pallas import tpu as pltpu
from jax.sharding import PartitionSpec as P

C = 256
REACH = 2
F32 = jnp.float32
BF = jnp.bfloat16
MESH = pl.DeviceIdType.MESH
VMEM_LIMIT = 60 * 2**20
EARLY = 31
LATE = 31
ROW = 128


def split3(t):
    a = t.astype(BF).astype(F32)
    r = t - a
    b = r.astype(BF).astype(F32)
    return a, b, r - b


def split2(t):
    a = t.astype(BF).astype(F32)
    return a, t - a


def wide(v):
    return jnp.broadcast_to(v, (8, C))


def row_index():
    return lax.broadcasted_iota(jnp.int32, (8, C), 0)


def prep(f, g, lhs_ref, rhs_ref, w_ref, keep_ref):
    row = row_index()
    isp = row < 3

    def at(k, v):
        return jnp.where(row == k, v, 0.0)

    af = wide(f[6:7, :])
    ag = wide(g[6:7, :])
    ctr = jnp.where(isp, wide(jnp.sum(f, axis=1, keepdims=True) * (1.0 / C)), 0.0)

    def parts(t):
        p = jnp.where(isp, t - ctr, 0.0)
        n = jnp.where(isp, pltpu.roll(t, 5, 0), 0.0)
        return p, n, wide(jnp.sum(p * p, axis=0, keepdims=True)), wide(jnp.sum(p * n, axis=0, keepdims=True))

    pf, nf, sf, cf = parts(f)
    pg, ng, sg, cg = parts(g)
    iaf = 1.0 / af
    iag = 1.0 / ag

    def left(t):
        u0, u1, u2 = split3(t)
        return jnp.concatenate([u0, u0, u0, u1, u1, u2], axis=0).T.astype(BF)

    def right(t):
        u0, u1, u2 = split3(t)
        return jnp.concatenate([u0, u1, u2, u0, u1, u0], axis=0).astype(BF)

    lhs_ref[0] = left(pf + at(3, sf + 1.0) + at(4, 1.0))
    lhs_ref[1] = left(af * (nf + at(3, cf) + pltpu.roll(pf, 4, 0) + at(7, 1.0)))
    rhs_ref[0] = right(-2.0 * pg + at(3, 1.0) + at(4, sg))
    rhs_ref[1] = right(ag * (at(3, 1.0) - pg))
    rhs_ref[2] = right(ag * (pltpu.roll(ng, 4, 0) - at(7, cg)))
    sums = (2.0 * nf, iaf * (at(6, 6.0) - 6.0 * pltpu.roll(pf, 3, 0)), iag * (6.0 * pg - at(3, 6.0)))
    for j, v in enumerate(sums):
        w_ref[j] = jnp.concatenate(split2(v), axis=0).astype(BF)
    for i, v in enumerate((nf, pf, iaf, ng, pg, iag)):
        keep_ref[i] = v


def terms(base, rows, sub, n, cs, lhs_ref, rhs_ref, l_ref, x_ref):
    def half(v):
        return v[:, :128] + v[:, 128:]

    big = slice(base, base + rows)
    left = lhs_ref[1, big, :]
    all_r2 = jnp.dot(lhs_ref[0, big, :], rhs_ref[0], preferred_element_type=F32)
    all_sf = jnp.dot(left, rhs_ref[1], preferred_element_type=F32)
    all_sg = jnp.dot(left, rhs_ref[2], preferred_element_type=F32)
    for s in range(0, rows, sub):
        sl = slice(base + s, base + s + sub)
        q = slice(s, s + sub)
        inv = 1.0 / all_r2[q]
        sf = all_sf[q]
        sg = all_sg[q]
        inv3 = inv * inv * inv
        lf = inv3 * sf
        lg = inv3 * sg
        rad = inv * (lf * sf + lg * sg)
        for j, v in ((0, lf), (2, rad)):
            h = v.astype(BF)
            l_ref[j, sl, :] = h
            l_ref[j + 1, sl, :] = (v - h.astype(F32)).astype(BF)
        for t in range(0, sub, 8):
            o = slice(t, t + 8)
            so = slice(base + s + t, base + s + t + 8)
            cs = cs + lg[o]
            x_ref[3, so, :] = half(lf[o])
            for k in range(3):
                x_ref[k, so, :] = half(lg[o] * n[k])
    return cs


def along(w, tile):
    return lax.dot_general(w, tile, (((1,), (0,)), ((), ())), preferred_element_type=F32)


def across(w, tile):
    return lax.dot_general(w, tile, (((1,), (1,)), ((), ())), preferred_element_type=F32)


def stage(h, now, before, ws, ks, load, save, rows=64, sub=16):
    lhs, rhs, w, keep, tiles, x, csr = now
    w_b, keep_b, tiles_b, x_b, csr_b = before[2:]
    ws[...] = w_b[...]
    ks[...] = keep_b[...]
    normal = [wide(keep[3, k : k + 1, :]) for k in range(3)]
    cs = jnp.zeros((8, C), F32)
    xs = [[None, None] for _ in range(4)]
    col = []
    rsum = []
    count = C // rows
    for c in range(count):
        cs = terms(c * rows, rows, sub, normal, cs, lhs, rhs, tiles, x)
        for e in range(c * 8 // count, (c + 1) * 8 // count):
            k, s = e // 2, e % 2
            xs[k][s] = jnp.sum(x_b[k, s * 128 : (s + 1) * 128, :].T, axis=0, keepdims=True)
            if e < 4:
                col.append(along(ws[e // 2], tiles_b[e]))
            elif e < 6:
                rsum.append(across(ws[2], tiles_b[e - 2]))
        if c == count // 2 - 1:
            prep(*load(h + 1), *before[:4])
    csr_old = csr_b[...]
    csr[...] = cs
    row = row_index()
    ct = (col[0] + col[1]) + (col[2] + col[3])
    rt = rsum[0] + rsum[1]
    ct = ct[0:8] + ct[8:16]
    rt = rt[0:8] + rt[8:16]
    nf, pf, iaf, ng, pg, iag = (ks[i] for i in range(6))
    xv = [wide(jnp.concatenate(v, axis=1)) for v in xs]
    lean = jnp.where(row == 0, xv[0], jnp.where(row == 1, xv[1], xv[2]))
    gf = 2.0 * (nf * xv[3] + lean) + iaf * (rt + pf * wide(rt[3:4]))
    csum = wide(jnp.sum(csr_old, axis=0, keepdims=True))
    gg = -(ct + ng * (2.0 * csum) + iag * (pltpu.roll(ct, 5, 0) + pg * wide(ct[6:7])))
    save(h - 1, gf, gg)


STAGE = [
    pltpu.VMEM((2, C, 48), BF),
    pltpu.VMEM((3, 48, C), BF),
    pltpu.VMEM((3, 16, C), BF),
    pltpu.VMEM((6, 8, C), F32),
    pltpu.VMEM((4, C, C), BF),
    pltpu.VMEM((4, C, 128), F32),
    pltpu.VMEM((8, C), F32),
]
KEPT = [pltpu.VMEM((3, 16, C), BF), pltpu.VMEM((6, 8, C), F32)]


def lanes(c):
    return pl.ds(pl.multiple_of(c * C, C), C)


def place(flat):
    inner = lax.axis_size("gy")
    total = lax.axis_size("gx") * inner
    flat = (flat + total) % total
    return (flat // inner, flat % inner)


def position():
    return lax.axis_index("gx") * lax.axis_size("gy") + lax.axis_index("gy")


def greet(devices):
    barrier = pltpu.get_barrier_semaphore()
    for d in devices:
        pl.semaphore_signal(barrier, inc=1, device_id=d, device_id_type=MESH)
    pl.semaphore_wait(barrier, len(devices))


def sort_out(positions, normals, areas, pair_first, pair_second, pair_count):
    faces = positions.shape[1]
    clusters = faces // C

    def kernel(pos, nor, area, pf, ps, count, geometry, lists):
        for c in range(clusters):
            sl = slice(c * C, (c + 1) * C)
            geometry[c, 0:3, :] = pos[:, sl]
            geometry[c, 3:6, :] = nor[:, sl]
            geometry[c, 6:7, :] = area[:, sl]
            geometry[c, 7:8, :] = jnp.zeros((1, C), F32)
        me = position()
        odd = me % 2

        def clear(i, carry):
            for r in range(4):
                lists[r * ROW + i] = 0
            return carry

        lax.fori_loop(0, EARLY + 1, clear, 0)
        lists[4 * ROW] = 0
        lists[5 * ROW] = 0

        def step(j, carry):
            n1, n3, n2 = carry
            f = pf[j] - me * clusters
            s = ps[j]
            owner = s // clusters
            local = s - owner * clusters
            h = owner - me
            beside = h == 1 - 2 * odd
            inside = h == 0
            late = inside & (n3 < LATE)
            early = (beside | inside) & (n1 < EARLY) & jnp.logical_not(late)
            rest = jnp.logical_not(late | early)
            near = (h == 1) | (h == -1)
            slot = REACH + jnp.where(near, h * (1 - 2 * odd), h)
            base = jnp.where(late, 2 * ROW + n3, jnp.where(early, n1, 4 * ROW + n2))
            lists[base] = jnp.where(rest, f + REACH * clusters, f)
            lists[base + ROW] = jnp.where(rest, slot * clusters, jnp.where(beside, clusters, 0)) + local
            return (
                n1 + early.astype(jnp.int32),
                n3 + late.astype(jnp.int32),
                n2 + rest.astype(jnp.int32),
            )

        n1, n3, n2 = lax.fori_loop(0, count[0], step, (0, 0, 0))
        lists[6 * ROW] = n1
        lists[6 * ROW + 1] = n3
        lists[6 * ROW + 2] = n2

    vmem = pl.BlockSpec(memory_space=pltpu.VMEM)
    smem = pl.BlockSpec(memory_space=pltpu.SMEM)
    return pl.pallas_call(
        kernel,
        out_shape=[jax.ShapeDtypeStruct((clusters, 8, C), F32), jax.ShapeDtypeStruct((7 * ROW,), jnp.int32)],
        in_specs=[vmem] * 3 + [smem] * 3,
        out_specs=[vmem, smem],
        compiler_params=pltpu.CompilerParams(vmem_limit_bytes=VMEM_LIMIT),
    )(positions, normals, areas.reshape(1, faces), pair_first, pair_second, pair_count)


def gather(geometry, lists, rows=7, chunks=4):
    clusters = geometry.shape[0]
    part = clusters // chunks

    def kernel(own, lists, low, far, sib, high, made, seen, *refs):
        even, odds = refs[:7], refs[7:14]
        ws, ks, send, recv, fetch = refs[14:]
        me = position()
        odd = me % 2
        up, down, other = place(me + 2), place(me - 2), place(me + 1 - 2 * odd)
        mine = pltpu.make_async_copy(own, seen.at[pl.ds(0, clusters)], fetch.at[0])
        mine.start()
        greet((up, down, other))

        def move(kind, i, src, dst, device):
            sl = (pl.ds(i * part, part), pl.ds(0, rows))
            return pltpu.make_async_remote_copy(
                src_ref=src.at[sl],
                dst_ref=dst.at[sl],
                send_sem=send.at[kind, i],
                recv_sem=recv.at[kind, i],
                device_id=device,
                device_id_type=MESH,
            )

        for i in range(chunks):
            move(0, i, own, low, up).start()
            move(1, i, own, high, down).start()
            move(2, i, own, sib, other).start()
        for i in range(chunks):
            move(2, i, own, sib, other).wait_recv()
        beside = pltpu.make_async_copy(sib, seen.at[pl.ds(clusters, clusters)], fetch.at[1])
        beside.start()
        mine.wait()
        beside.wait()

        def load(h):
            q = jnp.minimum(h, EARLY)
            return seen[lists[q]], seen[lists[ROW + q]]

        def save(h, gf, gg):
            made[h + 1, 0] = gf
            made[h + 1, 1] = gg

        prep(*load(0), *even[:4])

        def step(i, carry):
            stage(2 * i, even, odds, ws, ks, load, save)
            stage(2 * i + 1, odds, even, ws, ks, load, save)
            return carry

        halves = (EARLY + 1) // 2
        for i in range(chunks):
            lax.fori_loop(i * halves // chunks, (i + 1) * halves // chunks, step, 0)
            move(0, i, own, low, up).wait_recv()
            move(1, i, own, high, down).wait_recv()

            @pl.when(odd == 0)
            def _():
                move(3, i, high, far, other).start()

            @pl.when(odd == 1)
            def _():
                move(3, i, low, far, other).start()

        for i in range(chunks):
            move(3, i, own, far, other).wait_recv()
        for i in range(chunks):
            for kind in range(4):
                move(kind, i, own, low, up).wait_send()

    hbm = pl.BlockSpec(memory_space=pl.ANY)
    return pl.pallas_call(
        kernel,
        out_shape=[jax.ShapeDtypeStruct((clusters, 8, C), F32)] * 4
        + [jax.ShapeDtypeStruct((EARLY + 1, 2, 8, C), F32)],
        in_specs=[hbm, pl.BlockSpec(memory_space=pltpu.SMEM)],
        out_specs=[hbm] * 4 + [pl.BlockSpec(memory_space=pltpu.VMEM)],
        scratch_shapes=[pltpu.VMEM((2 * clusters, 8, C), F32)]
        + STAGE
        + STAGE
        + KEPT
        + [pltpu.SemaphoreType.DMA((4, chunks)), pltpu.SemaphoreType.DMA((4, chunks)), pltpu.SemaphoreType.DMA((2,))],
        compiler_params=pltpu.CompilerParams(
            collective_id=0, has_side_effects=True, vmem_limit_bytes=VMEM_LIMIT
        ),
    )(geometry, lists)


def near_field(lists, geos, made, sib_slot):
    nwin = len(geos)
    clusters = geos[0].shape[0]
    faces = clusters * C

    def kernel(lists, made, *refs):
        geo = refs[:nwin]
        outs = refs[nwin : 2 * nwin]
        win, acc, early = refs[2 * nwin : 2 * nwin + 3]
        even = refs[2 * nwin + 3 : 2 * nwin + 10]
        odd = refs[2 * nwin + 10 : 2 * nwin + 17]
        ws, ks, sem = refs[2 * nwin + 17 :]
        copies = [
            pltpu.make_async_copy(geo[k], win.at[pl.ds(k * clusters, clusters)], sem.at[k]) for k in range(nwin)
        ] + [pltpu.make_async_copy(made, early, sem.at[nwin])]
        for c in copies:
            c.start()
        acc[...] = jnp.zeros_like(acc)
        for c in copies:
            c.wait()
        n = lists[6 * ROW + 2]
        last = jnp.maximum(n - 1, 0)

        def load(h):
            q = jnp.minimum(h, last)
            return win[lists[4 * ROW + q]], win[lists[5 * ROW + q]]

        def save(h, gf, gg):
            live = (h >= 0) & (h < n)
            q = jnp.clip(h, 0, last)
            fi = lists[4 * ROW + q]
            si = lists[5 * ROW + q]
            acc[fi] += jnp.where(live, gf, 0.0)
            acc[si] += jnp.where(live, gg, 0.0)

        prep(*load(0), *even[:4])

        def add(j, carry):
            acc[lists[j] + sib_slot * clusters] += early[j + 1, 0]
            acc[lists[ROW + j] + sib_slot * clusters] += early[j + 1, 1]
            return carry

        lax.fori_loop(0, lists[6 * ROW], add, 0)

        def step(i, carry):
            stage(2 * i, even, odd, ws, ks, load, save)
            stage(2 * i + 1, odd, even, ws, ks, load, save)
            return carry

        lax.fori_loop(0, (n + 2) // 2, step, 0)
        for k in range(nwin):
            for c in range(clusters):
                outs[k][:, c * C : (c + 1) * C] = acc[k * clusters + c, 0:3, :]

    hbm = pl.BlockSpec(memory_space=pl.ANY)
    return pl.pallas_call(
        kernel,
        out_shape=[jax.ShapeDtypeStruct((3, faces), F32)] * nwin,
        in_specs=[pl.BlockSpec(memory_space=pltpu.SMEM)] + [hbm] * (nwin + 1),
        out_specs=[pl.BlockSpec(memory_space=pltpu.VMEM)] * nwin,
        scratch_shapes=[pltpu.VMEM((nwin * clusters, 8, C), F32)] * 2
        + [pltpu.VMEM((EARLY + 1, 2, 8, C), F32)]
        + STAGE
        + STAGE
        + KEPT
        + [pltpu.SemaphoreType.DMA((nwin + 1,))],
        compiler_params=pltpu.CompilerParams(vmem_limit_bytes=VMEM_LIMIT),
    )(lists, made, *geos)


def give_back(low, far, sib, high, geometry, lists):
    faces = low.shape[1]
    clusters = faces // C

    def kernel(low, far, sib, high, own, lists, *refs):
        boxes = refs[:4]
        made, seen = refs[4:6]
        even, odds = refs[6:13], refs[13:20]
        ws, ks, send, recv, fetch = refs[20:]
        me = position()
        odd = me % 2
        targets = (place(me - 2), place(me - 1 + 2 * odd), place(me + 1 - 2 * odd), place(me + 2))
        mine = pltpu.make_async_copy(own, seen, fetch.at[0])
        mine.start()
        greet(targets)
        copies = [
            pltpu.make_async_remote_copy(
                src_ref=src,
                dst_ref=boxes[k],
                send_sem=send.at[k],
                recv_sem=recv.at[k],
                device_id=device,
                device_id_type=MESH,
            )
            for k, (src, device) in enumerate(zip((low, far, sib, high), targets, strict=True))
        ]
        for k in (0, 3, 1, 2):
            copies[k].start()
        mine.wait()

        def load(h):
            q = jnp.minimum(h, LATE)
            return seen[lists[2 * ROW + q]], seen[lists[3 * ROW + q]]

        def save(h, gf, gg):
            made[h + 1, 0] = gf
            made[h + 1, 1] = gg

        prep(*load(0), *even[:4])

        def step(i, carry):
            stage(2 * i, even, odds, ws, ks, load, save)
            stage(2 * i + 1, odds, even, ws, ks, load, save)
            return carry

        lax.fori_loop(0, (LATE + 1) // 2, step, 0)
        for c in copies:
            c.wait()

    hbm = pl.BlockSpec(memory_space=pl.ANY)
    return pl.pallas_call(
        kernel,
        out_shape=[jax.ShapeDtypeStruct((3, faces), F32)] * 4
        + [jax.ShapeDtypeStruct((LATE + 1, 2, 8, C), F32)],
        in_specs=[hbm] * 5 + [pl.BlockSpec(memory_space=pltpu.SMEM)],
        out_specs=[hbm] * 4 + [pl.BlockSpec(memory_space=pltpu.VMEM)],
        scratch_shapes=[pltpu.VMEM((clusters, 8, C), F32)]
        + STAGE
        + STAGE
        + KEPT
        + [pltpu.SemaphoreType.DMA((4,)), pltpu.SemaphoreType.DMA((4,)), pltpu.SemaphoreType.DMA((1,))],
        compiler_params=pltpu.CompilerParams(
            collective_id=1, has_side_effects=True, vmem_limit_bytes=VMEM_LIMIT
        ),
    )(low, far, sib, high, geometry, lists)


def finish(own, boxes, made, lists):
    def kernel(lists, own, b0, b1, b2, b3, made, out):
        out[...] = own[...] + ((b0[...] + b3[...]) + (b1[...] + b2[...]))

        def add(j, carry):
            fi = lanes(lists[2 * ROW + j])
            out[:, fi] += made[j + 1, 0, 0:3, :]
            si = lanes(lists[3 * ROW + j])
            out[:, si] += made[j + 1, 1, 0:3, :]
            return carry

        lax.fori_loop(0, lists[6 * ROW + 1], add, 0)

    vmem = pl.BlockSpec(memory_space=pltpu.VMEM)
    return pl.pallas_call(
        kernel,
        out_shape=jax.ShapeDtypeStruct(own.shape, F32),
        in_specs=[pl.BlockSpec(memory_space=pltpu.SMEM)] + [vmem] * 6,
        out_specs=vmem,
        compiler_params=pltpu.CompilerParams(vmem_limit_bytes=VMEM_LIMIT),
    )(lists, own, *boxes, made)


def body(positions, normals, areas, pair_first, pair_second, pair_count):
    geometry, lists = sort_out(positions, normals, areas, pair_first, pair_second, pair_count)
    low, far, sib, high, early = gather(geometry, lists)
    outs = near_field(lists, [low, far, geometry, sib, high], early, REACH)
    *boxes, late = give_back(outs[0], outs[1], outs[3], outs[4], geometry, lists)
    return finish(outs[2], boxes, late, lists)


def solution(mesh):
    flat = P(("gx", "gy"))
    deep = P(None, ("gx", "gy"))
    return jax.shard_map(
        body, mesh=mesh, in_specs=(deep, deep, flat, flat, flat, flat), out_specs=deep, check_vma=False
    )
```

```python
import jax
import jax.numpy as jnp
from jax import lax
from jax.experimental import pallas as pl
from jax.experimental.pallas import tpu as pltpu
from jax.sharding import PartitionSpec as P

C = 256
REACH = 2
F32 = jnp.float32
BF = jnp.bfloat16
MESH = pl.DeviceIdType.MESH
VMEM_LIMIT = 60 * 2**20
INSIDE = 9
EARLY = 31
LATE = 23
ROW = 128


def split3(t):
    a = t.astype(BF).astype(F32)
    r = t - a
    b = r.astype(BF).astype(F32)
    return a, b, r - b


def split2(t):
    a = t.astype(BF).astype(F32)
    return a, t - a


def wide(v):
    return jnp.broadcast_to(v, (8, C))


def row_index():
    return lax.broadcasted_iota(jnp.int32, (8, C), 0)


def prep(f, g, lhs_ref, rhs_ref, w_ref, keep_ref):
    row = row_index()
    isp = row < 3

    def at(k, v):
        return jnp.where(row == k, v, 0.0)

    af = wide(f[6:7, :])
    ag = wide(g[6:7, :])
    ctr = jnp.where(isp, wide(jnp.sum(f, axis=1, keepdims=True) * (1.0 / C)), 0.0)

    def parts(t):
        p = jnp.where(isp, t - ctr, 0.0)
        n = jnp.where(isp, pltpu.roll(t, 5, 0), 0.0)
        return p, n, wide(jnp.sum(p * p, axis=0, keepdims=True)), wide(jnp.sum(p * n, axis=0, keepdims=True))

    pf, nf, sf, cf = parts(f)
    pg, ng, sg, cg = parts(g)
    iaf = 1.0 / af
    iag = 1.0 / ag

    def left(t):
        u0, u1, u2 = split3(t)
        return jnp.concatenate([u0, u0, u0, u1, u1, u2], axis=0).T.astype(BF)

    def right(t):
        u0, u1, u2 = split3(t)
        return jnp.concatenate([u0, u1, u2, u0, u1, u0], axis=0).astype(BF)

    lhs_ref[0] = left(pf + at(3, sf + 1.0) + at(4, 1.0))
    lhs_ref[1] = left(af * (nf + at(3, cf) + pltpu.roll(pf, 4, 0) + at(7, 1.0)))
    rhs_ref[0] = right(-2.0 * pg + at(3, 1.0) + at(4, sg))
    rhs_ref[1] = right(ag * (at(3, 1.0) - pg))
    rhs_ref[2] = right(ag * (pltpu.roll(ng, 4, 0) - at(7, cg)))
    sums = (2.0 * nf, iaf * (at(6, 6.0) - 6.0 * pltpu.roll(pf, 3, 0)), iag * (6.0 * pg - at(3, 6.0)))
    for j, v in enumerate(sums):
        w_ref[j] = jnp.concatenate(split2(v), axis=0).astype(BF)
    for i, v in enumerate((nf, pf, iaf, ng, pg, iag)):
        keep_ref[i] = v


def terms(base, rows, sub, n, cs, lhs_ref, rhs_ref, l_ref, x_ref):
    def half(v):
        return v[:, :128] + v[:, 128:]

    big = slice(base, base + rows)
    left = lhs_ref[1, big, :]
    all_r2 = jnp.dot(lhs_ref[0, big, :], rhs_ref[0], preferred_element_type=F32)
    all_sf = jnp.dot(left, rhs_ref[1], preferred_element_type=F32)
    all_sg = jnp.dot(left, rhs_ref[2], preferred_element_type=F32)
    for s in range(0, rows, sub):
        sl = slice(base + s, base + s + sub)
        q = slice(s, s + sub)
        inv = 1.0 / all_r2[q]
        sf = all_sf[q]
        sg = all_sg[q]
        inv3 = inv * inv * inv
        lf = inv3 * sf
        lg = inv3 * sg
        rad = inv * (lf * sf + lg * sg)
        for j, v in ((0, lf), (2, rad)):
            h = v.astype(BF)
            l_ref[j, sl, :] = h
            l_ref[j + 1, sl, :] = (v - h.astype(F32)).astype(BF)
        for t in range(0, sub, 8):
            o = slice(t, t + 8)
            so = slice(base + s + t, base + s + t + 8)
            cs = cs + lg[o]
            x_ref[3, so, :] = half(lf[o])
            for k in range(3):
                x_ref[k, so, :] = half(lg[o] * n[k])
    return cs


def along(w, tile):
    return lax.dot_general(w, tile, (((1,), (0,)), ((), ())), preferred_element_type=F32)


def across(w, tile):
    return lax.dot_general(w, tile, (((1,), (1,)), ((), ())), preferred_element_type=F32)


def stage(h, now, before, ws, ks, load, save, rows=64, sub=16):
    lhs, rhs, w, keep, tiles, x, csr = now
    w_b, keep_b, tiles_b, x_b, csr_b = before[2:]
    ws[...] = w_b[...]
    ks[...] = keep_b[...]
    normal = [wide(keep[3, k : k + 1, :]) for k in range(3)]
    cs = jnp.zeros((8, C), F32)
    xs = [[None, None] for _ in range(4)]
    col = []
    rsum = []
    count = C // rows
    for c in range(count):
        cs = terms(c * rows, rows, sub, normal, cs, lhs, rhs, tiles, x)
        for e in range(c * 8 // count, (c + 1) * 8 // count):
            k, s = e // 2, e % 2
            xs[k][s] = jnp.sum(x_b[k, s * 128 : (s + 1) * 128, :].T, axis=0, keepdims=True)
            if e < 4:
                col.append(along(ws[e // 2], tiles_b[e]))
            elif e < 6:
                rsum.append(across(ws[2], tiles_b[e - 2]))
        if c == count // 2 - 1:
            prep(*load(h + 1), *before[:4])
    csr_old = csr_b[...]
    csr[...] = cs
    row = row_index()
    ct = (col[0] + col[1]) + (col[2] + col[3])
    rt = rsum[0] + rsum[1]
    ct = ct[0:8] + ct[8:16]
    rt = rt[0:8] + rt[8:16]
    nf, pf, iaf, ng, pg, iag = (ks[i] for i in range(6))
    xv = [wide(jnp.concatenate(v, axis=1)) for v in xs]
    lean = jnp.where(row == 0, xv[0], jnp.where(row == 1, xv[1], xv[2]))
    gf = 2.0 * (nf * xv[3] + lean) + iaf * (rt + pf * wide(rt[3:4]))
    csum = wide(jnp.sum(csr_old, axis=0, keepdims=True))
    gg = -(ct + ng * (2.0 * csum) + iag * (pltpu.roll(ct, 5, 0) + pg * wide(ct[6:7])))
    save(h - 1, gf, gg)


STAGE = [
    pltpu.VMEM((2, C, 48), BF),
    pltpu.VMEM((3, 48, C), BF),
    pltpu.VMEM((3, 16, C), BF),
    pltpu.VMEM((6, 8, C), F32),
    pltpu.VMEM((4, C, C), BF),
    pltpu.VMEM((4, C, 128), F32),
    pltpu.VMEM((8, C), F32),
]
KEPT = [pltpu.VMEM((3, 16, C), BF), pltpu.VMEM((6, 8, C), F32)]


def lanes(c):
    return pl.ds(pl.multiple_of(c * C, C), C)


def place(flat):
    inner = lax.axis_size("gy")
    total = lax.axis_size("gx") * inner
    flat = (flat + total) % total
    return (flat // inner, flat % inner)


def position():
    return lax.axis_index("gx") * lax.axis_size("gy") + lax.axis_index("gy")


def greet(devices):
    barrier = pltpu.get_barrier_semaphore()
    for d in devices:
        pl.semaphore_signal(barrier, inc=1, device_id=d, device_id_type=MESH)
    pl.semaphore_wait(barrier, len(devices))


def sort_out(positions, normals, areas, pair_first, pair_second, pair_count):
    faces = positions.shape[1]
    clusters = faces // C

    def kernel(pos, nor, area, pf, ps, count, geometry, lists):
        for c in range(clusters):
            sl = slice(c * C, (c + 1) * C)
            geometry[c, 0:3, :] = pos[:, sl]
            geometry[c, 3:6, :] = nor[:, sl]
            geometry[c, 6:7, :] = area[:, sl]
            geometry[c, 7:8, :] = jnp.zeros((1, C), F32)
        me = position()
        odd = me % 2

        def clear(i, carry):
            for r in range(4):
                lists[r * ROW + i] = 0
            return carry

        lax.fori_loop(0, EARLY + 1, clear, 0)
        lists[4 * ROW] = 0
        lists[5 * ROW] = 0

        live = count[0]

        def one(j, carry):
            n0, n1, n3, n2 = carry
            f = pf[j] - me * clusters
            s = ps[j]
            owner = s // clusters
            local = s - owner * clusters
            h = owner - me
            ok = j < live
            beside = h == 1 - 2 * odd
            inside = h == 0
            first = ok & inside & (n0 < INSIDE)
            late = ok & inside & jnp.logical_not(first) & (n3 < LATE)
            early = ok & (beside | (inside & jnp.logical_not(first | late))) & (n1 < EARLY)
            rest = ok & jnp.logical_not(first | late | early)
            near = (h == 1) | (h == -1)
            slot = REACH + jnp.where(near, h * (1 - 2 * odd), h)
            base = jnp.where(first, n0, jnp.where(late, 2 * ROW + n3, jnp.where(early, n1, 4 * ROW + n2)))
            lists[base] = jnp.where(rest, f + REACH * clusters, f)
            lists[base + ROW] = jnp.where(rest, slot * clusters, jnp.where(beside, clusters, 0)) + local
            return (
                n0 + first.astype(jnp.int32),
                n1 + early.astype(jnp.int32),
                n3 + late.astype(jnp.int32),
                n2 + rest.astype(jnp.int32),
            )

        def step(i, carry):
            for u in range(4):
                carry = one(4 * i + u, carry)
            return carry

        n0, n1, n3, n2 = lax.fori_loop(0, (live + 3) // 4, step, (0, INSIDE, 0, 0))
        lists[6 * ROW] = n0
        lists[6 * ROW + 1] = n1
        lists[6 * ROW + 2] = n3
        lists[6 * ROW + 3] = n2

    vmem = pl.BlockSpec(memory_space=pltpu.VMEM)
    smem = pl.BlockSpec(memory_space=pltpu.SMEM)
    return pl.pallas_call(
        kernel,
        out_shape=[jax.ShapeDtypeStruct((clusters, 8, C), F32), jax.ShapeDtypeStruct((7 * ROW,), jnp.int32)],
        in_specs=[vmem] * 3 + [smem] * 3,
        out_specs=[vmem, smem],
        compiler_params=pltpu.CompilerParams(vmem_limit_bytes=VMEM_LIMIT),
    )(positions, normals, areas.reshape(1, faces), pair_first, pair_second, pair_count)


def gather(geometry, lists, rows=7, chunks=4):
    clusters = geometry.shape[0]
    part = clusters // chunks

    def kernel(own, lists, low, far, sib, high, made, near, seen, *refs):
        even, odds = refs[:7], refs[7:14]
        ws, ks, send, recv, fetch = refs[14:]
        me = position()
        odd = me % 2
        up, down, other = place(me + 2), place(me - 2), place(me + 1 - 2 * odd)
        mine = pltpu.make_async_copy(own, near, fetch.at[0])
        mine.start()
        again = pltpu.make_async_copy(own, seen.at[pl.ds(0, clusters)], fetch.at[2])
        again.start()
        above = me + 2 < lax.axis_size("gx") * lax.axis_size("gy")
        below = me >= 2
        greet((up, down, other))

        def move(kind, i, src, dst, device):
            sl = (pl.ds(i * part, part), pl.ds(0, rows))
            return pltpu.make_async_remote_copy(
                src_ref=src.at[sl],
                dst_ref=dst.at[sl],
                send_sem=send.at[kind, i],
                recv_sem=recv.at[kind, i],
                device_id=device,
                device_id_type=MESH,
            )

        for i in range(chunks):
            move(2, i, own, sib, other).start()

        @pl.when(above)
        def _():
            for i in range(chunks):
                move(0, i, own, low, up).start()

        @pl.when(below)
        def _():
            for i in range(chunks):
                move(1, i, own, high, down).start()

        mine.wait()

        def load(h):
            q = jnp.minimum(h, EARLY)
            return seen[lists[q]], seen[lists[ROW + q]]

        def save(h, gf, gg):
            made[h + 1, 0] = gf
            made[h + 1, 1] = gg

        def step(i, carry):
            stage(2 * i, even, odds, ws, ks, load, save)
            stage(2 * i + 1, odds, even, ws, ks, load, save)
            return carry

        def fresh(h):
            return near[lists[h]], near[lists[ROW + h]]

        def inner(i, carry):
            stage(2 * i, even, odds, ws, ks, fresh, save)
            stage(2 * i + 1, odds, even, ws, ks, fresh, save)
            return carry

        prep(*fresh(0), *even[:4])
        lead = (INSIDE - 1) // 2
        lax.fori_loop(0, lead, inner, 0)
        for i in range(chunks):
            move(2, i, own, sib, other).wait_recv()
        beside = pltpu.make_async_copy(sib, seen.at[pl.ds(clusters, clusters)], fetch.at[1])
        beside.start()
        again.wait()
        beside.wait()
        halves = (EARLY + 1) // 2 - lead
        for i in range(chunks):
            lax.fori_loop(lead + i * halves // chunks, lead + (i + 1) * halves // chunks, step, 0)

            @pl.when(below)
            def _():
                move(0, i, own, low, up).wait_recv()

                @pl.when(odd == 1)
                def _():
                    move(3, i, low, far, other).start()

            @pl.when(above)
            def _():
                move(1, i, own, high, down).wait_recv()

                @pl.when(odd == 0)
                def _():
                    move(3, i, high, far, other).start()

        @pl.when(((odd == 0) & below) | ((odd == 1) & above))
        def _():
            for i in range(chunks):
                move(3, i, own, far, other).wait_recv()

        @pl.when(((odd == 0) & above) | ((odd == 1) & below))
        def _():
            for i in range(chunks):
                move(3, i, own, far, other).wait_send()

        @pl.when(above)
        def _():
            for i in range(chunks):
                move(0, i, own, low, up).wait_send()

        @pl.when(below)
        def _():
            for i in range(chunks):
                move(1, i, own, high, down).wait_send()

        for i in range(chunks):
            move(2, i, own, sib, other).wait_send()

    hbm = pl.BlockSpec(memory_space=pl.ANY)
    return pl.pallas_call(
        kernel,
        out_shape=[jax.ShapeDtypeStruct((clusters, 8, C), F32)] * 4
        + [jax.ShapeDtypeStruct((EARLY + 1, 2, 8, C), F32)],
        in_specs=[hbm, pl.BlockSpec(memory_space=pltpu.SMEM)],
        out_specs=[hbm] * 4 + [pl.BlockSpec(memory_space=pltpu.VMEM)],
        scratch_shapes=[pltpu.VMEM((clusters, 8, C), F32), pltpu.VMEM((2 * clusters, 8, C), F32)]
        + STAGE
        + STAGE
        + KEPT
        + [pltpu.SemaphoreType.DMA((4, chunks)), pltpu.SemaphoreType.DMA((4, chunks)), pltpu.SemaphoreType.DMA((3,))],
        compiler_params=pltpu.CompilerParams(
            collective_id=0, has_side_effects=True, vmem_limit_bytes=VMEM_LIMIT
        ),
    )(geometry, lists)


def near_field(lists, geos, made, sib_slot):
    nwin = len(geos)
    clusters = geos[0].shape[0]

    def kernel(lists, made, *refs):
        geo = refs[:nwin]
        acc, win, early = refs[nwin : nwin + 3]
        even = refs[nwin + 3 : nwin + 10]
        odd = refs[nwin + 10 : nwin + 17]
        ws, ks, sem = refs[nwin + 17 :]
        copies = [
            pltpu.make_async_copy(geo[k], win.at[pl.ds(k * clusters, clusters)], sem.at[k]) for k in range(nwin)
        ] + [pltpu.make_async_copy(made, early, sem.at[nwin])]
        for c in copies:
            c.start()
        acc[...] = jnp.zeros_like(acc)
        for c in copies:
            c.wait()
        n = lists[6 * ROW + 3]
        last = jnp.maximum(n - 1, 0)

        def load(h):
            q = jnp.minimum(h, last)
            return win[lists[4 * ROW + q]], win[lists[5 * ROW + q]]

        def save(h, gf, gg):
            live = (h >= 0) & (h < n)
            q = jnp.clip(h, 0, last)
            fi = lists[4 * ROW + q]
            si = lists[5 * ROW + q]
            acc[fi] += jnp.where(live, gf, 0.0)
            acc[si] += jnp.where(live, gg, 0.0)

        prep(*load(0), *even[:4])

        def add(j, carry):
            acc[lists[j] + sib_slot * clusters] += early[j + 1, 0]
            acc[lists[ROW + j] + sib_slot * clusters] += early[j + 1, 1]
            return carry

        lax.fori_loop(0, lists[6 * ROW], add, 0)
        lax.fori_loop(INSIDE, lists[6 * ROW + 1], add, 0)

        def step(i, carry):
            stage(2 * i, even, odd, ws, ks, load, save)
            stage(2 * i + 1, odd, even, ws, ks, load, save)
            return carry

        lax.fori_loop(0, (n + 2) // 2, step, 0)

    hbm = pl.BlockSpec(memory_space=pl.ANY)
    return pl.pallas_call(
        kernel,
        out_shape=jax.ShapeDtypeStruct((nwin * clusters, 8, C), F32),
        in_specs=[pl.BlockSpec(memory_space=pltpu.SMEM)] + [hbm] * (nwin + 1),
        out_specs=pl.BlockSpec(memory_space=pltpu.VMEM),
        scratch_shapes=[pltpu.VMEM((nwin * clusters, 8, C), F32)]
        + [pltpu.VMEM((EARLY + 1, 2, 8, C), F32)]
        + STAGE
        + STAGE
        + KEPT
        + [pltpu.SemaphoreType.DMA((nwin + 1,))],
        compiler_params=pltpu.CompilerParams(vmem_limit_bytes=VMEM_LIMIT),
    )(lists, made, *geos)


def give_back(sums, geometry, lists):
    clusters = geometry.shape[0]

    def kernel(sums, own, lists, *refs):
        boxes = refs[:4]
        made, seen = refs[4:6]
        even, odds = refs[6:13], refs[13:20]
        ws, ks, send, recv, fetch = refs[20:]
        me = position()
        odd = me % 2
        targets = (place(me - 2), place(me - 1 + 2 * odd), place(me + 1 - 2 * odd), place(me + 2))
        mine = pltpu.make_async_copy(own, seen, fetch.at[0])
        mine.start()
        greet(targets)
        copies = [
            pltpu.make_async_remote_copy(
                src_ref=sums.at[pl.ds(slot * clusters, clusters), pl.ds(0, 3)],
                dst_ref=boxes[k].at[:, pl.ds(0, 3)],
                send_sem=send.at[k],
                recv_sem=recv.at[k],
                device_id=device,
                device_id_type=MESH,
            )
            for k, (slot, device) in enumerate(zip((0, 1, 3, 4), targets, strict=True))
        ]
        for k in (0, 3, 1, 2):
            copies[k].start()
        mine.wait()

        def load(h):
            q = jnp.minimum(h, LATE)
            return seen[lists[2 * ROW + q]], seen[lists[3 * ROW + q]]

        def save(h, gf, gg):
            made[h + 1, 0] = gf
            made[h + 1, 1] = gg

        prep(*load(0), *even[:4])

        def step(i, carry):
            stage(2 * i, even, odds, ws, ks, load, save)
            stage(2 * i + 1, odds, even, ws, ks, load, save)
            return carry

        lax.fori_loop(0, (LATE + 1) // 2, step, 0)
        for c in copies:
            c.wait()

    hbm = pl.BlockSpec(memory_space=pl.ANY)
    return pl.pallas_call(
        kernel,
        out_shape=[jax.ShapeDtypeStruct((clusters, 8, C), F32)] * 4
        + [jax.ShapeDtypeStruct((LATE + 1, 2, 8, C), F32)],
        in_specs=[hbm] * 2 + [pl.BlockSpec(memory_space=pltpu.SMEM)],
        out_specs=[hbm] * 4 + [pl.BlockSpec(memory_space=pltpu.VMEM)],
        scratch_shapes=[pltpu.VMEM((clusters, 8, C), F32)]
        + STAGE
        + STAGE
        + KEPT
        + [pltpu.SemaphoreType.DMA((4,)), pltpu.SemaphoreType.DMA((4,)), pltpu.SemaphoreType.DMA((1,))],
        compiler_params=pltpu.CompilerParams(
            collective_id=1, has_side_effects=True, vmem_limit_bytes=VMEM_LIMIT
        ),
    )(sums, geometry, lists)


def finish(sums, boxes, made, lists):
    clusters = boxes[0].shape[0]

    def kernel(lists, sums, b0, b1, b2, b3, made, out, held, sem):
        lay = pl.ds(0, 3)
        sources = [sums.at[pl.ds(REACH * clusters, clusters), lay]] + [b.at[:, lay] for b in (b0, b1, b2, b3)]
        copies = [
            pltpu.make_async_copy(src, held.at[pl.ds(k * clusters, clusters), lay], sem.at[k])
            for k, src in enumerate(sources)
        ]
        for c in copies:
            c.start()
        for c in copies:
            c.wait()

        def add(j, carry):
            held[lists[2 * ROW + j]] += made[j + 1, 0]
            held[lists[3 * ROW + j]] += made[j + 1, 1]
            return carry

        lax.fori_loop(0, lists[6 * ROW + 2], add, 0)
        for c in range(clusters):
            a, p0, p1, p2, p3 = (held[k * clusters + c] for k in range(5))
            out[:, c * C : (c + 1) * C] = (a + ((p0 + p3) + (p1 + p2)))[0:3]

    hbm = pl.BlockSpec(memory_space=pl.ANY)
    return pl.pallas_call(
        kernel,
        out_shape=jax.ShapeDtypeStruct((3, clusters * C), F32),
        in_specs=[pl.BlockSpec(memory_space=pltpu.SMEM)] + [hbm] * 5 + [pl.BlockSpec(memory_space=pltpu.VMEM)],
        out_specs=pl.BlockSpec(memory_space=pltpu.VMEM),
        scratch_shapes=[pltpu.VMEM((5 * clusters, 8, C), F32), pltpu.SemaphoreType.DMA((5,))],
        compiler_params=pltpu.CompilerParams(vmem_limit_bytes=VMEM_LIMIT),
    )(lists, sums, *boxes, made)


def body(positions, normals, areas, pair_first, pair_second, pair_count):
    geometry, lists = sort_out(positions, normals, areas, pair_first, pair_second, pair_count)
    low, far, sib, high, early = gather(geometry, lists)
    sums = near_field(lists, [low, far, geometry, sib, high], early, REACH)
    *boxes, late = give_back(sums, geometry, lists)
    return finish(sums, boxes, late, lists)


def solution(mesh):
    flat = P(("gx", "gy"))
    deep = P(None, ("gx", "gy"))
    return jax.shard_map(
        body, mesh=mesh, in_specs=(deep, deep, flat, flat, flat, flat), out_specs=deep, check_vma=False
    )
```

```python
import jax
import jax.numpy as jnp
from jax import lax
from jax.experimental import pallas as pl
from jax.experimental.pallas import tpu as pltpu
from jax.sharding import PartitionSpec as P

C = 256
REACH = 2
F32 = jnp.float32
BF = jnp.bfloat16
MESH = pl.DeviceIdType.MESH
VMEM_LIMIT = 60 * 2**20
INSIDE = 9
EARLY = 31
LATE = 23
ROW = 128
COUNTS = 6 * ROW
NUMBERS = 8 * ROW


def split3(t):
    a = t.astype(BF).astype(F32)
    r = t - a
    b = r.astype(BF).astype(F32)
    return a, b, r - b


def split2(t):
    a = t.astype(BF).astype(F32)
    return a, t - a


def wide(v):
    return jnp.broadcast_to(v, (8, C))


def row_index():
    return lax.broadcasted_iota(jnp.int32, (8, C), 0)


def prep(f, g, lhs_ref, rhs_ref, w_ref, keep_ref):
    row = row_index()
    isp = row < 3

    def at(k, v):
        return jnp.where(row == k, v, 0.0)

    af = wide(f[6:7, :])
    ag = wide(g[6:7, :])
    ctr = jnp.where(isp, wide(jnp.sum(f, axis=1, keepdims=True) * (1.0 / C)), 0.0)

    def parts(t):
        p = jnp.where(isp, t - ctr, 0.0)
        n = jnp.where(isp, pltpu.roll(t, 5, 0), 0.0)
        return p, n, wide(jnp.sum(p * p, axis=0, keepdims=True)), wide(jnp.sum(p * n, axis=0, keepdims=True))

    pf, nf, sf, cf = parts(f)
    pg, ng, sg, cg = parts(g)
    iaf = 1.0 / af
    iag = 1.0 / ag

    def left(t):
        u0, u1, u2 = split3(t)
        return jnp.concatenate([u0, u0, u0, u1, u1, u2], axis=0).T.astype(BF)

    def right(t):
        u0, u1, u2 = split3(t)
        return jnp.concatenate([u0, u1, u2, u0, u1, u0], axis=0).astype(BF)

    lhs_ref[0] = left(pf + at(3, sf + 1.0) + at(4, 1.0))
    lhs_ref[1] = left(af * (nf + at(3, cf) + pltpu.roll(pf, 4, 0) + at(7, 1.0)))
    rhs_ref[0] = right(-2.0 * pg + at(3, 1.0) + at(4, sg))
    rhs_ref[1] = right(ag * (at(3, 1.0) - pg))
    rhs_ref[2] = right(ag * (pltpu.roll(ng, 4, 0) - at(7, cg)))
    sums = (2.0 * nf, iaf * (at(6, 6.0) - 6.0 * pltpu.roll(pf, 3, 0)), iag * (6.0 * pg - at(3, 6.0)))
    for j, v in enumerate(sums):
        w_ref[j] = jnp.concatenate(split2(v), axis=0).astype(BF)
    for i, v in enumerate((nf, pf, iaf, ng, pg, iag)):
        keep_ref[i] = v


def terms(base, rows, sub, n, cs, lhs_ref, rhs_ref, l_ref, x_ref):
    def half(v):
        return v[:, :128] + v[:, 128:]

    big = slice(base, base + rows)
    left = lhs_ref[1, big, :]
    all_r2 = jnp.dot(lhs_ref[0, big, :], rhs_ref[0], preferred_element_type=F32)
    all_sf = jnp.dot(left, rhs_ref[1], preferred_element_type=F32)
    all_sg = jnp.dot(left, rhs_ref[2], preferred_element_type=F32)
    for s in range(0, rows, sub):
        sl = slice(base + s, base + s + sub)
        q = slice(s, s + sub)
        inv = 1.0 / all_r2[q]
        sf = all_sf[q]
        sg = all_sg[q]
        inv3 = inv * inv * inv
        lf = inv3 * sf
        lg = inv3 * sg
        rad = inv * (lf * sf + lg * sg)
        for j, v in ((0, lf), (2, rad)):
            h = v.astype(BF)
            l_ref[j, sl, :] = h
            l_ref[j + 1, sl, :] = (v - h.astype(F32)).astype(BF)
        for t in range(0, sub, 8):
            o = slice(t, t + 8)
            so = slice(base + s + t, base + s + t + 8)
            cs = cs + lg[o]
            x_ref[3, so, :] = half(lf[o])
            for k in range(3):
                x_ref[k, so, :] = half(lg[o] * n[k])
    return cs


def along(w, tile):
    return lax.dot_general(w, tile, (((1,), (0,)), ((), ())), preferred_element_type=F32)


def across(w, tile):
    return lax.dot_general(w, tile, (((1,), (1,)), ((), ())), preferred_element_type=F32)


def stage(h, now, before, ws, ks, load, save, rows=128, sub=16):
    lhs, rhs, w, keep, tiles, x, csr = now
    w_b, keep_b, tiles_b, x_b, csr_b = before[2:]
    ws[...] = w_b[...]
    ks[...] = keep_b[...]
    normal = [wide(keep[3, k : k + 1, :]) for k in range(3)]
    cs = jnp.zeros((8, C), F32)
    xs = [[None, None] for _ in range(4)]
    col = []
    rsum = []
    count = C // rows
    for c in range(count):
        cs = terms(c * rows, rows, sub, normal, cs, lhs, rhs, tiles, x)
        for e in range(c * 8 // count, (c + 1) * 8 // count):
            k, s = e // 2, e % 2
            xs[k][s] = jnp.sum(x_b[k, s * 128 : (s + 1) * 128, :].T, axis=0, keepdims=True)
            if e < 4:
                col.append(along(ws[e // 2], tiles_b[e]))
            elif e < 6:
                rsum.append(across(ws[2], tiles_b[e - 2]))
        if c == count // 2 - 1:
            prep(*load(h + 1), *before[:4])
    csr_old = csr_b[...]
    csr[...] = cs
    row = row_index()
    ct = (col[0] + col[1]) + (col[2] + col[3])
    rt = rsum[0] + rsum[1]
    ct = ct[0:8] + ct[8:16]
    rt = rt[0:8] + rt[8:16]
    nf, pf, iaf, ng, pg, iag = (ks[i] for i in range(6))
    xv = [wide(jnp.concatenate(v, axis=1)) for v in xs]
    lean = jnp.where(row == 0, xv[0], jnp.where(row == 1, xv[1], xv[2]))
    gf = 2.0 * (nf * xv[3] + lean) + iaf * (rt + pf * wide(rt[3:4]))
    csum = wide(jnp.sum(csr_old, axis=0, keepdims=True))
    gg = -(ct + ng * (2.0 * csum) + iag * (pltpu.roll(ct, 5, 0) + pg * wide(ct[6:7])))
    save(h - 1, gf, gg)


STAGE = [
    pltpu.VMEM((2, C, 48), BF),
    pltpu.VMEM((3, 48, C), BF),
    pltpu.VMEM((3, 16, C), BF),
    pltpu.VMEM((6, 8, C), F32),
    pltpu.VMEM((4, C, C), BF),
    pltpu.VMEM((4, C, 128), F32),
    pltpu.VMEM((8, C), F32),
]
KEPT = [pltpu.VMEM((3, 16, C), BF), pltpu.VMEM((6, 8, C), F32)]


def lanes(c):
    return pl.ds(pl.multiple_of(c * C, C), C)


def place(flat):
    inner = lax.axis_size("gy")
    total = lax.axis_size("gx") * inner
    flat = (flat + total) % total
    return (flat // inner, flat % inner)


def position():
    return lax.axis_index("gx") * lax.axis_size("gy") + lax.axis_index("gy")


def greet(devices):
    barrier = pltpu.get_barrier_semaphore()
    for d in devices:
        pl.semaphore_signal(barrier, inc=1, device_id=d, device_id_type=MESH)
    pl.semaphore_wait(barrier, len(devices))


def sort_out(positions, normals, areas, pair_first, pair_second, pair_count):
    faces = positions.shape[1]
    clusters = faces // C

    def kernel(pos, nor, area, pf, ps, count, geometry, lists):
        for c in range(clusters):
            sl = slice(c * C, (c + 1) * C)
            geometry[c, 0:3, :] = pos[:, sl]
            geometry[c, 3:6, :] = nor[:, sl]
            geometry[c, 6:7, :] = area[:, sl]
            geometry[c, 7:8, :] = jnp.zeros((1, C), F32)
        me = position()
        odd = me % 2

        def clear(i, carry):
            lists[i] = 0
            lists[ROW + i] = 0
            return carry

        lax.fori_loop(0, INSIDE + LATE + 2, clear, 0)
        for k in range(6):
            lists[COUNTS + k] = 0
        live = count[0]

        def one(j):
            s = ps[j]
            h = s // clusters - me
            outer = jnp.where(h == 2, 4, 2)
            inner = jnp.where(h == 1 - 2 * odd, 1, 3)
            k = jnp.where(h == 0, 0, jnp.where(jnp.abs(h) == 2, outer, inner))
            k = jnp.where(j < live, k, 5)
            n = lists[COUNTS + k]
            lists[k * ROW + n] = (pf[j] - me * clusters) * clusters + s % clusters
            lists[COUNTS + k] = n + 1

        def step(i, carry):
            for u in range(4):
                one(4 * i + u)
            return carry

        lax.fori_loop(0, (live + 3) // 4, step, 0)

    vmem = pl.BlockSpec(memory_space=pltpu.VMEM)
    smem = pl.BlockSpec(memory_space=pltpu.SMEM)
    return pl.pallas_call(
        kernel,
        out_shape=[jax.ShapeDtypeStruct((clusters, 8, C), F32), jax.ShapeDtypeStruct((NUMBERS,), jnp.int32)],
        in_specs=[vmem] * 3 + [smem] * 3,
        out_specs=[vmem, smem],
        compiler_params=pltpu.CompilerParams(vmem_limit_bytes=VMEM_LIMIT),
    )(positions, normals, areas.reshape(1, faces), pair_first, pair_second, pair_count)


def gather(geometry, lists, rows=7, chunks=4):
    clusters = geometry.shape[0]
    part = clusters // chunks

    def kernel(own, lists, told, low, far, sib, high, made, lo, fa, hi, near, seen, *refs):
        even, odds = refs[:7], refs[7:14]
        ws, ks, send, recv, fetch, news_send, news_recv = refs[14:]
        me = position()
        odd = me % 2
        up, down, other = place(me + 2), place(me - 2), place(me + 1 - 2 * odd)
        away = place(me - 1 + 2 * odd)
        mine = pltpu.make_async_copy(own, near, fetch.at[0])
        mine.start()
        again = pltpu.make_async_copy(own, seen.at[pl.ds(0, clusters)], fetch.at[2])
        again.start()
        above = me + 2 < lax.axis_size("gx") * lax.axis_size("gy")
        below = me >= 2
        greet((up, down, other, away))

        def move(kind, i, src, dst, device):
            sl = (pl.ds(i * part, part), pl.ds(0, rows))
            return pltpu.make_async_remote_copy(
                src_ref=src.at[sl],
                dst_ref=dst.at[sl],
                send_sem=send.at[kind, i],
                recv_sem=recv.at[kind, i],
                device_id=device,
                device_id_type=MESH,
            )

        news = [
            pltpu.make_async_remote_copy(
                src_ref=told,
                dst_ref=dst,
                send_sem=news_send.at[k],
                recv_sem=news_recv.at[k],
                device_id=device,
                device_id_type=MESH,
            )
            for k, (dst, device) in enumerate(((lo, up), (fa, away), (hi, down)))
        ]
        for c in news:
            c.start()
        for i in range(chunks):
            move(2, i, own, sib, other).start()

        @pl.when(above)
        def _():
            for i in range(chunks):
                move(0, i, own, low, up).start()

        @pl.when(below)
        def _():
            for i in range(chunks):
                move(1, i, own, high, down).start()

        mine.wait()

        def load(h):
            v = lists[ROW + jnp.minimum(h, EARLY) - INSIDE]
            return seen[v // clusters], seen[clusters + v % clusters]

        def save(h, gf, gg):
            made[h + 1, 0] = gf
            made[h + 1, 1] = gg

        def step(i, carry):
            stage(2 * i, even, odds, ws, ks, load, save)
            stage(2 * i + 1, odds, even, ws, ks, load, save)
            return carry

        def fresh(h):
            v = lists[h]
            return near[v // clusters], near[v % clusters]

        def inner(i, carry):
            stage(2 * i, even, odds, ws, ks, fresh, save)
            stage(2 * i + 1, odds, even, ws, ks, fresh, save)
            return carry

        prep(*fresh(0), *even[:4])
        lead = (INSIDE - 1) // 2
        lax.fori_loop(0, lead, inner, 0)
        for i in range(chunks):
            move(2, i, own, sib, other).wait_recv()
        beside = pltpu.make_async_copy(sib, seen.at[pl.ds(clusters, clusters)], fetch.at[1])
        beside.start()
        again.wait()
        beside.wait()
        halves = (EARLY + 1) // 2 - lead
        for i in range(chunks):
            lax.fori_loop(lead + i * halves // chunks, lead + (i + 1) * halves // chunks, step, 0)

            @pl.when(below)
            def _():
                move(0, i, own, low, up).wait_recv()

                @pl.when(odd == 1)
                def _():
                    move(3, i, low, far, other).start()

            @pl.when(above)
            def _():
                move(1, i, own, high, down).wait_recv()

                @pl.when(odd == 0)
                def _():
                    move(3, i, high, far, other).start()

        @pl.when(((odd == 0) & below) | ((odd == 1) & above))
        def _():
            for i in range(chunks):
                move(3, i, own, far, other).wait_recv()

        @pl.when(((odd == 0) & above) | ((odd == 1) & below))
        def _():
            for i in range(chunks):
                move(3, i, own, far, other).wait_send()

        @pl.when(above)
        def _():
            for i in range(chunks):
                move(0, i, own, low, up).wait_send()

        @pl.when(below)
        def _():
            for i in range(chunks):
                move(1, i, own, high, down).wait_send()

        for i in range(chunks):
            move(2, i, own, sib, other).wait_send()
        for c in news:
            c.wait()

    hbm = pl.BlockSpec(memory_space=pl.ANY)
    return pl.pallas_call(
        kernel,
        out_shape=[jax.ShapeDtypeStruct((clusters, 8, C), F32)] * 4
        + [jax.ShapeDtypeStruct((EARLY + 1, 2, 8, C), F32)]
        + [jax.ShapeDtypeStruct((NUMBERS,), jnp.int32)] * 3,
        in_specs=[hbm, pl.BlockSpec(memory_space=pltpu.SMEM), hbm],
        out_specs=[hbm] * 4 + [pl.BlockSpec(memory_space=pltpu.VMEM)] + [hbm] * 3,
        scratch_shapes=[pltpu.VMEM((clusters, 8, C), F32), pltpu.VMEM((2 * clusters, 8, C), F32)]
        + STAGE
        + STAGE
        + KEPT
        + [pltpu.SemaphoreType.DMA((4, chunks)), pltpu.SemaphoreType.DMA((4, chunks))]
        + [pltpu.SemaphoreType.DMA((3,))] * 3,
        compiler_params=pltpu.CompilerParams(
            collective_id=0, has_side_effects=True, vmem_limit_bytes=VMEM_LIMIT
        ),
    )(geometry, lists, lists)


def near_field(lists, news, geos, made):
    nwin = len(geos)
    clusters = geos[0].shape[0]

    def kernel(lists, lo, fa, hi, made, *refs):
        geo = refs[:nwin]
        acc, win, early = refs[nwin : nwin + 3]
        even = refs[nwin + 3 : nwin + 10]
        odd = refs[nwin + 10 : nwin + 17]
        ws, ks, work, sem = refs[nwin + 17 :]
        copies = [
            pltpu.make_async_copy(geo[k], win.at[pl.ds(k * clusters, clusters)], sem.at[k]) for k in range(nwin)
        ] + [pltpu.make_async_copy(made, early, sem.at[nwin])]
        for c in copies:
            c.start()

        def spare(ref):
            inside = jnp.maximum(ref[COUNTS] - INSIDE - LATE, 0)
            beside = jnp.maximum(ref[COUNTS + 1] - (EARLY - INSIDE), 0)
            return inside + beside + ref[COUNTS + 2] + ref[COUNTS + 3] + ref[COUNTS + 4]

        def enlist(n, ref, k, start, stop, first_at, second_at):
            def put(j, carry):
                v = ref[k * ROW + j]
                work[n + j - start] = first_at * clusters + v // clusters
                work[2 * ROW + n + j - start] = second_at * clusters + v % clusters
                return carry

            lax.fori_loop(start, stop, put, 0)
            return n + jnp.maximum(stop - start, 0)

        work[0] = 0
        work[2 * ROW] = 0
        mine = spare(lists)
        n = enlist(0, lists, 0, INSIDE + LATE, lists[COUNTS], REACH, REACH)
        n = enlist(n, lists, 1, EARLY - INSIDE, lists[COUNTS + 1], REACH, REACH + 1)
        for ref, k, theirs, at in ((lo, 2, 4, 0), (fa, 3, 3, 1), (hi, 4, 2, 4)):
            more = mine - spare(ref)
            given = jnp.clip(more // 4, 0, lists[COUNTS + k])
            taken = jnp.clip((0 - more) // 4, 0, ref[COUNTS + theirs])
            n = enlist(n, lists, k, given, lists[COUNTS + k], REACH, at)
            n = enlist(n, ref, theirs, 0, taken, at, REACH)
        acc[...] = jnp.zeros_like(acc)
        for c in copies:
            c.wait()
        last = jnp.maximum(n - 1, 0)

        def load(h):
            q = jnp.minimum(h, last)
            return win[work[q]], win[work[2 * ROW + q]]

        def save(h, gf, gg):
            live = (h >= 0) & (h < n)
            q = jnp.clip(h, 0, last)
            fi = work[q]
            si = work[2 * ROW + q]
            acc[fi] += jnp.where(live, gf, 0.0)
            acc[si] += jnp.where(live, gg, 0.0)

        prep(*load(0), *even[:4])

        def add(k, at, slot):
            def one(j, carry):
                v = lists[k * ROW + j]
                acc[REACH * clusters + v // clusters] += early[at + j, 0]
                acc[slot * clusters + v % clusters] += early[at + j, 1]
                return carry

            return one

        lax.fori_loop(0, jnp.minimum(lists[COUNTS], INSIDE), add(0, 1, REACH), 0)
        lax.fori_loop(0, jnp.minimum(lists[COUNTS + 1], EARLY - INSIDE), add(1, 1 + INSIDE, REACH + 1), 0)

        def step(i, carry):
            stage(2 * i, even, odd, ws, ks, load, save)
            stage(2 * i + 1, odd, even, ws, ks, load, save)
            return carry

        lax.fori_loop(0, (n + 2) // 2, step, 0)

    hbm = pl.BlockSpec(memory_space=pl.ANY)
    return pl.pallas_call(
        kernel,
        out_shape=jax.ShapeDtypeStruct((nwin * clusters, 8, C), F32),
        in_specs=[pl.BlockSpec(memory_space=pltpu.SMEM)] * 4 + [hbm] * (nwin + 1),
        out_specs=pl.BlockSpec(memory_space=pltpu.VMEM),
        scratch_shapes=[pltpu.VMEM((nwin * clusters, 8, C), F32)]
        + [pltpu.VMEM((EARLY + 1, 2, 8, C), F32)]
        + STAGE
        + STAGE
        + KEPT
        + [pltpu.SMEM((4 * ROW,), jnp.int32), pltpu.SemaphoreType.DMA((nwin + 1,))],
        compiler_params=pltpu.CompilerParams(vmem_limit_bytes=VMEM_LIMIT),
    )(lists, *news, made, *geos)


def give_back(sums, geometry, lists):
    clusters = geometry.shape[0]

    def kernel(sums, own, lists, *refs):
        boxes = refs[:4]
        made, seen = refs[4:6]
        even, odds = refs[6:13], refs[13:20]
        ws, ks, send, recv, fetch = refs[20:]
        me = position()
        odd = me % 2
        targets = (place(me - 2), place(me - 1 + 2 * odd), place(me + 1 - 2 * odd), place(me + 2))
        mine = pltpu.make_async_copy(own, seen, fetch.at[0])
        mine.start()
        greet(targets)
        copies = [
            pltpu.make_async_remote_copy(
                src_ref=sums.at[pl.ds(slot * clusters, clusters), pl.ds(0, 3)],
                dst_ref=boxes[k].at[:, pl.ds(0, 3)],
                send_sem=send.at[k],
                recv_sem=recv.at[k],
                device_id=device,
                device_id_type=MESH,
            )
            for k, (slot, device) in enumerate(zip((0, 1, 3, 4), targets, strict=True))
        ]
        for k in (0, 3, 1, 2):
            copies[k].start()
        mine.wait()

        def load(h):
            v = lists[INSIDE + jnp.minimum(h, LATE)]
            return seen[v // clusters], seen[v % clusters]

        def save(h, gf, gg):
            made[h + 1, 0] = gf
            made[h + 1, 1] = gg

        prep(*load(0), *even[:4])

        def step(i, carry):
            stage(2 * i, even, odds, ws, ks, load, save)
            stage(2 * i + 1, odds, even, ws, ks, load, save)
            return carry

        lax.fori_loop(0, (LATE + 1) // 2, step, 0)
        for c in copies:
            c.wait()

    hbm = pl.BlockSpec(memory_space=pl.ANY)
    return pl.pallas_call(
        kernel,
        out_shape=[jax.ShapeDtypeStruct((clusters, 8, C), F32)] * 4
        + [jax.ShapeDtypeStruct((LATE + 1, 2, 8, C), F32)],
        in_specs=[hbm] * 2 + [pl.BlockSpec(memory_space=pltpu.SMEM)],
        out_specs=[hbm] * 4 + [pl.BlockSpec(memory_space=pltpu.VMEM)],
        scratch_shapes=[pltpu.VMEM((clusters, 8, C), F32)]
        + STAGE
        + STAGE
        + KEPT
        + [pltpu.SemaphoreType.DMA((4,)), pltpu.SemaphoreType.DMA((4,)), pltpu.SemaphoreType.DMA((1,))],
        compiler_params=pltpu.CompilerParams(
            collective_id=1, has_side_effects=True, vmem_limit_bytes=VMEM_LIMIT
        ),
    )(sums, geometry, lists)


def finish(sums, boxes, made, lists):
    clusters = boxes[0].shape[0]

    def kernel(lists, sums, b0, b1, b2, b3, made, out, held, sem):
        lay = pl.ds(0, 3)
        sources = [sums.at[pl.ds(REACH * clusters, clusters), lay]] + [b.at[:, lay] for b in (b0, b1, b2, b3)]
        copies = [
            pltpu.make_async_copy(src, held.at[pl.ds(k * clusters, clusters), lay], sem.at[k])
            for k, src in enumerate(sources)
        ]
        for c in copies:
            c.start()
        for c in copies:
            c.wait()

        def add(j, carry):
            v = lists[INSIDE + j]
            held[v // clusters] += made[j + 1, 0]
            held[v % clusters] += made[j + 1, 1]
            return carry

        lax.fori_loop(0, jnp.clip(lists[COUNTS] - INSIDE, 0, LATE), add, 0)
        for c in range(clusters):
            a, p0, p1, p2, p3 = (held[k * clusters + c] for k in range(5))
            out[:, c * C : (c + 1) * C] = (a + ((p0 + p3) + (p1 + p2)))[0:3]

    hbm = pl.BlockSpec(memory_space=pl.ANY)
    return pl.pallas_call(
        kernel,
        out_shape=jax.ShapeDtypeStruct((3, clusters * C), F32),
        in_specs=[pl.BlockSpec(memory_space=pltpu.SMEM)] + [hbm] * 5 + [pl.BlockSpec(memory_space=pltpu.VMEM)],
        out_specs=pl.BlockSpec(memory_space=pltpu.VMEM),
        scratch_shapes=[pltpu.VMEM((5 * clusters, 8, C), F32), pltpu.SemaphoreType.DMA((5,))],
        compiler_params=pltpu.CompilerParams(vmem_limit_bytes=VMEM_LIMIT),
    )(lists, sums, *boxes, made)


def body(positions, normals, areas, pair_first, pair_second, pair_count):
    geometry, lists = sort_out(positions, normals, areas, pair_first, pair_second, pair_count)
    low, far, sib, high, early, *news = gather(geometry, lists)
    sums = near_field(lists, news, [low, far, geometry, sib, high], early)
    *boxes, late = give_back(sums, geometry, lists)
    return finish(sums, boxes, late, lists)


def solution(mesh):
    flat = P(("gx", "gy"))
    deep = P(None, ("gx", "gy"))
    return jax.shard_map(
        body, mesh=mesh, in_specs=(deep, deep, flat, flat, flat, flat), out_specs=deep, check_vma=False
    )
```

```python
import functools

import jax
import jax.numpy as jnp
from jax import lax
from jax.experimental import pallas as pl
from jax.experimental.pallas import tpu as pltpu
from jax.sharding import PartitionSpec as P

C = 256
REACH = 2
F32 = jnp.float32
BF = jnp.bfloat16
MESH = pl.DeviceIdType.MESH
VMEM_LIMIT = 60 * 2**20
INSIDE = 9
EARLY = 35
LATE = 23
ROW = 128
COUNTS = 6 * ROW
NUMBERS = 8 * ROW


def split3(t):
    a = t.astype(BF).astype(F32)
    r = t - a
    b = r.astype(BF).astype(F32)
    return a, b, r - b


def split2(t):
    a = t.astype(BF).astype(F32)
    return a, t - a


def wide(v):
    return jnp.broadcast_to(v, (8, C))


def row_index():
    return lax.broadcasted_iota(jnp.int32, (8, C), 0)


def prep(f, g, lhs_ref, rhs_ref, w_ref, keep_ref):
    row = row_index()
    isp = row < 3

    def at(k, v):
        return jnp.where(row == k, v, 0.0)

    af = wide(f[6:7, :])
    ag = wide(g[6:7, :])
    ctr = jnp.where(isp, wide(jnp.sum(f, axis=1, keepdims=True) * (1.0 / C)), 0.0)

    def parts(t):
        p = jnp.where(isp, t - ctr, 0.0)
        n = jnp.where(isp, pltpu.roll(t, 5, 0), 0.0)
        return p, n, wide(jnp.sum(p * p, axis=0, keepdims=True)), wide(jnp.sum(p * n, axis=0, keepdims=True))

    pf, nf, sf, cf = parts(f)
    pg, ng, sg, cg = parts(g)
    iaf = 1.0 / af
    iag = 1.0 / ag

    def left(t):
        u0, u1, u2 = split3(t)
        return jnp.concatenate([u0, u0, u0, u1, u1, u2], axis=0).T.astype(BF)

    def right(t):
        u0, u1, u2 = split3(t)
        return jnp.concatenate([u0, u1, u2, u0, u1, u0], axis=0).astype(BF)

    lhs_ref[0] = left(pf + at(3, sf + 1.0) + at(4, 1.0))
    lhs_ref[1] = left(af * (nf + at(3, cf) + pltpu.roll(pf, 4, 0) + at(7, 1.0)))
    rhs_ref[0] = right(-2.0 * pg + at(3, 1.0) + at(4, sg))
    rhs_ref[1] = right(ag * (at(3, 1.0) - pg))
    rhs_ref[2] = right(ag * (pltpu.roll(ng, 4, 0) - at(7, cg)))
    sums = (2.0 * nf, iaf * (at(6, 6.0) - 6.0 * pltpu.roll(pf, 3, 0)), iag * (6.0 * pg - at(3, 6.0)))
    for j, v in enumerate(sums):
        w_ref[j] = jnp.concatenate(split2(v), axis=0).astype(BF)
    for i, v in enumerate((nf, pf, iaf, ng, pg, iag)):
        keep_ref[i] = v


def terms(base, rows, sub, n, cs, lhs_ref, rhs_ref, l_ref, x_ref):
    def half(v):
        return v[:, :128] + v[:, 128:]

    big = slice(base, base + rows)
    left = lhs_ref[1, big, :]
    all_r2 = jnp.dot(lhs_ref[0, big, :], rhs_ref[0], preferred_element_type=F32)
    all_sf = jnp.dot(left, rhs_ref[1], preferred_element_type=F32)
    all_sg = jnp.dot(left, rhs_ref[2], preferred_element_type=F32)
    for s in range(0, rows, sub):
        sl = slice(base + s, base + s + sub)
        q = slice(s, s + sub)
        inv = 1.0 / all_r2[q]
        sf = all_sf[q]
        sg = all_sg[q]
        inv3 = inv * inv * inv
        lf = inv3 * sf
        lg = inv3 * sg
        rad = inv * (lf * sf + lg * sg)
        for j, v in ((0, lf), (2, rad)):
            h = v.astype(BF)
            l_ref[j, sl, :] = h
            l_ref[j + 1, sl, :] = (v - h.astype(F32)).astype(BF)
        for t in range(0, sub, 8):
            o = slice(t, t + 8)
            so = slice(base + s + t, base + s + t + 8)
            cs = cs + lg[o]
            x_ref[3, so, :] = half(lf[o])
            for k in range(3):
                x_ref[k, so, :] = half(lg[o] * n[k])
    return cs


def along(w, tile):
    return lax.dot_general(w, tile, (((1,), (0,)), ((), ())), preferred_element_type=F32)


def across(w, tile):
    return lax.dot_general(w, tile, (((1,), (1,)), ((), ())), preferred_element_type=F32)


def stage(h, now, before, ws, ks, load, save, rows=128, sub=16):
    lhs, rhs, w, keep, tiles, x, csr = now
    w_b, keep_b, tiles_b, x_b, csr_b = before[2:]
    ws[...] = w_b[...]
    ks[...] = keep_b[...]
    normal = [wide(keep[3, k : k + 1, :]) for k in range(3)]
    cs = jnp.zeros((8, C), F32)
    xs = [[None, None] for _ in range(4)]
    col = []
    rsum = []
    count = C // rows
    for c in range(count):
        cs = terms(c * rows, rows, sub, normal, cs, lhs, rhs, tiles, x)
        for e in range(c * 8 // count, (c + 1) * 8 // count):
            k, s = e // 2, e % 2
            xs[k][s] = jnp.sum(x_b[k, s * 128 : (s + 1) * 128, :].T, axis=0, keepdims=True)
            if e < 4:
                col.append(along(ws[e // 2], tiles_b[e]))
            elif e < 6:
                rsum.append(across(ws[2], tiles_b[e - 2]))
        if c == count // 2 - 1:
            prep(*load(h + 1), *before[:4])
    csr_old = csr_b[...]
    csr[...] = cs
    row = row_index()
    ct = (col[0] + col[1]) + (col[2] + col[3])
    rt = rsum[0] + rsum[1]
    ct = ct[0:8] + ct[8:16]
    rt = rt[0:8] + rt[8:16]
    nf, pf, iaf, ng, pg, iag = (ks[i] for i in range(6))
    xv = [wide(jnp.concatenate(v, axis=1)) for v in xs]
    lean = jnp.where(row == 0, xv[0], jnp.where(row == 1, xv[1], xv[2]))
    gf = 2.0 * (nf * xv[3] + lean) + iaf * (rt + pf * wide(rt[3:4]))
    csum = wide(jnp.sum(csr_old, axis=0, keepdims=True))
    gg = -(ct + ng * (2.0 * csum) + iag * (pltpu.roll(ct, 5, 0) + pg * wide(ct[6:7])))
    save(h - 1, gf, gg)


STAGE = [
    pltpu.VMEM((2, C, 48), BF),
    pltpu.VMEM((3, 48, C), BF),
    pltpu.VMEM((3, 16, C), BF),
    pltpu.VMEM((6, 8, C), F32),
    pltpu.VMEM((4, C, C), BF),
    pltpu.VMEM((4, C, 128), F32),
    pltpu.VMEM((8, C), F32),
]
KEPT = [pltpu.VMEM((3, 16, C), BF), pltpu.VMEM((6, 8, C), F32)]


def lanes(c):
    return pl.ds(pl.multiple_of(c * C, C), C)


def place(flat):
    inner = lax.axis_size("gy")
    total = lax.axis_size("gx") * inner
    flat = (flat + total) % total
    return (flat // inner, flat % inner)


def position():
    return lax.axis_index("gx") * lax.axis_size("gy") + lax.axis_index("gy")


def around(me):
    total = lax.axis_size("gx") * lax.axis_size("gy")
    odd = me % 2
    above = (2 * total - 3 - me) // total
    below = (me + total - 2) // total
    return above, below, odd * above + (1 - odd) * below


def greet(always, maybe, there):
    barrier = pltpu.get_barrier_semaphore()

    def tell(device):
        pl.semaphore_signal(barrier, inc=1, device_id=device, device_id_type=MESH)

    tell(always)
    for device, yes in zip(maybe, there, strict=True):
        pl.when(yes == 1)(functools.partial(tell, device))
    pl.semaphore_wait(barrier, 1 + there[0] + there[1] + there[2])


def sort_out(positions, normals, areas, pair_first, pair_second, pair_count):
    faces = positions.shape[1]
    clusters = faces // C

    def kernel(pos, nor, area, pf, ps, count, geometry, lists):
        for c in range(clusters):
            sl = slice(c * C, (c + 1) * C)
            geometry[c, 0:3, :] = pos[:, sl]
            geometry[c, 3:6, :] = nor[:, sl]
            geometry[c, 6:7, :] = area[:, sl]
            geometry[c, 7:8, :] = jnp.zeros((1, C), F32)
        me = position()
        odd = me % 2

        def clear(i, carry):
            lists[i] = 0
            lists[ROW + i] = 0
            return carry

        lax.fori_loop(0, INSIDE + LATE + 2, clear, 0)
        for k in range(6):
            lists[COUNTS + k] = 0
        live = count[0]

        def one(j):
            s = ps[j]
            h = s // clusters - me
            outer = jnp.where(h == 2, 4, 2)
            inner = jnp.where(h == 1 - 2 * odd, 1, 3)
            k = jnp.where(h == 0, 0, jnp.where(jnp.abs(h) == 2, outer, inner))
            k = jnp.where(j < live, k, 5)
            n = lists[COUNTS + k]
            lists[k * ROW + n] = (pf[j] - me * clusters) * clusters + s % clusters
            lists[COUNTS + k] = n + 1

        def step(i, carry):
            for u in range(4):
                one(4 * i + u)
            return carry

        lax.fori_loop(0, (live + 3) // 4, step, 0)

    vmem = pl.BlockSpec(memory_space=pltpu.VMEM)
    smem = pl.BlockSpec(memory_space=pltpu.SMEM)
    return pl.pallas_call(
        kernel,
        out_shape=[jax.ShapeDtypeStruct((clusters, 8, C), F32), jax.ShapeDtypeStruct((NUMBERS,), jnp.int32)],
        in_specs=[vmem] * 3 + [smem] * 3,
        out_specs=[vmem, smem],
        compiler_params=pltpu.CompilerParams(vmem_limit_bytes=VMEM_LIMIT),
    )(positions, normals, areas.reshape(1, faces), pair_first, pair_second, pair_count)


def gather(geometry, lists, rows=7, chunks=4):
    clusters = geometry.shape[0]
    part = clusters // chunks

    def kernel(own, lists, told, low, far, sib, high, made, lo, fa, hi, near, seen, *refs):
        even, odds = refs[:7], refs[7:14]
        ws, ks, send, recv, fetch, news_send, news_recv = refs[14:]
        me = position()
        odd = me % 2
        up, down, other = place(me + 2), place(me - 2), place(me + 1 - 2 * odd)
        away = place(me - 1 + 2 * odd)
        mine = pltpu.make_async_copy(own, near, fetch.at[0])
        mine.start()
        again = pltpu.make_async_copy(own, seen.at[pl.ds(0, clusters)], fetch.at[2])
        again.start()
        there = around(me)
        greet(other, (up, down, away), there)
        above, below, beyond = (yes == 1 for yes in there)

        def move(kind, i, src, dst, device):
            sl = (pl.ds(i * part, part), pl.ds(0, rows))
            return pltpu.make_async_remote_copy(
                src_ref=src.at[sl],
                dst_ref=dst.at[sl],
                send_sem=send.at[kind, i],
                recv_sem=recv.at[kind, i],
                device_id=device,
                device_id_type=MESH,
            )

        news = [
            pltpu.make_async_remote_copy(
                src_ref=told,
                dst_ref=dst,
                send_sem=news_send.at[k],
                recv_sem=news_recv.at[k],
                device_id=device,
                device_id_type=MESH,
            )
            for k, (dst, device) in enumerate(((lo, up), (fa, away), (hi, down)))
        ]
        for c, yes in zip(news, (above, beyond, below), strict=True):
            pl.when(yes)(c.start)
        for i in range(chunks):
            move(2, i, own, sib, other).start()

        @pl.when(above)
        def _():
            for i in range(chunks):
                move(0, i, own, low, up).start()

        @pl.when(below)
        def _():
            for i in range(chunks):
                move(1, i, own, high, down).start()

        mine.wait()

        def load(h):
            v = lists[ROW + jnp.minimum(h, EARLY) - INSIDE]
            return seen[v // clusters], seen[clusters + v % clusters]

        def save(h, gf, gg):
            made[h + 1, 0] = gf
            made[h + 1, 1] = gg

        def step(i, carry):
            stage(2 * i, even, odds, ws, ks, load, save)
            stage(2 * i + 1, odds, even, ws, ks, load, save)
            return carry

        def fresh(h):
            v = lists[h]
            return near[v // clusters], near[v % clusters]

        def inner(i, carry):
            stage(2 * i, even, odds, ws, ks, fresh, save)
            stage(2 * i + 1, odds, even, ws, ks, fresh, save)
            return carry

        prep(*fresh(0), *even[:4])
        lead = (INSIDE - 1) // 2
        lax.fori_loop(0, lead, inner, 0)
        for i in range(chunks):
            move(2, i, own, sib, other).wait_recv()
        beside = pltpu.make_async_copy(sib, seen.at[pl.ds(clusters, clusters)], fetch.at[1])
        beside.start()
        again.wait()
        beside.wait()
        halves = (EARLY + 1) // 2 - lead
        for i in range(chunks):
            lax.fori_loop(lead + i * halves // chunks, lead + (i + 1) * halves // chunks, step, 0)

            @pl.when(below)
            def _():
                move(0, i, own, low, up).wait_recv()

                @pl.when(odd == 1)
                def _():
                    move(3, i, low, far, other).start()

            @pl.when(above)
            def _():
                move(1, i, own, high, down).wait_recv()

                @pl.when(odd == 0)
                def _():
                    move(3, i, high, far, other).start()

        @pl.when(beyond)
        def _():
            for i in range(chunks):
                move(3, i, own, far, other).wait_recv()

        @pl.when(((odd == 0) & above) | ((odd == 1) & below))
        def _():
            for i in range(chunks):
                move(3, i, own, far, other).wait_send()

        @pl.when(above)
        def _():
            for i in range(chunks):
                move(0, i, own, low, up).wait_send()

        @pl.when(below)
        def _():
            for i in range(chunks):
                move(1, i, own, high, down).wait_send()

        for i in range(chunks):
            move(2, i, own, sib, other).wait_send()
        for c, there_in, there_out in zip(news, (below, beyond, above), (above, beyond, below), strict=True):
            pl.when(there_in)(c.wait_recv)
            pl.when(there_out)(c.wait_send)

    hbm = pl.BlockSpec(memory_space=pl.ANY)
    return pl.pallas_call(
        kernel,
        out_shape=[jax.ShapeDtypeStruct((clusters, 8, C), F32)] * 4
        + [jax.ShapeDtypeStruct((EARLY + 1, 2, 8, C), F32)]
        + [jax.ShapeDtypeStruct((NUMBERS,), jnp.int32)] * 3,
        in_specs=[hbm, pl.BlockSpec(memory_space=pltpu.SMEM), hbm],
        out_specs=[hbm] * 4 + [pl.BlockSpec(memory_space=pltpu.VMEM)] + [hbm] * 3,
        scratch_shapes=[pltpu.VMEM((clusters, 8, C), F32), pltpu.VMEM((2 * clusters, 8, C), F32)]
        + STAGE
        + STAGE
        + KEPT
        + [pltpu.SemaphoreType.DMA((4, chunks)), pltpu.SemaphoreType.DMA((4, chunks))]
        + [pltpu.SemaphoreType.DMA((3,))] * 3,
        compiler_params=pltpu.CompilerParams(
            collective_id=0, has_side_effects=True, vmem_limit_bytes=VMEM_LIMIT
        ),
    )(geometry, lists, lists)


def near_field(lists, news, geos, made):
    nwin = len(geos)
    clusters = geos[0].shape[0]

    def kernel(lists, lo, fa, hi, made, *refs):
        geo = refs[:nwin]
        acc, win, early = refs[nwin : nwin + 3]
        even = refs[nwin + 3 : nwin + 10]
        odd = refs[nwin + 10 : nwin + 17]
        ws, ks, work, sem = refs[nwin + 17 :]
        copies = [
            pltpu.make_async_copy(geo[k], win.at[pl.ds(k * clusters, clusters)], sem.at[k]) for k in range(nwin)
        ] + [pltpu.make_async_copy(made, early, sem.at[nwin])]
        for c in copies:
            c.start()

        def spare(ref):
            inside = jnp.maximum(ref[COUNTS] - INSIDE - LATE, 0)
            beside = jnp.maximum(ref[COUNTS + 1] - (EARLY - INSIDE), 0)
            return inside + beside + ref[COUNTS + 2] + ref[COUNTS + 3] + ref[COUNTS + 4]

        def enlist(n, ref, k, start, stop, first_at, second_at):
            def put(j, carry):
                v = ref[k * ROW + j]
                work[n + j - start] = first_at * clusters + v // clusters
                work[2 * ROW + n + j - start] = second_at * clusters + v % clusters
                return carry

            lax.fori_loop(start, stop, put, 0)
            return n + jnp.maximum(stop - start, 0)

        work[0] = 0
        work[2 * ROW] = 0
        mine = spare(lists)
        above, below, beyond = around(position())
        n = enlist(0, lists, 0, INSIDE + LATE, lists[COUNTS], REACH, REACH)
        n = enlist(n, lists, 1, EARLY - INSIDE, lists[COUNTS + 1], REACH, REACH + 1)
        for ref, k, theirs, at, there in ((lo, 2, 4, 0, below), (fa, 3, 3, 1, beyond), (hi, 4, 2, 4, above)):
            more = mine - spare(ref)
            given = jnp.clip(more // 4, 0, lists[COUNTS + k])
            taken = jnp.where(there == 1, jnp.clip((0 - more) // 4, 0, ref[COUNTS + theirs]), 0)
            n = enlist(n, lists, k, given, lists[COUNTS + k], REACH, at)
            n = enlist(n, ref, theirs, 0, taken, at, REACH)
        acc[...] = jnp.zeros_like(acc)
        for c in copies:
            c.wait()
        last = jnp.maximum(n - 1, 0)

        def load(h):
            q = jnp.minimum(h, last)
            return win[work[q]], win[work[2 * ROW + q]]

        def save(h, gf, gg):
            live = (h >= 0) & (h < n)
            q = jnp.clip(h, 0, last)
            fi = work[q]
            si = work[2 * ROW + q]
            acc[fi] += jnp.where(live, gf, 0.0)
            acc[si] += jnp.where(live, gg, 0.0)

        prep(*load(0), *even[:4])

        def add(k, at, slot):
            def one(j, carry):
                v = lists[k * ROW + j]
                acc[REACH * clusters + v // clusters] += early[at + j, 0]
                acc[slot * clusters + v % clusters] += early[at + j, 1]
                return carry

            return one

        lax.fori_loop(0, jnp.minimum(lists[COUNTS], INSIDE), add(0, 1, REACH), 0)
        lax.fori_loop(0, jnp.minimum(lists[COUNTS + 1], EARLY - INSIDE), add(1, 1 + INSIDE, REACH + 1), 0)

        def step(i, carry):
            stage(2 * i, even, odd, ws, ks, load, save)
            stage(2 * i + 1, odd, even, ws, ks, load, save)
            return carry

        lax.fori_loop(0, (n + 2) // 2, step, 0)

    hbm = pl.BlockSpec(memory_space=pl.ANY)
    return pl.pallas_call(
        kernel,
        out_shape=jax.ShapeDtypeStruct((nwin * clusters, 8, C), F32),
        in_specs=[pl.BlockSpec(memory_space=pltpu.SMEM)] * 4 + [hbm] * (nwin + 1),
        out_specs=pl.BlockSpec(memory_space=pltpu.VMEM),
        scratch_shapes=[pltpu.VMEM((nwin * clusters, 8, C), F32)]
        + [pltpu.VMEM((EARLY + 1, 2, 8, C), F32)]
        + STAGE
        + STAGE
        + KEPT
        + [pltpu.SMEM((4 * ROW,), jnp.int32), pltpu.SemaphoreType.DMA((nwin + 1,))],
        compiler_params=pltpu.CompilerParams(vmem_limit_bytes=VMEM_LIMIT),
    )(lists, *news, made, *geos)


def give_back(sums, geometry, lists):
    clusters = geometry.shape[0]

    def kernel(sums, own, lists, *refs):
        boxes = refs[:4]
        made, seen = refs[4:6]
        even, odds = refs[6:13], refs[13:20]
        ws, ks, send, recv, fetch = refs[20:]
        me = position()
        odd = me % 2
        targets = (place(me - 2), place(me - 1 + 2 * odd), place(me + 1 - 2 * odd), place(me + 2))
        mine = pltpu.make_async_copy(own, seen, fetch.at[0])
        mine.start()
        there = around(me)
        greet(targets[2], (targets[3], targets[0], targets[1]), there)
        above, below, beyond = (yes == 1 for yes in there)
        copies = [
            pltpu.make_async_remote_copy(
                src_ref=sums.at[pl.ds(slot * clusters, clusters), pl.ds(0, 3)],
                dst_ref=boxes[k].at[:, pl.ds(0, 3)],
                send_sem=send.at[k],
                recv_sem=recv.at[k],
                device_id=device,
                device_id_type=MESH,
            )
            for k, (slot, device) in enumerate(zip((0, 1, 3, 4), targets, strict=True))
        ]
        pl.when(below)(copies[0].start)
        pl.when(above)(copies[3].start)
        pl.when(beyond)(copies[1].start)
        copies[2].start()
        mine.wait()

        def load(h):
            v = lists[INSIDE + jnp.minimum(h, LATE)]
            return seen[v // clusters], seen[v % clusters]

        def save(h, gf, gg):
            made[h + 1, 0] = gf
            made[h + 1, 1] = gg

        prep(*load(0), *even[:4])

        def step(i, carry):
            stage(2 * i, even, odds, ws, ks, load, save)
            stage(2 * i + 1, odds, even, ws, ks, load, save)
            return carry

        lax.fori_loop(0, (LATE + 1) // 2, step, 0)
        pl.when(below)(copies[0].wait_send)
        pl.when(above)(copies[0].wait_recv)
        pl.when(above)(copies[3].wait_send)
        pl.when(below)(copies[3].wait_recv)
        pl.when(beyond)(copies[1].wait)
        copies[2].wait()

    hbm = pl.BlockSpec(memory_space=pl.ANY)
    return pl.pallas_call(
        kernel,
        out_shape=[jax.ShapeDtypeStruct((clusters, 8, C), F32)] * 4
        + [jax.ShapeDtypeStruct((LATE + 1, 2, 8, C), F32)],
        in_specs=[hbm] * 2 + [pl.BlockSpec(memory_space=pltpu.SMEM)],
        out_specs=[hbm] * 4 + [pl.BlockSpec(memory_space=pltpu.VMEM)],
        scratch_shapes=[pltpu.VMEM((clusters, 8, C), F32)]
        + STAGE
        + STAGE
        + KEPT
        + [pltpu.SemaphoreType.DMA((4,)), pltpu.SemaphoreType.DMA((4,)), pltpu.SemaphoreType.DMA((1,))],
        compiler_params=pltpu.CompilerParams(
            collective_id=1, has_side_effects=True, vmem_limit_bytes=VMEM_LIMIT
        ),
    )(sums, geometry, lists)


def finish(sums, boxes, made, lists):
    clusters = boxes[0].shape[0]

    def kernel(lists, sums, b0, b1, b2, b3, made, out, held, sem):
        lay = pl.ds(0, 3)
        above, below, beyond = around(position())
        sources = [sums.at[pl.ds(REACH * clusters, clusters), lay]] + [b.at[:, lay] for b in (b0, b1, b2, b3)]
        copies = [
            pltpu.make_async_copy(src, held.at[pl.ds(k * clusters, clusters), lay], sem.at[k])
            for k, src in enumerate(sources)
        ]
        for c in copies:
            c.start()
        for c in copies:
            c.wait()

        def add(j, carry):
            v = lists[INSIDE + j]
            held[v // clusters] += made[j + 1, 0]
            held[v % clusters] += made[j + 1, 1]
            return carry

        lax.fori_loop(0, jnp.clip(lists[COUNTS] - INSIDE, 0, LATE), add, 0)
        for c in range(clusters):
            a, p0, p1, p2, p3 = (held[k * clusters + c] for k in range(5))
            p0, p1, p3 = (jnp.where(yes == 1, p, 0.0) for p, yes in ((p0, above), (p1, beyond), (p3, below)))
            out[:, c * C : (c + 1) * C] = (a + ((p0 + p3) + (p1 + p2)))[0:3]

    hbm = pl.BlockSpec(memory_space=pl.ANY)
    return pl.pallas_call(
        kernel,
        out_shape=jax.ShapeDtypeStruct((3, clusters * C), F32),
        in_specs=[pl.BlockSpec(memory_space=pltpu.SMEM)] + [hbm] * 5 + [pl.BlockSpec(memory_space=pltpu.VMEM)],
        out_specs=pl.BlockSpec(memory_space=pltpu.VMEM),
        scratch_shapes=[pltpu.VMEM((5 * clusters, 8, C), F32), pltpu.SemaphoreType.DMA((5,))],
        compiler_params=pltpu.CompilerParams(vmem_limit_bytes=VMEM_LIMIT),
    )(lists, sums, *boxes, made)


def body(positions, normals, areas, pair_first, pair_second, pair_count):
    geometry, lists = sort_out(positions, normals, areas, pair_first, pair_second, pair_count)
    low, far, sib, high, early, *news = gather(geometry, lists)
    sums = near_field(lists, news, [low, far, geometry, sib, high], early)
    *boxes, late = give_back(sums, geometry, lists)
    return finish(sums, boxes, late, lists)


def solution(mesh):
    flat = P(("gx", "gy"))
    deep = P(None, ("gx", "gy"))
    return jax.shard_map(
        body, mesh=mesh, in_specs=(deep, deep, flat, flat, flat, flat), out_specs=deep, check_vma=False
    )
```

```python
import functools

import jax
import jax.numpy as jnp
from jax import lax
from jax.experimental import pallas as pl
from jax.experimental.pallas import tpu as pltpu
from jax.sharding import PartitionSpec as P

C = 256
REACH = 2
F32 = jnp.float32
BF = jnp.bfloat16
MESH = pl.DeviceIdType.MESH
VMEM_LIMIT = 60 * 2**20
INSIDE = 9
EARLY = 35
LATE = 19
ROW = 128
COUNTS = 6 * ROW
NUMBERS = 8 * ROW


def split3(t):
    a = t.astype(BF).astype(F32)
    r = t - a
    b = r.astype(BF).astype(F32)
    return a, b, r - b


def split2(t):
    a = t.astype(BF).astype(F32)
    return a, t - a


def wide(v):
    return jnp.broadcast_to(v, (8, C))


def row_index():
    return lax.broadcasted_iota(jnp.int32, (8, C), 0)


def prep(f, g, lhs_ref, rhs_ref, w_ref, keep_ref):
    row = row_index()
    isp = row < 3

    def at(k, v):
        return jnp.where(row == k, v, 0.0)

    af = wide(f[6:7, :])
    ag = wide(g[6:7, :])
    ctr = jnp.where(isp, wide(jnp.sum(f, axis=1, keepdims=True) * (1.0 / C)), 0.0)

    def parts(t):
        p = jnp.where(isp, t - ctr, 0.0)
        n = jnp.where(isp, pltpu.roll(t, 5, 0), 0.0)
        return p, n, wide(jnp.sum(p * p, axis=0, keepdims=True)), wide(jnp.sum(p * n, axis=0, keepdims=True))

    pf, nf, sf, cf = parts(f)
    pg, ng, sg, cg = parts(g)
    iaf = 1.0 / af
    iag = 1.0 / ag

    def left(t):
        u0, u1, u2 = split3(t)
        return jnp.concatenate([u0, u0, u0, u1, u1, u2], axis=0).T.astype(BF)

    def right(t):
        u0, u1, u2 = split3(t)
        return jnp.concatenate([u0, u1, u2, u0, u1, u0], axis=0).astype(BF)

    lhs_ref[0] = left(pf + at(3, sf + 1.0) + at(4, 1.0))
    lhs_ref[1] = left(af * (nf + at(3, cf) + pltpu.roll(pf, 4, 0) + at(7, 1.0)))
    rhs_ref[0] = right(-2.0 * pg + at(3, 1.0) + at(4, sg))
    rhs_ref[1] = right(ag * (at(3, 1.0) - pg))
    rhs_ref[2] = right(ag * (pltpu.roll(ng, 4, 0) - at(7, cg)))
    sums = (2.0 * nf, iaf * (at(6, 6.0) - 6.0 * pltpu.roll(pf, 3, 0)), iag * (6.0 * pg - at(3, 6.0)))
    for j, v in enumerate(sums):
        w_ref[j] = jnp.concatenate(split2(v), axis=0).astype(BF)
    for i, v in enumerate((nf, pf, iaf, ng, pg, iag)):
        keep_ref[i] = v


def terms(base, rows, sub, n, cs, lhs_ref, rhs_ref, l_ref, x_ref):
    def half(v):
        return v[:, :128] + v[:, 128:]

    big = slice(base, base + rows)
    left = lhs_ref[1, big, :]
    all_r2 = jnp.dot(lhs_ref[0, big, :], rhs_ref[0], preferred_element_type=F32)
    all_sf = jnp.dot(left, rhs_ref[1], preferred_element_type=F32)
    all_sg = jnp.dot(left, rhs_ref[2], preferred_element_type=F32)
    for s in range(0, rows, sub):
        sl = slice(base + s, base + s + sub)
        q = slice(s, s + sub)
        inv = 1.0 / all_r2[q]
        sf = all_sf[q]
        sg = all_sg[q]
        inv3 = inv * inv * inv
        lf = inv3 * sf
        lg = inv3 * sg
        rad = inv * (lf * sf + lg * sg)
        for j, v in ((0, lf), (2, rad)):
            h = v.astype(BF)
            l_ref[j, sl, :] = h
            l_ref[j + 1, sl, :] = (v - h.astype(F32)).astype(BF)
        for t in range(0, sub, 8):
            o = slice(t, t + 8)
            so = slice(base + s + t, base + s + t + 8)
            cs = cs + lg[o]
            x_ref[3, so, :] = half(lf[o])
            for k in range(3):
                x_ref[k, so, :] = half(lg[o] * n[k])
    return cs


def along(w, tile):
    return lax.dot_general(w, tile, (((1,), (0,)), ((), ())), preferred_element_type=F32)


def across(w, tile):
    return lax.dot_general(w, tile, (((1,), (1,)), ((), ())), preferred_element_type=F32)


def stage(h, now, before, ws, ks, load, save, rows=128, sub=16):
    lhs, rhs, w, keep, tiles, x, csr = now
    w_b, keep_b, tiles_b, x_b, csr_b = before[2:]
    ws[...] = w_b[...]
    ks[...] = keep_b[...]
    normal = [wide(keep[3, k : k + 1, :]) for k in range(3)]
    cs = jnp.zeros((8, C), F32)
    xs = [[None, None] for _ in range(4)]
    col = []
    rsum = []
    count = C // rows
    for c in range(count):
        cs = terms(c * rows, rows, sub, normal, cs, lhs, rhs, tiles, x)
        for e in range(c * 8 // count, (c + 1) * 8 // count):
            k, s = e // 2, e % 2
            xs[k][s] = jnp.sum(x_b[k, s * 128 : (s + 1) * 128, :].T, axis=0, keepdims=True)
            if e < 4:
                col.append(along(ws[e // 2], tiles_b[e]))
            elif e < 6:
                rsum.append(across(ws[2], tiles_b[e - 2]))
        if c == count // 2 - 1:
            prep(*load(h + 1), *before[:4])
    csr_old = csr_b[...]
    csr[...] = cs
    row = row_index()
    ct = (col[0] + col[1]) + (col[2] + col[3])
    rt = rsum[0] + rsum[1]
    ct = ct[0:8] + ct[8:16]
    rt = rt[0:8] + rt[8:16]
    nf, pf, iaf, ng, pg, iag = (ks[i] for i in range(6))
    xv = [wide(jnp.concatenate(v, axis=1)) for v in xs]
    lean = jnp.where(row == 0, xv[0], jnp.where(row == 1, xv[1], xv[2]))
    gf = 2.0 * (nf * xv[3] + lean) + iaf * (rt + pf * wide(rt[3:4]))
    csum = wide(jnp.sum(csr_old, axis=0, keepdims=True))
    gg = -(ct + ng * (2.0 * csum) + iag * (pltpu.roll(ct, 5, 0) + pg * wide(ct[6:7])))
    save(h - 1, gf, gg)


STAGE = [
    pltpu.VMEM((2, C, 48), BF),
    pltpu.VMEM((3, 48, C), BF),
    pltpu.VMEM((3, 16, C), BF),
    pltpu.VMEM((6, 8, C), F32),
    pltpu.VMEM((4, C, C), BF),
    pltpu.VMEM((4, C, 128), F32),
    pltpu.VMEM((8, C), F32),
]
KEPT = [pltpu.VMEM((3, 16, C), BF), pltpu.VMEM((6, 8, C), F32)]


def lanes(c):
    return pl.ds(pl.multiple_of(c * C, C), C)


def place(flat):
    inner = lax.axis_size("gy")
    total = lax.axis_size("gx") * inner
    flat = (flat + total) % total
    return (flat // inner, flat % inner)


def position():
    return lax.axis_index("gx") * lax.axis_size("gy") + lax.axis_index("gy")


def around(me):
    total = lax.axis_size("gx") * lax.axis_size("gy")
    odd = me % 2
    above = (2 * total - 3 - me) // total
    below = (me + total - 2) // total
    return above, below, odd * above + (1 - odd) * below


def greet(always, maybe, there):
    barrier = pltpu.get_barrier_semaphore()

    def tell(device):
        pl.semaphore_signal(barrier, inc=1, device_id=device, device_id_type=MESH)

    tell(always)
    for device, yes in zip(maybe, there, strict=True):
        pl.when(yes == 1)(functools.partial(tell, device))
    pl.semaphore_wait(barrier, 1 + there[0] + there[1] + there[2])


def sort_out(positions, normals, areas, pair_first, pair_second, pair_count):
    faces = positions.shape[1]
    clusters = faces // C

    def kernel(pos, nor, area, pf, ps, count, geometry, lists):
        for c in range(clusters):
            sl = slice(c * C, (c + 1) * C)
            geometry[c, 0:3, :] = pos[:, sl]
            geometry[c, 3:6, :] = nor[:, sl]
            geometry[c, 6:7, :] = area[:, sl]
            geometry[c, 7:8, :] = jnp.zeros((1, C), F32)
        me = position()
        odd = me % 2

        def clear(i, carry):
            lists[i] = 0
            lists[ROW + i] = 0
            return carry

        lax.fori_loop(0, INSIDE + LATE + 2, clear, 0)
        for k in range(6):
            lists[COUNTS + k] = 0
        live = count[0]

        def one(j):
            s = ps[j]
            h = s // clusters - me
            outer = jnp.where(h == 2, 4, 2)
            inner = jnp.where(h == 1 - 2 * odd, 1, 3)
            k = jnp.where(h == 0, 0, jnp.where(jnp.abs(h) == 2, outer, inner))
            k = jnp.where(j < live, k, 5)
            n = lists[COUNTS + k]
            lists[k * ROW + n] = (pf[j] - me * clusters) * clusters + s % clusters
            lists[COUNTS + k] = n + 1

        def step(i, carry):
            for u in range(4):
                one(4 * i + u)
            return carry

        lax.fori_loop(0, (live + 3) // 4, step, 0)

    vmem = pl.BlockSpec(memory_space=pltpu.VMEM)
    smem = pl.BlockSpec(memory_space=pltpu.SMEM)
    return pl.pallas_call(
        kernel,
        out_shape=[jax.ShapeDtypeStruct((clusters, 8, C), F32), jax.ShapeDtypeStruct((NUMBERS,), jnp.int32)],
        in_specs=[vmem] * 3 + [smem] * 3,
        out_specs=[vmem, smem],
        compiler_params=pltpu.CompilerParams(vmem_limit_bytes=VMEM_LIMIT),
    )(positions, normals, areas.reshape(1, faces), pair_first, pair_second, pair_count)


def gather(geometry, lists, rows=7, chunks=4):
    clusters = geometry.shape[0]
    part = clusters // chunks

    def kernel(own, lists, told, low, far, sib, high, made, lo, fa, hi, near, seen, *refs):
        even, odds = refs[:7], refs[7:14]
        ws, ks, send, recv, fetch, news_send, news_recv = refs[14:]
        me = position()
        odd = me % 2
        up, down, other = place(me + 2), place(me - 2), place(me + 1 - 2 * odd)
        away = place(me - 1 + 2 * odd)
        mine = pltpu.make_async_copy(own, near, fetch.at[0])
        mine.start()
        again = pltpu.make_async_copy(own, seen.at[pl.ds(0, clusters)], fetch.at[2])
        again.start()
        there = around(me)
        greet(other, (up, down, away), there)
        above, below, beyond = (yes == 1 for yes in there)

        def move(kind, i, src, dst, device):
            sl = (pl.ds(i * part, part), pl.ds(0, rows))
            return pltpu.make_async_remote_copy(
                src_ref=src.at[sl],
                dst_ref=dst.at[sl],
                send_sem=send.at[kind, i],
                recv_sem=recv.at[kind, i],
                device_id=device,
                device_id_type=MESH,
            )

        news = [
            pltpu.make_async_remote_copy(
                src_ref=told,
                dst_ref=dst,
                send_sem=news_send.at[k],
                recv_sem=news_recv.at[k],
                device_id=device,
                device_id_type=MESH,
            )
            for k, (dst, device) in enumerate(((lo, up), (fa, away), (hi, down)))
        ]
        for c, yes in zip(news, (above, beyond, below), strict=True):
            pl.when(yes)(c.start)
        for i in range(chunks):
            move(2, i, own, sib, other).start()

        @pl.when(above)
        def _():
            for i in range(chunks):
                move(0, i, own, low, up).start()

        @pl.when(below)
        def _():
            for i in range(chunks):
                move(1, i, own, high, down).start()

        mine.wait()

        def load(h):
            v = lists[ROW + jnp.minimum(h, EARLY) - INSIDE]
            return seen[v // clusters], seen[clusters + v % clusters]

        def save(h, gf, gg):
            made[h + 1, 0] = gf
            made[h + 1, 1] = gg

        def step(i, carry):
            stage(2 * i, even, odds, ws, ks, load, save)
            stage(2 * i + 1, odds, even, ws, ks, load, save)
            return carry

        def fresh(h):
            v = lists[h]
            return near[v // clusters], near[v % clusters]

        def inner(i, carry):
            stage(2 * i, even, odds, ws, ks, fresh, save)
            stage(2 * i + 1, odds, even, ws, ks, fresh, save)
            return carry

        prep(*fresh(0), *even[:4])
        lead = (INSIDE - 1) // 2
        lax.fori_loop(0, lead, inner, 0)
        for i in range(chunks):
            move(2, i, own, sib, other).wait_recv()
        beside = pltpu.make_async_copy(sib, seen.at[pl.ds(clusters, clusters)], fetch.at[1])
        beside.start()
        again.wait()
        beside.wait()
        done = lead
        for i in range(chunks):
            lax.fori_loop(done, done + 3, step, 0)
            done += 3

            @pl.when(below)
            def _():
                move(0, i, own, low, up).wait_recv()

                @pl.when(odd == 1)
                def _():
                    move(3, i, low, far, other).start()

            @pl.when(above)
            def _():
                move(1, i, own, high, down).wait_recv()

                @pl.when(odd == 0)
                def _():
                    move(3, i, high, far, other).start()

        lax.fori_loop(done, (EARLY + 1) // 2, step, 0)

        @pl.when(beyond)
        def _():
            for i in range(chunks):
                move(3, i, own, far, other).wait_recv()

        @pl.when(((odd == 0) & above) | ((odd == 1) & below))
        def _():
            for i in range(chunks):
                move(3, i, own, far, other).wait_send()

        @pl.when(above)
        def _():
            for i in range(chunks):
                move(0, i, own, low, up).wait_send()

        @pl.when(below)
        def _():
            for i in range(chunks):
                move(1, i, own, high, down).wait_send()

        for i in range(chunks):
            move(2, i, own, sib, other).wait_send()
        for c, there_in, there_out in zip(news, (below, beyond, above), (above, beyond, below), strict=True):
            pl.when(there_in)(c.wait_recv)
            pl.when(there_out)(c.wait_send)

    hbm = pl.BlockSpec(memory_space=pl.ANY)
    return pl.pallas_call(
        kernel,
        out_shape=[jax.ShapeDtypeStruct((clusters, 8, C), F32)] * 4
        + [jax.ShapeDtypeStruct((EARLY + 1, 2, 8, C), F32)]
        + [jax.ShapeDtypeStruct((NUMBERS,), jnp.int32)] * 3,
        in_specs=[hbm, pl.BlockSpec(memory_space=pltpu.SMEM), hbm],
        out_specs=[hbm] * 4 + [pl.BlockSpec(memory_space=pltpu.VMEM)] + [hbm] * 3,
        scratch_shapes=[pltpu.VMEM((clusters, 8, C), F32), pltpu.VMEM((2 * clusters, 8, C), F32)]
        + STAGE
        + STAGE
        + KEPT
        + [pltpu.SemaphoreType.DMA((4, chunks)), pltpu.SemaphoreType.DMA((4, chunks))]
        + [pltpu.SemaphoreType.DMA((3,))] * 3,
        compiler_params=pltpu.CompilerParams(
            collective_id=0, has_side_effects=True, vmem_limit_bytes=VMEM_LIMIT
        ),
    )(geometry, lists, lists)


def near_field(lists, news, geos, made):
    nwin = len(geos)
    clusters = geos[0].shape[0]

    def kernel(lists, lo, fa, hi, made, *refs):
        geo = refs[:nwin]
        acc, win, early = refs[nwin : nwin + 3]
        even = refs[nwin + 3 : nwin + 10]
        odd = refs[nwin + 10 : nwin + 17]
        ws, ks, work, sem = refs[nwin + 17 :]
        copies = [
            pltpu.make_async_copy(geo[k], win.at[pl.ds(k * clusters, clusters)], sem.at[k]) for k in range(nwin)
        ] + [pltpu.make_async_copy(made, early, sem.at[nwin])]
        for c in copies:
            c.start()

        def spare(ref):
            inside = jnp.maximum(ref[COUNTS] - INSIDE - LATE, 0)
            beside = jnp.maximum(ref[COUNTS + 1] - (EARLY - INSIDE), 0)
            return inside + beside + ref[COUNTS + 2] + ref[COUNTS + 3] + ref[COUNTS + 4]

        def enlist(n, ref, k, start, stop, first_at, second_at):
            def put(j, carry):
                v = ref[k * ROW + j]
                work[n + j - start] = first_at * clusters + v // clusters
                work[2 * ROW + n + j - start] = second_at * clusters + v % clusters
                return carry

            lax.fori_loop(start, stop, put, 0)
            return n + jnp.maximum(stop - start, 0)

        work[0] = 0
        work[2 * ROW] = 0
        mine = spare(lists)
        above, below, beyond = around(position())
        n = enlist(0, lists, 0, INSIDE + LATE, lists[COUNTS], REACH, REACH)
        n = enlist(n, lists, 1, EARLY - INSIDE, lists[COUNTS + 1], REACH, REACH + 1)
        for ref, k, theirs, at, there in ((lo, 2, 4, 0, below), (fa, 3, 3, 1, beyond), (hi, 4, 2, 4, above)):
            more = mine - spare(ref)
            given = jnp.clip(more // 4, 0, lists[COUNTS + k])
            taken = jnp.where(there == 1, jnp.clip((0 - more) // 4, 0, ref[COUNTS + theirs]), 0)
            n = enlist(n, lists, k, given, lists[COUNTS + k], REACH, at)
            n = enlist(n, ref, theirs, 0, taken, at, REACH)
        acc[...] = jnp.zeros_like(acc)
        for c in copies:
            c.wait()
        last = jnp.maximum(n - 1, 0)

        def load(h):
            q = jnp.minimum(h, last)
            return win[work[q]], win[work[2 * ROW + q]]

        def save(h, gf, gg):
            live = (h >= 0) & (h < n)
            q = jnp.clip(h, 0, last)
            fi = work[q]
            si = work[2 * ROW + q]
            acc[fi] += jnp.where(live, gf, 0.0)
            acc[si] += jnp.where(live, gg, 0.0)

        prep(*load(0), *even[:4])

        def add(k, at, slot):
            def one(j, carry):
                v = lists[k * ROW + j]
                acc[REACH * clusters + v // clusters] += early[at + j, 0]
                acc[slot * clusters + v % clusters] += early[at + j, 1]
                return carry

            return one

        lax.fori_loop(0, jnp.minimum(lists[COUNTS], INSIDE), add(0, 1, REACH), 0)
        lax.fori_loop(0, jnp.minimum(lists[COUNTS + 1], EARLY - INSIDE), add(1, 1 + INSIDE, REACH + 1), 0)

        def step(i, carry):
            stage(2 * i, even, odd, ws, ks, load, save)
            stage(2 * i + 1, odd, even, ws, ks, load, save)
            return carry

        lax.fori_loop(0, (n + 2) // 2, step, 0)

    hbm = pl.BlockSpec(memory_space=pl.ANY)
    return pl.pallas_call(
        kernel,
        out_shape=jax.ShapeDtypeStruct((nwin * clusters, 8, C), F32),
        in_specs=[pl.BlockSpec(memory_space=pltpu.SMEM)] * 4 + [hbm] * (nwin + 1),
        out_specs=pl.BlockSpec(memory_space=pltpu.VMEM),
        scratch_shapes=[pltpu.VMEM((nwin * clusters, 8, C), F32)]
        + [pltpu.VMEM((EARLY + 1, 2, 8, C), F32)]
        + STAGE
        + STAGE
        + KEPT
        + [pltpu.SMEM((4 * ROW,), jnp.int32), pltpu.SemaphoreType.DMA((nwin + 1,))],
        compiler_params=pltpu.CompilerParams(vmem_limit_bytes=VMEM_LIMIT),
    )(lists, *news, made, *geos)


def give_back(sums, geometry, lists):
    clusters = geometry.shape[0]

    def kernel(sums, own, lists, *refs):
        boxes = refs[:4]
        made, seen = refs[4:6]
        even, odds = refs[6:13], refs[13:20]
        ws, ks, send, recv, fetch = refs[20:]
        me = position()
        odd = me % 2
        targets = (place(me - 2), place(me - 1 + 2 * odd), place(me + 1 - 2 * odd), place(me + 2))
        mine = pltpu.make_async_copy(own, seen, fetch.at[0])
        mine.start()
        there = around(me)
        greet(targets[2], (targets[3], targets[0], targets[1]), there)
        above, below, beyond = (yes == 1 for yes in there)
        copies = [
            pltpu.make_async_remote_copy(
                src_ref=sums.at[pl.ds(slot * clusters, clusters), pl.ds(0, 3)],
                dst_ref=boxes[k].at[:, pl.ds(0, 3)],
                send_sem=send.at[k],
                recv_sem=recv.at[k],
                device_id=device,
                device_id_type=MESH,
            )
            for k, (slot, device) in enumerate(zip((0, 1, 3, 4), targets, strict=True))
        ]
        pl.when(below)(copies[0].start)
        pl.when(above)(copies[3].start)
        pl.when(beyond)(copies[1].start)
        copies[2].start()
        mine.wait()

        def load(h):
            v = lists[INSIDE + jnp.minimum(h, LATE)]
            return seen[v // clusters], seen[v % clusters]

        def save(h, gf, gg):
            made[h + 1, 0] = gf
            made[h + 1, 1] = gg

        prep(*load(0), *even[:4])

        def step(i, carry):
            stage(2 * i, even, odds, ws, ks, load, save)
            stage(2 * i + 1, odds, even, ws, ks, load, save)
            return carry

        lax.fori_loop(0, (LATE + 1) // 2, step, 0)
        pl.when(below)(copies[0].wait_send)
        pl.when(above)(copies[0].wait_recv)
        pl.when(above)(copies[3].wait_send)
        pl.when(below)(copies[3].wait_recv)
        pl.when(beyond)(copies[1].wait)
        copies[2].wait()

    hbm = pl.BlockSpec(memory_space=pl.ANY)
    return pl.pallas_call(
        kernel,
        out_shape=[jax.ShapeDtypeStruct((clusters, 8, C), F32)] * 4
        + [jax.ShapeDtypeStruct((LATE + 1, 2, 8, C), F32)],
        in_specs=[hbm] * 2 + [pl.BlockSpec(memory_space=pltpu.SMEM)],
        out_specs=[hbm] * 4 + [pl.BlockSpec(memory_space=pltpu.VMEM)],
        scratch_shapes=[pltpu.VMEM((clusters, 8, C), F32)]
        + STAGE
        + STAGE
        + KEPT
        + [pltpu.SemaphoreType.DMA((4,)), pltpu.SemaphoreType.DMA((4,)), pltpu.SemaphoreType.DMA((1,))],
        compiler_params=pltpu.CompilerParams(
            collective_id=1, has_side_effects=True, vmem_limit_bytes=VMEM_LIMIT
        ),
    )(sums, geometry, lists)


def finish(sums, boxes, made, lists):
    clusters = boxes[0].shape[0]

    def kernel(lists, sums, b0, b1, b2, b3, made, out, held, sem):
        lay = pl.ds(0, 3)
        above, below, beyond = around(position())
        sources = [sums.at[pl.ds(REACH * clusters, clusters), lay]] + [b.at[:, lay] for b in (b0, b1, b2, b3)]
        copies = [
            pltpu.make_async_copy(src, held.at[pl.ds(k * clusters, clusters), lay], sem.at[k])
            for k, src in enumerate(sources)
        ]
        for c in copies:
            c.start()
        for c in copies:
            c.wait()

        def add(j, carry):
            v = lists[INSIDE + j]
            held[v // clusters] += made[j + 1, 0]
            held[v % clusters] += made[j + 1, 1]
            return carry

        lax.fori_loop(0, jnp.clip(lists[COUNTS] - INSIDE, 0, LATE), add, 0)
        for c in range(clusters):
            a, p0, p1, p2, p3 = (held[k * clusters + c] for k in range(5))
            p0, p1, p3 = (jnp.where(yes == 1, p, 0.0) for p, yes in ((p0, above), (p1, beyond), (p3, below)))
            out[:, c * C : (c + 1) * C] = (a + ((p0 + p3) + (p1 + p2)))[0:3]

    hbm = pl.BlockSpec(memory_space=pl.ANY)
    return pl.pallas_call(
        kernel,
        out_shape=jax.ShapeDtypeStruct((3, clusters * C), F32),
        in_specs=[pl.BlockSpec(memory_space=pltpu.SMEM)] + [hbm] * 5 + [pl.BlockSpec(memory_space=pltpu.VMEM)],
        out_specs=pl.BlockSpec(memory_space=pltpu.VMEM),
        scratch_shapes=[pltpu.VMEM((5 * clusters, 8, C), F32), pltpu.SemaphoreType.DMA((5,))],
        compiler_params=pltpu.CompilerParams(vmem_limit_bytes=VMEM_LIMIT),
    )(lists, sums, *boxes, made)


def body(positions, normals, areas, pair_first, pair_second, pair_count):
    geometry, lists = sort_out(positions, normals, areas, pair_first, pair_second, pair_count)
    low, far, sib, high, early, *news = gather(geometry, lists)
    sums = near_field(lists, news, [low, far, geometry, sib, high], early)
    *boxes, late = give_back(sums, geometry, lists)
    return finish(sums, boxes, late, lists)


def solution(mesh):
    flat = P(("gx", "gy"))
    deep = P(None, ("gx", "gy"))
    return jax.shard_map(
        body, mesh=mesh, in_specs=(deep, deep, flat, flat, flat, flat), out_specs=deep, check_vma=False
    )
```

```python
import functools

import jax
import jax.numpy as jnp
from jax import lax
from jax.experimental import pallas as pl
from jax.experimental.pallas import tpu as pltpu
from jax.sharding import PartitionSpec as P

C = 256
REACH = 2
F32 = jnp.float32
BF = jnp.bfloat16
MESH = pl.DeviceIdType.MESH
VMEM_LIMIT = 60 * 2**20
INSIDE = 9
EARLY = 35
LATE = 19
ROW = 128
COUNTS = 6 * ROW
NUMBERS = 8 * ROW


def split3(t):
    a = t.astype(BF).astype(F32)
    r = t - a
    b = r.astype(BF).astype(F32)
    return a, b, r - b


def split2(t):
    a = t.astype(BF).astype(F32)
    return a, t - a


def wide(v):
    return jnp.broadcast_to(v, (8, C))


def row_index():
    return lax.broadcasted_iota(jnp.int32, (8, C), 0)


def prep(f, g, lhs_ref, rhs_ref, w_ref, keep_ref):
    row = row_index()
    isp = row < 3

    def at(k, v):
        return jnp.where(row == k, v, 0.0)

    af = wide(f[6:7, :])
    ag = wide(g[6:7, :])
    ctr = jnp.where(isp, wide(jnp.sum(f, axis=1, keepdims=True) * (1.0 / C)), 0.0)

    def parts(t):
        p = jnp.where(isp, t - ctr, 0.0)
        n = jnp.where(isp, pltpu.roll(t, 5, 0), 0.0)
        return p, n, wide(jnp.sum(p * p, axis=0, keepdims=True)), wide(jnp.sum(p * n, axis=0, keepdims=True))

    pf, nf, sf, cf = parts(f)
    pg, ng, sg, cg = parts(g)
    iaf = 1.0 / af
    iag = 1.0 / ag

    def left(t):
        u0, u1, u2 = split3(t)
        return jnp.concatenate([u0, u0, u0, u1, u1, u2], axis=0).T.astype(BF)

    def right(t):
        u0, u1, u2 = split3(t)
        return jnp.concatenate([u0, u1, u2, u0, u1, u0], axis=0).astype(BF)

    lhs_ref[0] = left(pf + at(3, sf + 1.0) + at(4, 1.0))
    lhs_ref[1] = left(af * (nf + at(3, cf) + pltpu.roll(pf, 4, 0) + at(7, 1.0)))
    rhs_ref[0] = right(-2.0 * pg + at(3, 1.0) + at(4, sg))
    rhs_ref[1] = right(ag * (at(3, 1.0) - pg))
    rhs_ref[2] = right(ag * (pltpu.roll(ng, 4, 0) - at(7, cg)))
    sums = (2.0 * nf, iaf * (at(6, 6.0) - 6.0 * pltpu.roll(pf, 3, 0)), iag * (6.0 * pg - at(3, 6.0)))
    for j, v in enumerate(sums):
        w_ref[j] = jnp.concatenate(split2(v), axis=0).astype(BF)
    for i, v in enumerate((nf, pf, iaf, ng, pg, iag)):
        keep_ref[i] = v


def terms(base, rows, sub, n, cs, lhs_ref, rhs_ref, l_ref, x_ref):
    def half(v):
        return v[:, :128] + v[:, 128:]

    big = slice(base, base + rows)
    left = lhs_ref[1, big, :]
    all_r2 = jnp.dot(lhs_ref[0, big, :], rhs_ref[0], preferred_element_type=F32)
    all_sf = jnp.dot(left, rhs_ref[1], preferred_element_type=F32)
    all_sg = jnp.dot(left, rhs_ref[2], preferred_element_type=F32)
    for s in range(0, rows, sub):
        sl = slice(base + s, base + s + sub)
        q = slice(s, s + sub)
        inv = 1.0 / all_r2[q]
        sf = all_sf[q]
        sg = all_sg[q]
        inv3 = inv * inv * inv
        lf = inv3 * sf
        lg = inv3 * sg
        rad = inv * (lf * sf + lg * sg)
        for j, v in ((0, lf), (2, rad)):
            h = v.astype(BF)
            l_ref[j, sl, :] = h
            l_ref[j + 1, sl, :] = (v - h.astype(F32)).astype(BF)
        for t in range(0, sub, 8):
            o = slice(t, t + 8)
            so = slice(base + s + t, base + s + t + 8)
            cs = cs + lg[o]
            x_ref[3, so, :] = half(lf[o])
            for k in range(3):
                x_ref[k, so, :] = half(lg[o] * n[k])
    return cs


def along(w, tile):
    return lax.dot_general(w, tile, (((1,), (0,)), ((), ())), preferred_element_type=F32)


def across(w, tile):
    return lax.dot_general(w, tile, (((1,), (1,)), ((), ())), preferred_element_type=F32)


def stage(h, now, before, ws, ks, load, save, rows=128, sub=16):
    lhs, rhs, w, keep, tiles, x, csr = now
    w_b, keep_b, tiles_b, x_b, csr_b = before[2:]
    ws[...] = w_b[...]
    ks[...] = keep_b[...]
    normal = [wide(keep[3, k : k + 1, :]) for k in range(3)]
    cs = jnp.zeros((8, C), F32)
    xs = [[None, None] for _ in range(4)]
    col = []
    rsum = []
    count = C // rows
    for c in range(count):
        cs = terms(c * rows, rows, sub, normal, cs, lhs, rhs, tiles, x)
        for e in range(c * 8 // count, (c + 1) * 8 // count):
            k, s = e // 2, e % 2
            xs[k][s] = jnp.sum(x_b[k, s * 128 : (s + 1) * 128, :].T, axis=0, keepdims=True)
            if e < 4:
                col.append(along(ws[e // 2], tiles_b[e]))
            elif e < 6:
                rsum.append(across(ws[2], tiles_b[e - 2]))
        if c == count // 2 - 1:
            prep(*load(h + 1), *before[:4])
    csr_old = csr_b[...]
    csr[...] = cs
    row = row_index()
    ct = (col[0] + col[1]) + (col[2] + col[3])
    rt = rsum[0] + rsum[1]
    ct = ct[0:8] + ct[8:16]
    rt = rt[0:8] + rt[8:16]
    nf, pf, iaf, ng, pg, iag = (ks[i] for i in range(6))
    xv = [wide(jnp.concatenate(v, axis=1)) for v in xs]
    lean = jnp.where(row == 0, xv[0], jnp.where(row == 1, xv[1], xv[2]))
    gf = 2.0 * (nf * xv[3] + lean) + iaf * (rt + pf * wide(rt[3:4]))
    csum = wide(jnp.sum(csr_old, axis=0, keepdims=True))
    gg = -(ct + ng * (2.0 * csum) + iag * (pltpu.roll(ct, 5, 0) + pg * wide(ct[6:7])))
    save(h - 1, gf, gg)


STAGE = [
    pltpu.VMEM((2, C, 48), BF),
    pltpu.VMEM((3, 48, C), BF),
    pltpu.VMEM((3, 16, C), BF),
    pltpu.VMEM((6, 8, C), F32),
    pltpu.VMEM((4, C, C), BF),
    pltpu.VMEM((4, C, 128), F32),
    pltpu.VMEM((8, C), F32),
]
KEPT = [pltpu.VMEM((3, 16, C), BF), pltpu.VMEM((6, 8, C), F32)]


def lanes(c):
    return pl.ds(pl.multiple_of(c * C, C), C)


def place(flat):
    inner = lax.axis_size("gy")
    total = lax.axis_size("gx") * inner
    flat = (flat + total) % total
    return (flat // inner, flat % inner)


def position():
    return lax.axis_index("gx") * lax.axis_size("gy") + lax.axis_index("gy")


def around(me):
    total = lax.axis_size("gx") * lax.axis_size("gy")
    odd = me % 2
    above = (2 * total - 3 - me) // total
    below = (me + total - 2) // total
    return above, below, odd * above + (1 - odd) * below


def greet(always, maybe, there):
    barrier = pltpu.get_barrier_semaphore()

    def tell(device):
        pl.semaphore_signal(barrier, inc=1, device_id=device, device_id_type=MESH)

    tell(always)
    for device, yes in zip(maybe, there, strict=True):
        pl.when(yes == 1)(functools.partial(tell, device))
    pl.semaphore_wait(barrier, 1 + there[0] + there[1] + there[2])


def sort_out(positions, normals, areas, pair_first, pair_second, pair_count):
    faces = positions.shape[1]
    clusters = faces // C

    def kernel(pos, nor, area, pf, ps, count, geometry, lists):
        for c in range(clusters):
            sl = slice(c * C, (c + 1) * C)
            geometry[c, 0:3, :] = pos[:, sl]
            geometry[c, 3:6, :] = nor[:, sl]
            geometry[c, 6:7, :] = area[:, sl]
            geometry[c, 7:8, :] = jnp.zeros((1, C), F32)
        me = position()
        odd = me % 2

        def clear(i, carry):
            lists[i] = 0
            lists[ROW + i] = 0
            return carry

        lax.fori_loop(0, INSIDE + LATE + 2, clear, 0)
        for k in range(6):
            lists[COUNTS + k] = 0
        live = count[0]

        def one(j):
            s = ps[j]
            h = s // clusters - me
            outer = jnp.where(h == 2, 4, 2)
            inner = jnp.where(h == 1 - 2 * odd, 1, 3)
            k = jnp.where(h == 0, 0, jnp.where(jnp.abs(h) == 2, outer, inner))
            k = jnp.where(j < live, k, 5)
            n = lists[COUNTS + k]
            lists[k * ROW + n] = (pf[j] - me * clusters) * clusters + s % clusters
            lists[COUNTS + k] = n + 1

        def step(i, carry):
            for u in range(4):
                one(4 * i + u)
            return carry

        lax.fori_loop(0, (live + 3) // 4, step, 0)

    vmem = pl.BlockSpec(memory_space=pltpu.VMEM)
    smem = pl.BlockSpec(memory_space=pltpu.SMEM)
    return pl.pallas_call(
        kernel,
        out_shape=[jax.ShapeDtypeStruct((clusters, 8, C), F32), jax.ShapeDtypeStruct((NUMBERS,), jnp.int32)],
        in_specs=[vmem] * 3 + [smem] * 3,
        out_specs=[vmem, smem],
        compiler_params=pltpu.CompilerParams(vmem_limit_bytes=VMEM_LIMIT),
    )(positions, normals, areas.reshape(1, faces), pair_first, pair_second, pair_count)


def gather(geometry, lists, rows=7, chunks=4):
    clusters = geometry.shape[0]
    part = clusters // chunks

    def kernel(own, lists, told, low, far, sib, high, made, lo, fa, hi, second, near, seen, *refs):
        even, odds = refs[:7], refs[7:14]
        ws, ks, send, recv, fetch, news_send, news_recv, hop_send, hop_recv = refs[14:]
        me = position()
        odd = me % 2
        up, down, other = place(me + 2), place(me - 2), place(me + 1 - 2 * odd)
        away = place(me - 1 + 2 * odd)
        mine = pltpu.make_async_copy(own, near, fetch.at[0])
        mine.start()
        again = pltpu.make_async_copy(own, seen.at[pl.ds(0, clusters)], fetch.at[2])
        again.start()
        there = around(me)
        greet(other, (up, down, away), there)
        above, below, beyond = (yes == 1 for yes in there)

        def move(kind, i, src, dst, device):
            sl = (pl.ds(i * part, part), pl.ds(0, rows))
            return pltpu.make_async_remote_copy(
                src_ref=src.at[sl],
                dst_ref=dst.at[sl],
                send_sem=send.at[kind, i],
                recv_sem=recv.at[kind, i],
                device_id=device,
                device_id_type=MESH,
            )

        news = [
            pltpu.make_async_remote_copy(
                src_ref=told,
                dst_ref=dst,
                send_sem=news_send.at[k],
                recv_sem=news_recv.at[k],
                device_id=device,
                device_id_type=MESH,
            )
            for k, (dst, device) in enumerate(((lo, up), (fa, away), (hi, down)))
        ]
        for c, yes in zip(news, (above, beyond, below), strict=True):
            pl.when(yes)(c.start)
        for i in range(chunks):
            move(2, i, own, sib, other).start()

        @pl.when(above)
        def _():
            for i in range(chunks):
                move(0, i, own, low, up).start()

        @pl.when(below)
        def _():
            for i in range(chunks):
                move(1, i, own, high, down).start()

        mine.wait()

        def load(h):
            v = lists[ROW + jnp.minimum(h, EARLY) - INSIDE]
            return seen[v // clusters], seen[clusters + v % clusters]

        def save(h, gf, gg):
            made[h + 1, 0] = gf
            made[h + 1, 1] = gg

        def step(i, carry):
            stage(2 * i, even, odds, ws, ks, load, save)
            stage(2 * i + 1, odds, even, ws, ks, load, save)
            return carry

        def fresh(h):
            v = lists[h]
            return near[v // clusters], near[v % clusters]

        def inner(i, carry):
            stage(2 * i, even, odds, ws, ks, fresh, save)
            stage(2 * i + 1, odds, even, ws, ks, fresh, save)
            return carry

        prep(*fresh(0), *even[:4])
        lead = (INSIDE - 1) // 2
        lax.fori_loop(0, lead, inner, 0)
        pl.when(below)(news[0].wait_recv)
        pl.when(beyond)(news[1].wait_recv)
        pl.when(above)(news[2].wait_recv)
        tail = NUMBERS - COUNTS
        hops = [
            pltpu.make_async_remote_copy(
                src_ref=src.at[pl.ds(COUNTS, tail)],
                dst_ref=second.at[pl.ds(k * tail, tail)],
                send_sem=hop_send.at[k],
                recv_sem=hop_recv.at[k],
                device_id=device,
                device_id_type=MESH,
            )
            for k, (src, device) in enumerate(((lo, up), (fa, up), (lo, away), (hi, away), (fa, down), (hi, down)))
        ]
        going = (above, above, beyond, beyond, below, below)
        coming = (below, below, beyond, beyond, above, above)
        for c, yes in zip(hops, going, strict=True):
            pl.when(yes)(c.start)
        for i in range(chunks):
            move(2, i, own, sib, other).wait_recv()
        beside = pltpu.make_async_copy(sib, seen.at[pl.ds(clusters, clusters)], fetch.at[1])
        beside.start()
        again.wait()
        beside.wait()
        done = lead
        for i in range(chunks):
            lax.fori_loop(done, done + 3, step, 0)
            done += 3

            @pl.when(below)
            def _():
                move(0, i, own, low, up).wait_recv()

                @pl.when(odd == 1)
                def _():
                    move(3, i, low, far, other).start()

            @pl.when(above)
            def _():
                move(1, i, own, high, down).wait_recv()

                @pl.when(odd == 0)
                def _():
                    move(3, i, high, far, other).start()

        lax.fori_loop(done, (EARLY + 1) // 2, step, 0)

        @pl.when(beyond)
        def _():
            for i in range(chunks):
                move(3, i, own, far, other).wait_recv()

        @pl.when(((odd == 0) & above) | ((odd == 1) & below))
        def _():
            for i in range(chunks):
                move(3, i, own, far, other).wait_send()

        @pl.when(above)
        def _():
            for i in range(chunks):
                move(0, i, own, low, up).wait_send()

        @pl.when(below)
        def _():
            for i in range(chunks):
                move(1, i, own, high, down).wait_send()

        for i in range(chunks):
            move(2, i, own, sib, other).wait_send()
        for c, there_out in zip(news, (above, beyond, below), strict=True):
            pl.when(there_out)(c.wait_send)
        for c, there_in, there_out in zip(hops, coming, going, strict=True):
            pl.when(there_in)(c.wait_recv)
            pl.when(there_out)(c.wait_send)

    hbm = pl.BlockSpec(memory_space=pl.ANY)
    return pl.pallas_call(
        kernel,
        out_shape=[jax.ShapeDtypeStruct((clusters, 8, C), F32)] * 4
        + [jax.ShapeDtypeStruct((EARLY + 1, 2, 8, C), F32)]
        + [jax.ShapeDtypeStruct((NUMBERS,), jnp.int32)] * 3
        + [jax.ShapeDtypeStruct((6 * (NUMBERS - COUNTS),), jnp.int32)],
        in_specs=[hbm, pl.BlockSpec(memory_space=pltpu.SMEM), hbm],
        out_specs=[hbm] * 4 + [pl.BlockSpec(memory_space=pltpu.VMEM)] + [hbm] * 4,
        scratch_shapes=[pltpu.VMEM((clusters, 8, C), F32), pltpu.VMEM((2 * clusters, 8, C), F32)]
        + STAGE
        + STAGE
        + KEPT
        + [pltpu.SemaphoreType.DMA((4, chunks)), pltpu.SemaphoreType.DMA((4, chunks))]
        + [pltpu.SemaphoreType.DMA((3,))] * 3
        + [pltpu.SemaphoreType.DMA((6,))] * 2,
        compiler_params=pltpu.CompilerParams(
            collective_id=0, has_side_effects=True, vmem_limit_bytes=VMEM_LIMIT
        ),
    )(geometry, lists, lists)


def near_field(lists, news, geos, made):
    nwin = len(geos)
    clusters = geos[0].shape[0]

    def kernel(lists, lo, fa, hi, second, made, *refs):
        geo = refs[:nwin]
        acc, win, early = refs[nwin : nwin + 3]
        even = refs[nwin + 3 : nwin + 10]
        odd = refs[nwin + 10 : nwin + 17]
        ws, ks, work, sem = refs[nwin + 17 :]
        copies = [
            pltpu.make_async_copy(geo[k], win.at[pl.ds(k * clusters, clusters)], sem.at[k]) for k in range(nwin)
        ] + [pltpu.make_async_copy(made, early, sem.at[nwin])]
        for c in copies:
            c.start()

        def spare(ref, at=COUNTS):
            inside = jnp.maximum(ref[at] - INSIDE - LATE, 0)
            beside = jnp.maximum(ref[at + 1] - (EARLY - INSIDE), 0)
            return inside + beside + ref[at + 2] + ref[at + 3] + ref[at + 4]

        def quarter(v):
            return jnp.where(v >= 0, v // 4, 0 - (0 - v) // 4)

        def enlist(n, ref, k, start, stop, first_at, second_at):
            def put(j, carry):
                v = ref[k * ROW + j]
                work[n + j - start] = first_at * clusters + v // clusters
                work[2 * ROW + n + j - start] = second_at * clusters + v % clusters
                return carry

            lax.fori_loop(start, stop, put, 0)
            return n + jnp.maximum(stop - start, 0)

        work[0] = 0
        work[2 * ROW] = 0
        mine = spare(lists)
        n = enlist(0, lists, 0, INSIDE + LATE, lists[COUNTS], REACH, REACH)
        n = enlist(n, lists, 1, EARLY - INSIDE, lists[COUNTS + 1], REACH, REACH + 1)
        me = position()
        parity = me % 2
        total = lax.axis_size("gx") * lax.axis_size("gy")

        def there(d):
            return (d >= 0) & (d < total)

        def after(own, others):
            change = 0
            for d, r in others:
                change = change + jnp.where(there(d), quarter(own - r), 0)
            return own - change

        def hop(k):
            return spare(second, k * (NUMBERS - COUNTS))

        d_lo, d_fa, d_hi = me - 2, me - 1 + 2 * parity, me + 2
        r_lo, r_fa, r_hi = spare(lo), spare(fa), spare(hi)
        mine_after = after(mine, ((d_lo, r_lo), (d_fa, r_fa), (d_hi, r_hi)))
        lo_after = after(r_lo, ((me, mine), (d_lo - 2, hop(0)), (d_lo - 1 + 2 * parity, hop(1))))
        fa_after = after(r_fa, ((me, mine), (d_fa - 2, hop(2)), (d_fa + 2, hop(3))))
        hi_after = after(r_hi, ((me, mine), (d_hi - 1 + 2 * parity, hop(4)), (d_hi + 2, hop(5))))
        for ref, k, theirs, at, d, r, later in (
            (lo, 2, 4, 0, d_lo, r_lo, lo_after),
            (fa, 3, 3, 1, d_fa, r_fa, fa_after),
            (hi, 4, 2, 4, d_hi, r_hi, hi_after),
        ):
            more = quarter(mine - r) + quarter(mine_after - later)
            given = jnp.clip(more, 0, lists[COUNTS + k])
            taken = jnp.where(there(d), jnp.clip(0 - more, 0, ref[COUNTS + theirs]), 0)
            n = enlist(n, lists, k, given, lists[COUNTS + k], REACH, at)
            n = enlist(n, ref, theirs, 0, taken, at, REACH)
        acc[...] = jnp.zeros_like(acc)
        for c in copies:
            c.wait()
        last = jnp.maximum(n - 1, 0)

        def load(h):
            q = jnp.minimum(h, last)
            return win[work[q]], win[work[2 * ROW + q]]

        def save(h, gf, gg):
            live = (h >= 0) & (h < n)
            q = jnp.clip(h, 0, last)
            fi = work[q]
            si = work[2 * ROW + q]
            acc[fi] += jnp.where(live, gf, 0.0)
            acc[si] += jnp.where(live, gg, 0.0)

        prep(*load(0), *even[:4])

        def add(k, at, slot):
            def one(j, carry):
                v = lists[k * ROW + j]
                acc[REACH * clusters + v // clusters] += early[at + j, 0]
                acc[slot * clusters + v % clusters] += early[at + j, 1]
                return carry

            return one

        lax.fori_loop(0, jnp.minimum(lists[COUNTS], INSIDE), add(0, 1, REACH), 0)
        lax.fori_loop(0, jnp.minimum(lists[COUNTS + 1], EARLY - INSIDE), add(1, 1 + INSIDE, REACH + 1), 0)

        def step(i, carry):
            stage(2 * i, even, odd, ws, ks, load, save)
            stage(2 * i + 1, odd, even, ws, ks, load, save)
            return carry

        lax.fori_loop(0, (n + 2) // 2, step, 0)

    hbm = pl.BlockSpec(memory_space=pl.ANY)
    return pl.pallas_call(
        kernel,
        out_shape=jax.ShapeDtypeStruct((nwin * clusters, 8, C), F32),
        in_specs=[pl.BlockSpec(memory_space=pltpu.SMEM)] * 5 + [hbm] * (nwin + 1),
        out_specs=pl.BlockSpec(memory_space=pltpu.VMEM),
        scratch_shapes=[pltpu.VMEM((nwin * clusters, 8, C), F32)]
        + [pltpu.VMEM((EARLY + 1, 2, 8, C), F32)]
        + STAGE
        + STAGE
        + KEPT
        + [pltpu.SMEM((4 * ROW,), jnp.int32), pltpu.SemaphoreType.DMA((nwin + 1,))],
        compiler_params=pltpu.CompilerParams(vmem_limit_bytes=VMEM_LIMIT),
    )(lists, *news, made, *geos)


def give_back(sums, geometry, lists):
    clusters = geometry.shape[0]

    def kernel(sums, own, lists, *refs):
        boxes = refs[:4]
        made, seen = refs[4:6]
        even, odds = refs[6:13], refs[13:20]
        ws, ks, send, recv, fetch = refs[20:]
        me = position()
        odd = me % 2
        targets = (place(me - 2), place(me - 1 + 2 * odd), place(me + 1 - 2 * odd), place(me + 2))
        mine = pltpu.make_async_copy(own, seen, fetch.at[0])
        mine.start()
        there = around(me)
        greet(targets[2], (targets[3], targets[0], targets[1]), there)
        above, below, beyond = (yes == 1 for yes in there)
        copies = [
            pltpu.make_async_remote_copy(
                src_ref=sums.at[pl.ds(slot * clusters, clusters), pl.ds(0, 3)],
                dst_ref=boxes[k].at[:, pl.ds(0, 3)],
                send_sem=send.at[k],
                recv_sem=recv.at[k],
                device_id=device,
                device_id_type=MESH,
            )
            for k, (slot, device) in enumerate(zip((0, 1, 3, 4), targets, strict=True))
        ]
        pl.when(below)(copies[0].start)
        pl.when(above)(copies[3].start)
        pl.when(beyond)(copies[1].start)
        copies[2].start()
        mine.wait()

        def load(h):
            v = lists[INSIDE + jnp.minimum(h, LATE)]
            return seen[v // clusters], seen[v % clusters]

        def save(h, gf, gg):
            made[h + 1, 0] = gf
            made[h + 1, 1] = gg

        prep(*load(0), *even[:4])

        def step(i, carry):
            stage(2 * i, even, odds, ws, ks, load, save)
            stage(2 * i + 1, odds, even, ws, ks, load, save)
            return carry

        lax.fori_loop(0, (LATE + 1) // 2, step, 0)
        pl.when(below)(copies[0].wait_send)
        pl.when(above)(copies[0].wait_recv)
        pl.when(above)(copies[3].wait_send)
        pl.when(below)(copies[3].wait_recv)
        pl.when(beyond)(copies[1].wait)
        copies[2].wait()

    hbm = pl.BlockSpec(memory_space=pl.ANY)
    return pl.pallas_call(
        kernel,
        out_shape=[jax.ShapeDtypeStruct((clusters, 8, C), F32)] * 4
        + [jax.ShapeDtypeStruct((LATE + 1, 2, 8, C), F32)],
        in_specs=[hbm] * 2 + [pl.BlockSpec(memory_space=pltpu.SMEM)],
        out_specs=[hbm] * 4 + [pl.BlockSpec(memory_space=pltpu.VMEM)],
        scratch_shapes=[pltpu.VMEM((clusters, 8, C), F32)]
        + STAGE
        + STAGE
        + KEPT
        + [pltpu.SemaphoreType.DMA((4,)), pltpu.SemaphoreType.DMA((4,)), pltpu.SemaphoreType.DMA((1,))],
        compiler_params=pltpu.CompilerParams(
            collective_id=1, has_side_effects=True, vmem_limit_bytes=VMEM_LIMIT
        ),
    )(sums, geometry, lists)


def finish(sums, boxes, made, lists):
    clusters = boxes[0].shape[0]

    def kernel(lists, sums, b0, b1, b2, b3, made, out, held, sem):
        lay = pl.ds(0, 3)
        above, below, beyond = around(position())
        sources = [sums.at[pl.ds(REACH * clusters, clusters), lay]] + [b.at[:, lay] for b in (b0, b1, b2, b3)]
        copies = [
            pltpu.make_async_copy(src, held.at[pl.ds(k * clusters, clusters), lay], sem.at[k])
            for k, src in enumerate(sources)
        ]
        for c in copies:
            c.start()
        for c in copies:
            c.wait()

        def add(j, carry):
            v = lists[INSIDE + j]
            held[v // clusters] += made[j + 1, 0]
            held[v % clusters] += made[j + 1, 1]
            return carry

        lax.fori_loop(0, jnp.clip(lists[COUNTS] - INSIDE, 0, LATE), add, 0)
        for c in range(clusters):
            a, p0, p1, p2, p3 = (held[k * clusters + c] for k in range(5))
            p0, p1, p3 = (jnp.where(yes == 1, p, 0.0) for p, yes in ((p0, above), (p1, beyond), (p3, below)))
            out[:, c * C : (c + 1) * C] = (a + ((p0 + p3) + (p1 + p2)))[0:3]

    hbm = pl.BlockSpec(memory_space=pl.ANY)
    return pl.pallas_call(
        kernel,
        out_shape=jax.ShapeDtypeStruct((3, clusters * C), F32),
        in_specs=[pl.BlockSpec(memory_space=pltpu.SMEM)] + [hbm] * 5 + [pl.BlockSpec(memory_space=pltpu.VMEM)],
        out_specs=pl.BlockSpec(memory_space=pltpu.VMEM),
        scratch_shapes=[pltpu.VMEM((5 * clusters, 8, C), F32), pltpu.SemaphoreType.DMA((5,))],
        compiler_params=pltpu.CompilerParams(vmem_limit_bytes=VMEM_LIMIT),
    )(lists, sums, *boxes, made)


def body(positions, normals, areas, pair_first, pair_second, pair_count):
    geometry, lists = sort_out(positions, normals, areas, pair_first, pair_second, pair_count)
    low, far, sib, high, early, *news = gather(geometry, lists)
    sums = near_field(lists, news, [low, far, geometry, sib, high], early)
    *boxes, late = give_back(sums, geometry, lists)
    return finish(sums, boxes, late, lists)


def solution(mesh):
    flat = P(("gx", "gy"))
    deep = P(None, ("gx", "gy"))
    return jax.shard_map(
        body, mesh=mesh, in_specs=(deep, deep, flat, flat, flat, flat), out_specs=deep, check_vma=False
    )
```

```python
import functools

import jax
import jax.numpy as jnp
from jax import lax
from jax.experimental import pallas as pl
from jax.experimental.pallas import tpu as pltpu
from jax.sharding import PartitionSpec as P

C = 256
REACH = 2
F32 = jnp.float32
BF = jnp.bfloat16
MESH = pl.DeviceIdType.MESH
VMEM_LIMIT = 60 * 2**20
INSIDE = 9
EARLY = 35
LATE = 19
ROW = 128
COUNTS = 6 * ROW
NUMBERS = 8 * ROW


def split3(t):
    a = t.astype(BF).astype(F32)
    r = t - a
    b = r.astype(BF).astype(F32)
    return a, b, r - b


def split2(t):
    a = t.astype(BF).astype(F32)
    return a, t - a


def wide(v):
    return jnp.broadcast_to(v, (8, C))


def row_index():
    return lax.broadcasted_iota(jnp.int32, (8, C), 0)


def prep(f, g, lhs_ref, rhs_ref, w_ref, keep_ref):
    row = row_index()
    isp = row < 3

    def at(k, v):
        return jnp.where(row == k, v, 0.0)

    af = wide(f[6:7, :])
    ag = wide(g[6:7, :])
    ctr = jnp.where(isp, wide(jnp.sum(f, axis=1, keepdims=True) * (1.0 / C)), 0.0)

    def parts(t):
        p = jnp.where(isp, t - ctr, 0.0)
        n = jnp.where(isp, pltpu.roll(t, 5, 0), 0.0)
        return p, n, wide(jnp.sum(p * p, axis=0, keepdims=True)), wide(jnp.sum(p * n, axis=0, keepdims=True))

    pf, nf, sf, cf = parts(f)
    pg, ng, sg, cg = parts(g)
    iaf = 1.0 / af
    iag = 1.0 / ag

    def left(t):
        u0, u1, u2 = split3(t)
        return jnp.concatenate([u0, u0, u0, u1, u1, u2], axis=0).T.astype(BF)

    def right(t):
        u0, u1, u2 = split3(t)
        return jnp.concatenate([u0, u1, u2, u0, u1, u0], axis=0).astype(BF)

    lhs_ref[0] = left(pf + at(3, sf + 1.0) + at(4, 1.0))
    lhs_ref[1] = left(af * (nf + at(3, cf) + pltpu.roll(pf, 4, 0) + at(7, 1.0)))
    rhs_ref[0] = right(-2.0 * pg + at(3, 1.0) + at(4, sg))
    rhs_ref[1] = right(ag * (at(3, 1.0) - pg))
    rhs_ref[2] = right(ag * (pltpu.roll(ng, 4, 0) - at(7, cg)))
    sums = (2.0 * nf, iaf * (at(6, 6.0) - 6.0 * pltpu.roll(pf, 3, 0)), iag * (6.0 * pg - at(3, 6.0)))
    for j, v in enumerate(sums):
        w_ref[j] = jnp.concatenate(split2(v), axis=0).astype(BF)
    for i, v in enumerate((nf, pf, iaf, ng, pg, iag)):
        keep_ref[i] = v


def terms(base, rows, sub, n, cs, lhs_ref, rhs_ref, l_ref, x_ref):
    def half(v):
        return v[:, :128] + v[:, 128:]

    big = slice(base, base + rows)
    left = lhs_ref[1, big, :]
    all_r2 = jnp.dot(lhs_ref[0, big, :], rhs_ref[0], preferred_element_type=F32)
    all_sf = jnp.dot(left, rhs_ref[1], preferred_element_type=F32)
    all_sg = jnp.dot(left, rhs_ref[2], preferred_element_type=F32)
    for s in range(0, rows, sub):
        sl = slice(base + s, base + s + sub)
        q = slice(s, s + sub)
        inv = 1.0 / all_r2[q]
        sf = all_sf[q]
        sg = all_sg[q]
        inv3 = inv * inv * inv
        lf = inv3 * sf
        lg = inv3 * sg
        rad = inv * (lf * sf + lg * sg)
        for j, v in ((0, lf), (2, rad)):
            h = v.astype(BF)
            l_ref[j, sl, :] = h
            l_ref[j + 1, sl, :] = (v - h.astype(F32)).astype(BF)
        for t in range(0, sub, 8):
            o = slice(t, t + 8)
            so = slice(base + s + t, base + s + t + 8)
            cs = cs + lg[o]
            x_ref[3, so, :] = half(lf[o])
            for k in range(3):
                x_ref[k, so, :] = half(lg[o] * n[k])
    return cs


def along(w, tile):
    return lax.dot_general(w, tile, (((1,), (0,)), ((), ())), preferred_element_type=F32)


def across(w, tile):
    return lax.dot_general(w, tile, (((1,), (1,)), ((), ())), preferred_element_type=F32)


def stage(h, now, before, ws, ks, load, save, rows=128, sub=16):
    lhs, rhs, w, keep, tiles, x, csr = now
    w_b, keep_b, tiles_b, x_b, csr_b = before[2:]
    ws[...] = w_b[...]
    ks[...] = keep_b[...]
    normal = [wide(keep[3, k : k + 1, :]) for k in range(3)]
    cs = jnp.zeros((8, C), F32)
    xs = [[None, None] for _ in range(4)]
    col = []
    rsum = []
    count = C // rows
    for c in range(count):
        cs = terms(c * rows, rows, sub, normal, cs, lhs, rhs, tiles, x)
        for e in range(c * 8 // count, (c + 1) * 8 // count):
            k, s = e // 2, e % 2
            xs[k][s] = jnp.sum(x_b[k, s * 128 : (s + 1) * 128, :].T, axis=0, keepdims=True)
            if e < 4:
                col.append(along(ws[e // 2], tiles_b[e]))
            elif e < 6:
                rsum.append(across(ws[2], tiles_b[e - 2]))
        if c == count // 2 - 1:
            prep(*load(h + 1), *before[:4])
    csr_old = csr_b[...]
    csr[...] = cs
    row = row_index()
    ct = (col[0] + col[1]) + (col[2] + col[3])
    rt = rsum[0] + rsum[1]
    ct = ct[0:8] + ct[8:16]
    rt = rt[0:8] + rt[8:16]
    nf, pf, iaf, ng, pg, iag = (ks[i] for i in range(6))
    xv = [wide(jnp.concatenate(v, axis=1)) for v in xs]
    lean = jnp.where(row == 0, xv[0], jnp.where(row == 1, xv[1], xv[2]))
    gf = 2.0 * (nf * xv[3] + lean) + iaf * (rt + pf * wide(rt[3:4]))
    csum = wide(jnp.sum(csr_old, axis=0, keepdims=True))
    gg = -(ct + ng * (2.0 * csum) + iag * (pltpu.roll(ct, 5, 0) + pg * wide(ct[6:7])))
    save(h - 1, gf, gg)


STAGE = [
    pltpu.VMEM((2, C, 48), BF),
    pltpu.VMEM((3, 48, C), BF),
    pltpu.VMEM((3, 16, C), BF),
    pltpu.VMEM((6, 8, C), F32),
    pltpu.VMEM((4, C, C), BF),
    pltpu.VMEM((4, C, 128), F32),
    pltpu.VMEM((8, C), F32),
]
KEPT = [pltpu.VMEM((3, 16, C), BF), pltpu.VMEM((6, 8, C), F32)]


def lanes(c):
    return pl.ds(pl.multiple_of(c * C, C), C)


def place(flat):
    inner = lax.axis_size("gy")
    total = lax.axis_size("gx") * inner
    flat = (flat + total) % total
    return (flat // inner, flat % inner)


def position():
    return lax.axis_index("gx") * lax.axis_size("gy") + lax.axis_index("gy")


def around(me):
    total = lax.axis_size("gx") * lax.axis_size("gy")
    odd = me % 2
    above = (2 * total - 3 - me) // total
    below = (me + total - 2) // total
    return above, below, odd * above + (1 - odd) * below


def greet(always, maybe, there):
    barrier = pltpu.get_barrier_semaphore()

    def tell(device):
        pl.semaphore_signal(barrier, inc=1, device_id=device, device_id_type=MESH)

    tell(always)
    for device, yes in zip(maybe, there, strict=True):
        pl.when(yes == 1)(functools.partial(tell, device))
    pl.semaphore_wait(barrier, 1 + there[0] + there[1] + there[2])


def sort_out(positions, normals, areas, pair_first, pair_second, pair_count):
    faces = positions.shape[1]
    clusters = faces // C

    def kernel(pos_in, nor_in, area_in, pf, ps, count, out, lists, pos, nor, area, geometry, sem):
        copies = [
            pltpu.make_async_copy(src, dst, sem.at[k])
            for k, (src, dst) in enumerate(((pos_in, pos), (nor_in, nor), (area_in, area)))
        ]
        for c in copies:
            c.start()
        me = position()
        odd = me % 2

        def clear(i, carry):
            lists[i] = 0
            lists[ROW + i] = 0
            return carry

        lax.fori_loop(0, INSIDE + LATE + 2, clear, 0)
        for k in range(6):
            lists[COUNTS + k] = 0
        live = count[0]

        def one(j):
            s = ps[j]
            h = s // clusters - me
            outer = jnp.where(h == 2, 4, 2)
            inner = jnp.where(h == 1 - 2 * odd, 1, 3)
            k = jnp.where(h == 0, 0, jnp.where(jnp.abs(h) == 2, outer, inner))
            k = jnp.where(j < live, k, 5)
            n = lists[COUNTS + k]
            lists[k * ROW + n] = (pf[j] - me * clusters) * clusters + s % clusters
            lists[COUNTS + k] = n + 1

        def step(i, carry):
            for u in range(4):
                one(4 * i + u)
            return carry

        steps = (live + 3) // 4
        lax.fori_loop(0, steps // 2, step, 0)
        for c in copies:
            c.wait()
        for c in range(clusters):
            sl = slice(c * C, (c + 1) * C)
            geometry[c, 0:3, :] = pos[:, sl]
            geometry[c, 3:6, :] = nor[:, sl]
            geometry[c, 6:7, :] = area[:, sl]
            geometry[c, 7:8, :] = jnp.zeros((1, C), F32)
        leave = pltpu.make_async_copy(geometry, out, sem.at[3])
        leave.start()
        lax.fori_loop(steps // 2, steps, step, 0)
        leave.wait()

    hbm = pl.BlockSpec(memory_space=pl.ANY)
    smem = pl.BlockSpec(memory_space=pltpu.SMEM)
    return pl.pallas_call(
        kernel,
        out_shape=[jax.ShapeDtypeStruct((clusters, 8, C), F32), jax.ShapeDtypeStruct((NUMBERS,), jnp.int32)],
        in_specs=[hbm] * 3 + [smem] * 3,
        out_specs=[hbm, smem],
        scratch_shapes=[
            pltpu.VMEM((3, faces), F32),
            pltpu.VMEM((3, faces), F32),
            pltpu.VMEM((1, faces), F32),
            pltpu.VMEM((clusters, 8, C), F32),
            pltpu.SemaphoreType.DMA((4,)),
        ],
        compiler_params=pltpu.CompilerParams(vmem_limit_bytes=VMEM_LIMIT),
    )(positions, normals, areas.reshape(1, faces), pair_first, pair_second, pair_count)


def gather(geometry, lists, rows=7, chunks=4):
    clusters = geometry.shape[0]
    part = clusters // chunks

    def kernel(own, lists, told, low, far, sib, high, made, lo, fa, hi, second, near, seen, *refs):
        even, odds = refs[:7], refs[7:14]
        ws, ks, send, recv, fetch, news_send, news_recv, hop_send, hop_recv = refs[14:]
        me = position()
        odd = me % 2
        up, down, other = place(me + 2), place(me - 2), place(me + 1 - 2 * odd)
        away = place(me - 1 + 2 * odd)
        mine = pltpu.make_async_copy(own, near, fetch.at[0])
        mine.start()
        again = pltpu.make_async_copy(own, seen.at[pl.ds(0, clusters)], fetch.at[2])
        again.start()
        there = around(me)
        greet(other, (up, down, away), there)
        above, below, beyond = (yes == 1 for yes in there)

        def move(kind, i, src, dst, device):
            sl = (pl.ds(i * part, part), pl.ds(0, rows))
            return pltpu.make_async_remote_copy(
                src_ref=src.at[sl],
                dst_ref=dst.at[sl],
                send_sem=send.at[kind, i],
                recv_sem=recv.at[kind, i],
                device_id=device,
                device_id_type=MESH,
            )

        news = [
            pltpu.make_async_remote_copy(
                src_ref=told,
                dst_ref=dst,
                send_sem=news_send.at[k],
                recv_sem=news_recv.at[k],
                device_id=device,
                device_id_type=MESH,
            )
            for k, (dst, device) in enumerate(((lo, up), (fa, away), (hi, down)))
        ]
        for c, yes in zip(news, (above, beyond, below), strict=True):
            pl.when(yes)(c.start)
        @pl.when(above)
        def _():
            for i in range(chunks):
                move(0, i, own, low, up).start()

        @pl.when(below)
        def _():
            for i in range(chunks):
                move(1, i, own, high, down).start()

        for i in range(chunks):
            move(2, i, own, sib, other).start()
        mine.wait()

        def load(h):
            v = lists[ROW + jnp.minimum(h, EARLY) - INSIDE]
            return seen[v // clusters], seen[clusters + v % clusters]

        def save(h, gf, gg):
            made[h + 1, 0] = gf
            made[h + 1, 1] = gg

        def step(i, carry):
            stage(2 * i, even, odds, ws, ks, load, save)
            stage(2 * i + 1, odds, even, ws, ks, load, save)
            return carry

        def fresh(h):
            v = lists[h]
            return near[v // clusters], near[v % clusters]

        def inner(i, carry):
            stage(2 * i, even, odds, ws, ks, fresh, save)
            stage(2 * i + 1, odds, even, ws, ks, fresh, save)
            return carry

        prep(*fresh(0), *even[:4])
        lead = (INSIDE - 1) // 2
        lax.fori_loop(0, lead, inner, 0)
        pl.when(below)(news[0].wait_recv)
        pl.when(beyond)(news[1].wait_recv)
        pl.when(above)(news[2].wait_recv)
        tail = NUMBERS - COUNTS
        hops = [
            pltpu.make_async_remote_copy(
                src_ref=src.at[pl.ds(COUNTS, tail)],
                dst_ref=second.at[pl.ds(k * tail, tail)],
                send_sem=hop_send.at[k],
                recv_sem=hop_recv.at[k],
                device_id=device,
                device_id_type=MESH,
            )
            for k, (src, device) in enumerate(((lo, up), (fa, up), (lo, away), (hi, away), (fa, down), (hi, down)))
        ]
        going = (above, above, beyond, beyond, below, below)
        coming = (below, below, beyond, beyond, above, above)
        for c, yes in zip(hops, going, strict=True):
            pl.when(yes)(c.start)
        for i in range(chunks):
            move(2, i, own, sib, other).wait_recv()
        beside = pltpu.make_async_copy(sib, seen.at[pl.ds(clusters, clusters)], fetch.at[1])
        beside.start()
        again.wait()
        beside.wait()
        done = lead
        for i in range(chunks):
            lax.fori_loop(done, done + 3, step, 0)
            done += 3

            @pl.when(below)
            def _():
                move(0, i, own, low, up).wait_recv()

                @pl.when(odd == 1)
                def _():
                    move(3, i, low, far, other).start()

            @pl.when(above)
            def _():
                move(1, i, own, high, down).wait_recv()

                @pl.when(odd == 0)
                def _():
                    move(3, i, high, far, other).start()

        lax.fori_loop(done, (EARLY + 1) // 2, step, 0)

        @pl.when(beyond)
        def _():
            for i in range(chunks):
                move(3, i, own, far, other).wait_recv()

        @pl.when(((odd == 0) & above) | ((odd == 1) & below))
        def _():
            for i in range(chunks):
                move(3, i, own, far, other).wait_send()

        @pl.when(above)
        def _():
            for i in range(chunks):
                move(0, i, own, low, up).wait_send()

        @pl.when(below)
        def _():
            for i in range(chunks):
                move(1, i, own, high, down).wait_send()

        for i in range(chunks):
            move(2, i, own, sib, other).wait_send()
        for c, there_out in zip(news, (above, beyond, below), strict=True):
            pl.when(there_out)(c.wait_send)
        for c, there_in, there_out in zip(hops, coming, going, strict=True):
            pl.when(there_in)(c.wait_recv)
            pl.when(there_out)(c.wait_send)

    hbm = pl.BlockSpec(memory_space=pl.ANY)
    return pl.pallas_call(
        kernel,
        out_shape=[jax.ShapeDtypeStruct((clusters, 8, C), F32)] * 4
        + [jax.ShapeDtypeStruct((EARLY + 1, 2, 8, C), F32)]
        + [jax.ShapeDtypeStruct((NUMBERS,), jnp.int32)] * 3
        + [jax.ShapeDtypeStruct((6 * (NUMBERS - COUNTS),), jnp.int32)],
        in_specs=[hbm, pl.BlockSpec(memory_space=pltpu.SMEM), hbm],
        out_specs=[hbm] * 4 + [pl.BlockSpec(memory_space=pltpu.VMEM)] + [hbm] * 4,
        scratch_shapes=[pltpu.VMEM((clusters, 8, C), F32), pltpu.VMEM((2 * clusters, 8, C), F32)]
        + STAGE
        + STAGE
        + KEPT
        + [pltpu.SemaphoreType.DMA((4, chunks)), pltpu.SemaphoreType.DMA((4, chunks))]
        + [pltpu.SemaphoreType.DMA((3,))] * 3
        + [pltpu.SemaphoreType.DMA((6,))] * 2,
        compiler_params=pltpu.CompilerParams(
            collective_id=0, has_side_effects=True, vmem_limit_bytes=VMEM_LIMIT
        ),
    )(geometry, lists, lists)


def near_field(lists, news, geos, made):
    nwin = len(geos)
    clusters = geos[0].shape[0]

    def kernel(lists, lo, fa, hi, second, made, *refs):
        geo = refs[:nwin]
        acc, win, early = refs[nwin : nwin + 3]
        even = refs[nwin + 3 : nwin + 10]
        odd = refs[nwin + 10 : nwin + 17]
        ws, ks, work, sem = refs[nwin + 17 :]
        copies = [
            pltpu.make_async_copy(geo[k], win.at[pl.ds(k * clusters, clusters)], sem.at[k]) for k in range(nwin)
        ] + [pltpu.make_async_copy(made, early, sem.at[nwin])]
        for c in copies:
            c.start()

        def spare(ref, at=COUNTS):
            inside = jnp.maximum(ref[at] - INSIDE - LATE, 0)
            beside = jnp.maximum(ref[at + 1] - (EARLY - INSIDE), 0)
            return inside + beside + ref[at + 2] + ref[at + 3] + ref[at + 4]

        def quarter(v):
            return jnp.where(v >= 0, v // 4, 0 - (0 - v) // 4)

        def enlist(n, ref, k, start, stop, first_at, second_at):
            def put(j, carry):
                v = ref[k * ROW + j]
                work[n + j - start] = first_at * clusters + v // clusters
                work[2 * ROW + n + j - start] = second_at * clusters + v % clusters
                return carry

            lax.fori_loop(start, stop, put, 0)
            return n + jnp.maximum(stop - start, 0)

        work[0] = 0
        work[2 * ROW] = 0
        mine = spare(lists)
        n = enlist(0, lists, 0, INSIDE + LATE, lists[COUNTS], REACH, REACH)
        n = enlist(n, lists, 1, EARLY - INSIDE, lists[COUNTS + 1], REACH, REACH + 1)
        me = position()
        parity = me % 2
        total = lax.axis_size("gx") * lax.axis_size("gy")

        def there(d):
            return (d >= 0) & (d < total)

        def after(own, others):
            change = 0
            for d, r in others:
                change = change + jnp.where(there(d), quarter(own - r), 0)
            return own - change

        def hop(k):
            return spare(second, k * (NUMBERS - COUNTS))

        d_lo, d_fa, d_hi = me - 2, me - 1 + 2 * parity, me + 2
        r_lo, r_fa, r_hi = spare(lo), spare(fa), spare(hi)
        mine_after = after(mine, ((d_lo, r_lo), (d_fa, r_fa), (d_hi, r_hi)))
        lo_after = after(r_lo, ((me, mine), (d_lo - 2, hop(0)), (d_lo - 1 + 2 * parity, hop(1))))
        fa_after = after(r_fa, ((me, mine), (d_fa - 2, hop(2)), (d_fa + 2, hop(3))))
        hi_after = after(r_hi, ((me, mine), (d_hi - 1 + 2 * parity, hop(4)), (d_hi + 2, hop(5))))
        for ref, k, theirs, at, d, r, later in (
            (lo, 2, 4, 0, d_lo, r_lo, lo_after),
            (fa, 3, 3, 1, d_fa, r_fa, fa_after),
            (hi, 4, 2, 4, d_hi, r_hi, hi_after),
        ):
            more = quarter(mine - r) + quarter(mine_after - later)
            given = jnp.clip(more, 0, lists[COUNTS + k])
            taken = jnp.where(there(d), jnp.clip(0 - more, 0, ref[COUNTS + theirs]), 0)
            n = enlist(n, lists, k, given, lists[COUNTS + k], REACH, at)
            n = enlist(n, ref, theirs, 0, taken, at, REACH)
        acc[...] = jnp.zeros_like(acc)
        for c in copies:
            c.wait()
        last = jnp.maximum(n - 1, 0)

        def load(h):
            q = jnp.minimum(h, last)
            return win[work[q]], win[work[2 * ROW + q]]

        def save(h, gf, gg):
            live = (h >= 0) & (h < n)
            q = jnp.clip(h, 0, last)
            fi = work[q]
            si = work[2 * ROW + q]
            acc[fi] += jnp.where(live, gf, 0.0)
            acc[si] += jnp.where(live, gg, 0.0)

        prep(*load(0), *even[:4])

        def add(k, at, slot):
            def one(j, carry):
                v = lists[k * ROW + j]
                acc[REACH * clusters + v // clusters] += early[at + j, 0]
                acc[slot * clusters + v % clusters] += early[at + j, 1]
                return carry

            return one

        lax.fori_loop(0, jnp.minimum(lists[COUNTS], INSIDE), add(0, 1, REACH), 0)
        lax.fori_loop(0, jnp.minimum(lists[COUNTS + 1], EARLY - INSIDE), add(1, 1 + INSIDE, REACH + 1), 0)

        def step(i, carry):
            stage(2 * i, even, odd, ws, ks, load, save)
            stage(2 * i + 1, odd, even, ws, ks, load, save)
            return carry

        lax.fori_loop(0, (n + 2) // 2, step, 0)

    hbm = pl.BlockSpec(memory_space=pl.ANY)
    return pl.pallas_call(
        kernel,
        out_shape=jax.ShapeDtypeStruct((nwin * clusters, 8, C), F32),
        in_specs=[pl.BlockSpec(memory_space=pltpu.SMEM)] * 5 + [hbm] * (nwin + 1),
        out_specs=pl.BlockSpec(memory_space=pltpu.VMEM),
        scratch_shapes=[pltpu.VMEM((nwin * clusters, 8, C), F32)]
        + [pltpu.VMEM((EARLY + 1, 2, 8, C), F32)]
        + STAGE
        + STAGE
        + KEPT
        + [pltpu.SMEM((4 * ROW,), jnp.int32), pltpu.SemaphoreType.DMA((nwin + 1,))],
        compiler_params=pltpu.CompilerParams(vmem_limit_bytes=VMEM_LIMIT),
    )(lists, *news, made, *geos)


def give_back(sums, geometry, lists):
    clusters = geometry.shape[0]

    def kernel(sums, own, lists, *refs):
        boxes = refs[:4]
        made, seen = refs[4:6]
        even, odds = refs[6:13], refs[13:20]
        ws, ks, send, recv, fetch = refs[20:]
        me = position()
        odd = me % 2
        targets = (place(me - 2), place(me - 1 + 2 * odd), place(me + 1 - 2 * odd), place(me + 2))
        mine = pltpu.make_async_copy(own, seen, fetch.at[0])
        mine.start()
        there = around(me)
        greet(targets[2], (targets[3], targets[0], targets[1]), there)
        above, below, beyond = (yes == 1 for yes in there)
        copies = [
            pltpu.make_async_remote_copy(
                src_ref=sums.at[pl.ds(slot * clusters, clusters), pl.ds(0, 3)],
                dst_ref=boxes[k].at[:, pl.ds(0, 3)],
                send_sem=send.at[k],
                recv_sem=recv.at[k],
                device_id=device,
                device_id_type=MESH,
            )
            for k, (slot, device) in enumerate(zip((0, 1, 3, 4), targets, strict=True))
        ]
        pl.when(below)(copies[0].start)
        pl.when(above)(copies[3].start)
        pl.when(beyond)(copies[1].start)
        copies[2].start()
        mine.wait()

        def load(h):
            v = lists[INSIDE + jnp.minimum(h, LATE)]
            return seen[v // clusters], seen[v % clusters]

        def save(h, gf, gg):
            made[h + 1, 0] = gf
            made[h + 1, 1] = gg

        prep(*load(0), *even[:4])

        def step(i, carry):
            stage(2 * i, even, odds, ws, ks, load, save)
            stage(2 * i + 1, odds, even, ws, ks, load, save)
            return carry

        lax.fori_loop(0, (LATE + 1) // 2, step, 0)
        pl.when(below)(copies[0].wait_send)
        pl.when(above)(copies[0].wait_recv)
        pl.when(above)(copies[3].wait_send)
        pl.when(below)(copies[3].wait_recv)
        pl.when(beyond)(copies[1].wait)
        copies[2].wait()

    hbm = pl.BlockSpec(memory_space=pl.ANY)
    return pl.pallas_call(
        kernel,
        out_shape=[jax.ShapeDtypeStruct((clusters, 8, C), F32)] * 4
        + [jax.ShapeDtypeStruct((LATE + 1, 2, 8, C), F32)],
        in_specs=[hbm] * 2 + [pl.BlockSpec(memory_space=pltpu.SMEM)],
        out_specs=[hbm] * 4 + [pl.BlockSpec(memory_space=pltpu.VMEM)],
        scratch_shapes=[pltpu.VMEM((clusters, 8, C), F32)]
        + STAGE
        + STAGE
        + KEPT
        + [pltpu.SemaphoreType.DMA((4,)), pltpu.SemaphoreType.DMA((4,)), pltpu.SemaphoreType.DMA((1,))],
        compiler_params=pltpu.CompilerParams(
            collective_id=1, has_side_effects=True, vmem_limit_bytes=VMEM_LIMIT
        ),
    )(sums, geometry, lists)


def finish(sums, boxes, made, lists):
    clusters = boxes[0].shape[0]

    def kernel(lists, sums, b0, b1, b2, b3, made, out, held, sem):
        lay = pl.ds(0, 3)
        above, below, beyond = around(position())
        sources = [sums.at[pl.ds(REACH * clusters, clusters), lay]] + [b.at[:, lay] for b in (b0, b1, b2, b3)]
        copies = [
            pltpu.make_async_copy(src, held.at[pl.ds(k * clusters, clusters), lay], sem.at[k])
            for k, src in enumerate(sources)
        ]
        for c in copies:
            c.start()
        for c in copies:
            c.wait()

        def add(j, carry):
            v = lists[INSIDE + j]
            held[v // clusters] += made[j + 1, 0]
            held[v % clusters] += made[j + 1, 1]
            return carry

        lax.fori_loop(0, jnp.clip(lists[COUNTS] - INSIDE, 0, LATE), add, 0)
        for c in range(clusters):
            a, p0, p1, p2, p3 = (held[k * clusters + c] for k in range(5))
            p0, p1, p3 = (jnp.where(yes == 1, p, 0.0) for p, yes in ((p0, above), (p1, beyond), (p3, below)))
            out[:, c * C : (c + 1) * C] = (a + ((p0 + p3) + (p1 + p2)))[0:3]

    hbm = pl.BlockSpec(memory_space=pl.ANY)
    return pl.pallas_call(
        kernel,
        out_shape=jax.ShapeDtypeStruct((3, clusters * C), F32),
        in_specs=[pl.BlockSpec(memory_space=pltpu.SMEM)] + [hbm] * 5 + [pl.BlockSpec(memory_space=pltpu.VMEM)],
        out_specs=pl.BlockSpec(memory_space=pltpu.VMEM),
        scratch_shapes=[pltpu.VMEM((5 * clusters, 8, C), F32), pltpu.SemaphoreType.DMA((5,))],
        compiler_params=pltpu.CompilerParams(vmem_limit_bytes=VMEM_LIMIT),
    )(lists, sums, *boxes, made)


def body(positions, normals, areas, pair_first, pair_second, pair_count):
    geometry, lists = sort_out(positions, normals, areas, pair_first, pair_second, pair_count)
    low, far, sib, high, early, *news = gather(geometry, lists)
    sums = near_field(lists, news, [low, far, geometry, sib, high], early)
    *boxes, late = give_back(sums, geometry, lists)
    return finish(sums, boxes, late, lists)


def solution(mesh):
    flat = P(("gx", "gy"))
    deep = P(None, ("gx", "gy"))
    return jax.shard_map(
        body, mesh=mesh, in_specs=(deep, deep, flat, flat, flat, flat), out_specs=deep, check_vma=False
    )
```

```python
import functools

import jax
import jax.numpy as jnp
from jax import lax
from jax.experimental import pallas as pl
from jax.experimental.pallas import tpu as pltpu
from jax.sharding import PartitionSpec as P

C = 256
REACH = 2
F32 = jnp.float32
BF = jnp.bfloat16
MESH = pl.DeviceIdType.MESH
VMEM_LIMIT = 60 * 2**20
INSIDE = 9
EARLY = 35
LATE = 19
ROW = 128
COUNTS = 6 * ROW
NUMBERS = 8 * ROW


def split3(t):
    a = t.astype(BF).astype(F32)
    r = t - a
    b = r.astype(BF).astype(F32)
    return a, b, r - b


def split2(t):
    a = t.astype(BF).astype(F32)
    return a, t - a


def wide(v):
    return jnp.broadcast_to(v, (8, C))


def row_index():
    return lax.broadcasted_iota(jnp.int32, (8, C), 0)


def prep(f, g, lhs_ref, rhs_ref, w_ref, keep_ref):
    row = row_index()
    isp = row < 3

    def at(k, v):
        return jnp.where(row == k, v, 0.0)

    af = wide(f[6:7, :])
    ag = wide(g[6:7, :])
    ctr = jnp.where(isp, wide(jnp.sum(f, axis=1, keepdims=True) * (1.0 / C)), 0.0)

    def parts(t):
        p = jnp.where(isp, t - ctr, 0.0)
        n = jnp.where(isp, pltpu.roll(t, 5, 0), 0.0)
        return p, n, wide(jnp.sum(p * p, axis=0, keepdims=True)), wide(jnp.sum(p * n, axis=0, keepdims=True))

    pf, nf, sf, cf = parts(f)
    pg, ng, sg, cg = parts(g)
    iaf = 1.0 / af
    iag = 1.0 / ag

    def left(t):
        u0, u1, u2 = split3(t)
        return jnp.concatenate([u0, u0, u0, u1, u1, u2], axis=0).T.astype(BF)

    def right(t):
        u0, u1, u2 = split3(t)
        return jnp.concatenate([u0, u1, u2, u0, u1, u0], axis=0).astype(BF)

    lhs_ref[0] = left(pf + at(3, sf + 1.0) + at(4, 1.0))
    lhs_ref[1] = left(af * (nf + at(3, cf) + pltpu.roll(pf, 4, 0) + at(7, 1.0)))
    rhs_ref[0] = right(-2.0 * pg + at(3, 1.0) + at(4, sg))
    rhs_ref[1] = right(ag * (at(3, 1.0) - pg))
    rhs_ref[2] = right(ag * (pltpu.roll(ng, 4, 0) - at(7, cg)))
    sums = (2.0 * nf, iaf * (at(6, 6.0) - 6.0 * pltpu.roll(pf, 3, 0)), iag * (6.0 * pg - at(3, 6.0)))
    for j, v in enumerate(sums):
        w_ref[j] = jnp.concatenate(split2(v), axis=0).astype(BF)
    for i, v in enumerate((nf, pf, iaf, ng, pg, iag)):
        keep_ref[i] = v


def terms(base, rows, sub, n, cs, lhs_ref, rhs_ref, l_ref, x_ref):
    def half(v):
        return v[:, :128] + v[:, 128:]

    big = slice(base, base + rows)
    left = lhs_ref[1, big, :]
    all_r2 = jnp.dot(lhs_ref[0, big, :], rhs_ref[0], preferred_element_type=F32)
    all_sf = jnp.dot(left, rhs_ref[1], preferred_element_type=F32)
    all_sg = jnp.dot(left, rhs_ref[2], preferred_element_type=F32)
    for s in range(0, rows, sub):
        sl = slice(base + s, base + s + sub)
        q = slice(s, s + sub)
        inv = 1.0 / all_r2[q]
        sf = all_sf[q]
        sg = all_sg[q]
        inv3 = inv * inv * inv
        lf = inv3 * sf
        lg = inv3 * sg
        rad = inv * (lf * sf + lg * sg)
        for j, v in ((0, lf), (2, rad)):
            h = v.astype(BF)
            l_ref[j, sl, :] = h
            l_ref[j + 1, sl, :] = (v - h.astype(F32)).astype(BF)
        for t in range(0, sub, 8):
            o = slice(t, t + 8)
            so = slice(base + s + t, base + s + t + 8)
            cs = cs + lg[o]
            x_ref[3, so, :] = half(lf[o])
            for k in range(3):
                x_ref[k, so, :] = half(lg[o] * n[k])
    return cs


def along(w, tile):
    return lax.dot_general(w, tile, (((1,), (0,)), ((), ())), preferred_element_type=F32)


def across(w, tile):
    return lax.dot_general(w, tile, (((1,), (1,)), ((), ())), preferred_element_type=F32)


def stage(h, now, before, ws, ks, load, save, rows=128, sub=16):
    lhs, rhs, w, keep, tiles, x, csr = now
    w_b, keep_b, tiles_b, x_b, csr_b = before[2:]
    ws[...] = w_b[...]
    ks[...] = keep_b[...]
    normal = [wide(keep[3, k : k + 1, :]) for k in range(3)]
    cs = jnp.zeros((8, C), F32)
    xs = [[None, None] for _ in range(4)]
    col = []
    rsum = []
    count = C // rows
    for c in range(count):
        cs = terms(c * rows, rows, sub, normal, cs, lhs, rhs, tiles, x)
        for e in range(c * 8 // count, (c + 1) * 8 // count):
            k, s = e // 2, e % 2
            xs[k][s] = jnp.sum(x_b[k, s * 128 : (s + 1) * 128, :].T, axis=0, keepdims=True)
            if e < 4:
                col.append(along(ws[e // 2], tiles_b[e]))
            elif e < 6:
                rsum.append(across(ws[2], tiles_b[e - 2]))
        if c == count // 2 - 1:
            prep(*load(h + 1), *before[:4])
    csr_old = csr_b[...]
    csr[...] = cs
    row = row_index()
    ct = (col[0] + col[1]) + (col[2] + col[3])
    rt = rsum[0] + rsum[1]
    ct = ct[0:8] + ct[8:16]
    rt = rt[0:8] + rt[8:16]
    nf, pf, iaf, ng, pg, iag = (ks[i] for i in range(6))
    xv = [wide(jnp.concatenate(v, axis=1)) for v in xs]
    lean = jnp.where(row == 0, xv[0], jnp.where(row == 1, xv[1], xv[2]))
    gf = 2.0 * (nf * xv[3] + lean) + iaf * (rt + pf * wide(rt[3:4]))
    csum = wide(jnp.sum(csr_old, axis=0, keepdims=True))
    gg = -(ct + ng * (2.0 * csum) + iag * (pltpu.roll(ct, 5, 0) + pg * wide(ct[6:7])))
    save(h - 1, gf, gg)


STAGE = [
    pltpu.VMEM((2, C, 48), BF),
    pltpu.VMEM((3, 48, C), BF),
    pltpu.VMEM((3, 16, C), BF),
    pltpu.VMEM((6, 8, C), F32),
    pltpu.VMEM((4, C, C), BF),
    pltpu.VMEM((4, C, 128), F32),
    pltpu.VMEM((8, C), F32),
]
KEPT = [pltpu.VMEM((3, 16, C), BF), pltpu.VMEM((6, 8, C), F32)]


def lanes(c):
    return pl.ds(pl.multiple_of(c * C, C), C)


def place(flat):
    inner = lax.axis_size("gy")
    total = lax.axis_size("gx") * inner
    flat = (flat + total) % total
    return (flat // inner, flat % inner)


def position():
    return lax.axis_index("gx") * lax.axis_size("gy") + lax.axis_index("gy")


def around(me):
    total = lax.axis_size("gx") * lax.axis_size("gy")
    odd = me % 2
    above = (2 * total - 3 - me) // total
    below = (me + total - 2) // total
    return above, below, odd * above + (1 - odd) * below


def greet(always, maybe, there):
    barrier = pltpu.get_barrier_semaphore()

    def tell(device):
        pl.semaphore_signal(barrier, inc=1, device_id=device, device_id_type=MESH)

    tell(always)
    for device, yes in zip(maybe, there, strict=True):
        pl.when(yes == 1)(functools.partial(tell, device))
    pl.semaphore_wait(barrier, 1 + there[0] + there[1] + there[2])


def sort_out(positions, normals, areas, pair_first, pair_second, pair_count):
    faces = positions.shape[1]
    clusters = faces // C

    def kernel(pos, nor, area, pf, ps, count, geometry, lists):
        for c in range(clusters):
            sl = slice(c * C, (c + 1) * C)
            geometry[c, 0:3, :] = pos[:, sl]
            geometry[c, 3:6, :] = nor[:, sl]
            geometry[c, 6:7, :] = area[:, sl]
            geometry[c, 7:8, :] = jnp.zeros((1, C), F32)
        me = position()
        odd = me % 2

        def clear(i, carry):
            lists[i] = 0
            lists[ROW + i] = 0
            return carry

        lax.fori_loop(0, INSIDE + LATE + 2, clear, 0)
        for k in range(6):
            lists[COUNTS + k] = 0
        live = count[0]

        def one(j):
            s = ps[j]
            h = s // clusters - me
            outer = jnp.where(h == 2, 4, 2)
            inner = jnp.where(h == 1 - 2 * odd, 1, 3)
            k = jnp.where(h == 0, 0, jnp.where(jnp.abs(h) == 2, outer, inner))
            k = jnp.where(j < live, k, 5)
            n = lists[COUNTS + k]
            lists[k * ROW + n] = (pf[j] - me * clusters) * clusters + s % clusters
            lists[COUNTS + k] = n + 1

        def step(i, carry):
            for u in range(4):
                one(4 * i + u)
            return carry

        lax.fori_loop(0, (live + 3) // 4, step, 0)

    vmem = pl.BlockSpec(memory_space=pltpu.VMEM)
    smem = pl.BlockSpec(memory_space=pltpu.SMEM)
    return pl.pallas_call(
        kernel,
        out_shape=[jax.ShapeDtypeStruct((clusters, 8, C), F32), jax.ShapeDtypeStruct((NUMBERS,), jnp.int32)],
        in_specs=[vmem] * 3 + [smem] * 3,
        out_specs=[vmem, smem],
        compiler_params=pltpu.CompilerParams(vmem_limit_bytes=VMEM_LIMIT),
    )(positions, normals, areas.reshape(1, faces), pair_first, pair_second, pair_count)


def gather(geometry, lists, rows=7, chunks=4):
    clusters = geometry.shape[0]
    part = clusters // chunks

    def kernel(own, lists, told, low, far, sib, high, made, lo, fa, hi, second, near, seen, *refs):
        even, odds = refs[:7], refs[7:14]
        ws, ks, send, recv, fetch, news_send, news_recv, hop_send, hop_recv = refs[14:]
        me = position()
        odd = me % 2
        up, down, other = place(me + 2), place(me - 2), place(me + 1 - 2 * odd)
        away = place(me - 1 + 2 * odd)
        mine = pltpu.make_async_copy(own, near, fetch.at[0])
        mine.start()
        again = pltpu.make_async_copy(own, seen.at[pl.ds(0, clusters)], fetch.at[2])
        again.start()
        there = around(me)
        greet(other, (up, down, away), there)
        above, below, beyond = (yes == 1 for yes in there)

        def move(kind, i, src, dst, device):
            sl = (pl.ds(i * part, part), pl.ds(0, rows))
            return pltpu.make_async_remote_copy(
                src_ref=src.at[sl],
                dst_ref=dst.at[sl],
                send_sem=send.at[kind, i],
                recv_sem=recv.at[kind, i],
                device_id=device,
                device_id_type=MESH,
            )

        news = [
            pltpu.make_async_remote_copy(
                src_ref=told,
                dst_ref=dst,
                send_sem=news_send.at[k],
                recv_sem=news_recv.at[k],
                device_id=device,
                device_id_type=MESH,
            )
            for k, (dst, device) in enumerate(((lo, up), (fa, away), (hi, down)))
        ]
        for c, yes in zip(news, (above, beyond, below), strict=True):
            pl.when(yes)(c.start)
        @pl.when(above)
        def _():
            for i in range(chunks):
                move(0, i, own, low, up).start()

        @pl.when(below)
        def _():
            for i in range(chunks):
                move(1, i, own, high, down).start()

        for i in range(chunks):
            move(2, i, own, sib, other).start()
        mine.wait()

        def load(h):
            v = lists[ROW + jnp.minimum(h, EARLY) - INSIDE]
            return seen[v // clusters], seen[clusters + v % clusters]

        def save(h, gf, gg):
            made[h + 1, 0] = gf
            made[h + 1, 1] = gg

        def step(i, carry):
            stage(2 * i, even, odds, ws, ks, load, save)
            stage(2 * i + 1, odds, even, ws, ks, load, save)
            return carry

        def fresh(h):
            v = lists[h]
            return near[v // clusters], near[v % clusters]

        def inner(i, carry):
            stage(2 * i, even, odds, ws, ks, fresh, save)
            stage(2 * i + 1, odds, even, ws, ks, fresh, save)
            return carry

        prep(*fresh(0), *even[:4])
        lead = (INSIDE - 1) // 2
        lax.fori_loop(0, lead, inner, 0)
        pl.when(below)(news[0].wait_recv)
        pl.when(beyond)(news[1].wait_recv)
        pl.when(above)(news[2].wait_recv)
        tail = NUMBERS - COUNTS
        hops = [
            pltpu.make_async_remote_copy(
                src_ref=src.at[pl.ds(COUNTS, tail)],
                dst_ref=second.at[pl.ds(k * tail, tail)],
                send_sem=hop_send.at[k],
                recv_sem=hop_recv.at[k],
                device_id=device,
                device_id_type=MESH,
            )
            for k, (src, device) in enumerate(((lo, up), (fa, up), (lo, away), (hi, away), (fa, down), (hi, down)))
        ]
        going = (above, above, beyond, beyond, below, below)
        coming = (below, below, beyond, beyond, above, above)
        for c, yes in zip(hops, going, strict=True):
            pl.when(yes)(c.start)
        for i in range(chunks):
            move(2, i, own, sib, other).wait_recv()
        beside = pltpu.make_async_copy(sib, seen.at[pl.ds(clusters, clusters)], fetch.at[1])
        beside.start()
        again.wait()
        beside.wait()
        done = lead
        for i in range(chunks):
            lax.fori_loop(done, done + 3, step, 0)
            done += 3

            @pl.when(below)
            def _():
                move(0, i, own, low, up).wait_recv()

                @pl.when(odd == 1)
                def _():
                    move(3, i, low, far, other).start()

            @pl.when(above)
            def _():
                move(1, i, own, high, down).wait_recv()

                @pl.when(odd == 0)
                def _():
                    move(3, i, high, far, other).start()

        lax.fori_loop(done, (EARLY + 1) // 2, step, 0)

        @pl.when(beyond)
        def _():
            for i in range(chunks):
                move(3, i, own, far, other).wait_recv()

        @pl.when(((odd == 0) & above) | ((odd == 1) & below))
        def _():
            for i in range(chunks):
                move(3, i, own, far, other).wait_send()

        @pl.when(above)
        def _():
            for i in range(chunks):
                move(0, i, own, low, up).wait_send()

        @pl.when(below)
        def _():
            for i in range(chunks):
                move(1, i, own, high, down).wait_send()

        for i in range(chunks):
            move(2, i, own, sib, other).wait_send()
        for c, there_out in zip(news, (above, beyond, below), strict=True):
            pl.when(there_out)(c.wait_send)
        for c, there_in, there_out in zip(hops, coming, going, strict=True):
            pl.when(there_in)(c.wait_recv)
            pl.when(there_out)(c.wait_send)

    hbm = pl.BlockSpec(memory_space=pl.ANY)
    return pl.pallas_call(
        kernel,
        out_shape=[jax.ShapeDtypeStruct((clusters, 8, C), F32)] * 4
        + [jax.ShapeDtypeStruct((EARLY + 1, 2, 8, C), F32)]
        + [jax.ShapeDtypeStruct((NUMBERS,), jnp.int32)] * 3
        + [jax.ShapeDtypeStruct((6 * (NUMBERS - COUNTS),), jnp.int32)],
        in_specs=[hbm, pl.BlockSpec(memory_space=pltpu.SMEM), hbm],
        out_specs=[hbm] * 4 + [pl.BlockSpec(memory_space=pltpu.VMEM)] + [hbm] * 4,
        scratch_shapes=[pltpu.VMEM((clusters, 8, C), F32), pltpu.VMEM((2 * clusters, 8, C), F32)]
        + STAGE
        + STAGE
        + KEPT
        + [pltpu.SemaphoreType.DMA((4, chunks)), pltpu.SemaphoreType.DMA((4, chunks))]
        + [pltpu.SemaphoreType.DMA((3,))] * 3
        + [pltpu.SemaphoreType.DMA((6,))] * 2,
        compiler_params=pltpu.CompilerParams(
            collective_id=0, has_side_effects=True, vmem_limit_bytes=VMEM_LIMIT
        ),
    )(geometry, lists, lists)


def near_field(lists, news, geos, made):
    nwin = len(geos)
    clusters = geos[0].shape[0]

    def kernel(lists, lo, fa, hi, second, made, *refs):
        geo = refs[:nwin]
        acc, win, early = refs[nwin : nwin + 3]
        even = refs[nwin + 3 : nwin + 10]
        odd = refs[nwin + 10 : nwin + 17]
        ws, ks, work, sem = refs[nwin + 17 :]
        copies = [
            pltpu.make_async_copy(geo[k], win.at[pl.ds(k * clusters, clusters)], sem.at[k]) for k in range(nwin)
        ] + [pltpu.make_async_copy(made, early, sem.at[nwin])]
        for c in copies:
            c.start()

        def spare(ref, at=COUNTS):
            inside = jnp.maximum(ref[at] - INSIDE - LATE, 0)
            beside = jnp.maximum(ref[at + 1] - (EARLY - INSIDE), 0)
            return inside + beside + ref[at + 2] + ref[at + 3] + ref[at + 4]

        def quarter(v):
            return jnp.where(v >= 0, v // 4, 0 - (0 - v) // 4)

        def enlist(n, ref, k, start, stop, first_at, second_at):
            def put(j, carry):
                v = ref[k * ROW + j]
                work[n + j - start] = first_at * clusters + v // clusters
                work[2 * ROW + n + j - start] = second_at * clusters + v % clusters
                return carry

            lax.fori_loop(start, stop, put, 0)
            return n + jnp.maximum(stop - start, 0)

        work[0] = 0
        work[2 * ROW] = 0
        mine = spare(lists)
        n = enlist(0, lists, 0, INSIDE + LATE, lists[COUNTS], REACH, REACH)
        n = enlist(n, lists, 1, EARLY - INSIDE, lists[COUNTS + 1], REACH, REACH + 1)
        me = position()
        parity = me % 2
        total = lax.axis_size("gx") * lax.axis_size("gy")

        def there(d):
            return (d >= 0) & (d < total)

        def after(own, others):
            change = 0
            for d, r in others:
                change = change + jnp.where(there(d), quarter(own - r), 0)
            return own - change

        def hop(k):
            return spare(second, k * (NUMBERS - COUNTS))

        d_lo, d_fa, d_hi = me - 2, me - 1 + 2 * parity, me + 2
        r_lo, r_fa, r_hi = spare(lo), spare(fa), spare(hi)
        mine_after = after(mine, ((d_lo, r_lo), (d_fa, r_fa), (d_hi, r_hi)))
        lo_after = after(r_lo, ((me, mine), (d_lo - 2, hop(0)), (d_lo - 1 + 2 * parity, hop(1))))
        fa_after = after(r_fa, ((me, mine), (d_fa - 2, hop(2)), (d_fa + 2, hop(3))))
        hi_after = after(r_hi, ((me, mine), (d_hi - 1 + 2 * parity, hop(4)), (d_hi + 2, hop(5))))
        for ref, k, theirs, at, d, r, later in (
            (lo, 2, 4, 0, d_lo, r_lo, lo_after),
            (fa, 3, 3, 1, d_fa, r_fa, fa_after),
            (hi, 4, 2, 4, d_hi, r_hi, hi_after),
        ):
            more = quarter(mine - r) + quarter(mine_after - later)
            given = jnp.clip(more, 0, lists[COUNTS + k])
            taken = jnp.where(there(d), jnp.clip(0 - more, 0, ref[COUNTS + theirs]), 0)
            n = enlist(n, lists, k, given, lists[COUNTS + k], REACH, at)
            n = enlist(n, ref, theirs, 0, taken, at, REACH)
        acc[...] = jnp.zeros_like(acc)
        for c in copies:
            c.wait()
        last = jnp.maximum(n - 1, 0)

        def load(h):
            q = jnp.minimum(h, last)
            return win[work[q]], win[work[2 * ROW + q]]

        def save(h, gf, gg):
            live = (h >= 0) & (h < n)
            q = jnp.clip(h, 0, last)
            fi = work[q]
            si = work[2 * ROW + q]
            acc[fi] += jnp.where(live, gf, 0.0)
            acc[si] += jnp.where(live, gg, 0.0)

        prep(*load(0), *even[:4])

        def add(k, at, slot):
            def one(j, carry):
                v = lists[k * ROW + j]
                acc[REACH * clusters + v // clusters] += early[at + j, 0]
                acc[slot * clusters + v % clusters] += early[at + j, 1]
                return carry

            return one

        lax.fori_loop(0, jnp.minimum(lists[COUNTS], INSIDE), add(0, 1, REACH), 0)
        lax.fori_loop(0, jnp.minimum(lists[COUNTS + 1], EARLY - INSIDE), add(1, 1 + INSIDE, REACH + 1), 0)

        def step(i, carry):
            stage(2 * i, even, odd, ws, ks, load, save)
            stage(2 * i + 1, odd, even, ws, ks, load, save)
            return carry

        lax.fori_loop(0, (n + 2) // 2, step, 0)

    hbm = pl.BlockSpec(memory_space=pl.ANY)
    return pl.pallas_call(
        kernel,
        out_shape=jax.ShapeDtypeStruct((nwin * clusters, 8, C), F32),
        in_specs=[pl.BlockSpec(memory_space=pltpu.SMEM)] * 5 + [hbm] * (nwin + 1),
        out_specs=pl.BlockSpec(memory_space=pltpu.VMEM),
        scratch_shapes=[pltpu.VMEM((nwin * clusters, 8, C), F32)]
        + [pltpu.VMEM((EARLY + 1, 2, 8, C), F32)]
        + STAGE
        + STAGE
        + KEPT
        + [pltpu.SMEM((4 * ROW,), jnp.int32), pltpu.SemaphoreType.DMA((nwin + 1,))],
        compiler_params=pltpu.CompilerParams(vmem_limit_bytes=VMEM_LIMIT),
    )(lists, *news, made, *geos)


def give_back(sums, geometry, lists):
    clusters = geometry.shape[0]

    def kernel(sums, own, lists, *refs):
        boxes = refs[:4]
        made, seen = refs[4:6]
        even, odds = refs[6:13], refs[13:20]
        ws, ks, send, recv, fetch = refs[20:]
        me = position()
        odd = me % 2
        targets = (place(me - 2), place(me - 1 + 2 * odd), place(me + 1 - 2 * odd), place(me + 2))
        mine = pltpu.make_async_copy(own, seen, fetch.at[0])
        mine.start()
        there = around(me)
        greet(targets[2], (targets[3], targets[0], targets[1]), there)
        above, below, beyond = (yes == 1 for yes in there)
        copies = [
            pltpu.make_async_remote_copy(
                src_ref=sums.at[pl.ds(slot * clusters, clusters), pl.ds(0, 3)],
                dst_ref=boxes[k].at[:, pl.ds(0, 3)],
                send_sem=send.at[k],
                recv_sem=recv.at[k],
                device_id=device,
                device_id_type=MESH,
            )
            for k, (slot, device) in enumerate(zip((0, 1, 3, 4), targets, strict=True))
        ]
        pl.when(below)(copies[0].start)
        pl.when(above)(copies[3].start)
        pl.when(beyond)(copies[1].start)
        copies[2].start()
        mine.wait()

        def load(h):
            v = lists[INSIDE + jnp.minimum(h, LATE)]
            return seen[v // clusters], seen[v % clusters]

        def save(h, gf, gg):
            made[h + 1, 0] = gf
            made[h + 1, 1] = gg

        prep(*load(0), *even[:4])

        def step(i, carry):
            stage(2 * i, even, odds, ws, ks, load, save)
            stage(2 * i + 1, odds, even, ws, ks, load, save)
            return carry

        lax.fori_loop(0, (LATE + 1) // 2, step, 0)
        pl.when(below)(copies[0].wait_send)
        pl.when(above)(copies[0].wait_recv)
        pl.when(above)(copies[3].wait_send)
        pl.when(below)(copies[3].wait_recv)
        pl.when(beyond)(copies[1].wait)
        copies[2].wait()

    hbm = pl.BlockSpec(memory_space=pl.ANY)
    return pl.pallas_call(
        kernel,
        out_shape=[jax.ShapeDtypeStruct((clusters, 8, C), F32)] * 4
        + [jax.ShapeDtypeStruct((LATE + 1, 2, 8, C), F32)],
        in_specs=[hbm] * 2 + [pl.BlockSpec(memory_space=pltpu.SMEM)],
        out_specs=[hbm] * 4 + [pl.BlockSpec(memory_space=pltpu.VMEM)],
        scratch_shapes=[pltpu.VMEM((clusters, 8, C), F32)]
        + STAGE
        + STAGE
        + KEPT
        + [pltpu.SemaphoreType.DMA((4,)), pltpu.SemaphoreType.DMA((4,)), pltpu.SemaphoreType.DMA((1,))],
        compiler_params=pltpu.CompilerParams(
            collective_id=1, has_side_effects=True, vmem_limit_bytes=VMEM_LIMIT
        ),
    )(sums, geometry, lists)


def finish(sums, boxes, made, lists):
    clusters = boxes[0].shape[0]

    def kernel(lists, sums, b0, b1, b2, b3, made, out, held, sem):
        lay = pl.ds(0, 3)
        above, below, beyond = around(position())
        sources = [sums.at[pl.ds(REACH * clusters, clusters), lay]] + [b.at[:, lay] for b in (b0, b1, b2, b3)]
        copies = [
            pltpu.make_async_copy(src, held.at[pl.ds(k * clusters, clusters), lay], sem.at[k])
            for k, src in enumerate(sources)
        ]
        for c in copies:
            c.start()
        for c in copies:
            c.wait()

        def add(j, carry):
            v = lists[INSIDE + j]
            held[v // clusters] += made[j + 1, 0]
            held[v % clusters] += made[j + 1, 1]
            return carry

        lax.fori_loop(0, jnp.clip(lists[COUNTS] - INSIDE, 0, LATE), add, 0)
        for c in range(clusters):
            a, p0, p1, p2, p3 = (held[k * clusters + c] for k in range(5))
            p0, p1, p3 = (jnp.where(yes == 1, p, 0.0) for p, yes in ((p0, above), (p1, beyond), (p3, below)))
            out[:, c * C : (c + 1) * C] = (a + ((p0 + p3) + (p1 + p2)))[0:3]

    hbm = pl.BlockSpec(memory_space=pl.ANY)
    return pl.pallas_call(
        kernel,
        out_shape=jax.ShapeDtypeStruct((3, clusters * C), F32),
        in_specs=[pl.BlockSpec(memory_space=pltpu.SMEM)] + [hbm] * 5 + [pl.BlockSpec(memory_space=pltpu.VMEM)],
        out_specs=pl.BlockSpec(memory_space=pltpu.VMEM),
        scratch_shapes=[pltpu.VMEM((5 * clusters, 8, C), F32), pltpu.SemaphoreType.DMA((5,))],
        compiler_params=pltpu.CompilerParams(vmem_limit_bytes=VMEM_LIMIT),
    )(lists, sums, *boxes, made)


def body(positions, normals, areas, pair_first, pair_second, pair_count):
    geometry, lists = sort_out(positions, normals, areas, pair_first, pair_second, pair_count)
    low, far, sib, high, early, *news = gather(geometry, lists)
    sums = near_field(lists, news, [low, far, geometry, sib, high], early)
    *boxes, late = give_back(sums, geometry, lists)
    return finish(sums, boxes, late, lists)


def solution(mesh):
    flat = P(("gx", "gy"))
    deep = P(None, ("gx", "gy"))
    return jax.shard_map(
        body, mesh=mesh, in_specs=(deep, deep, flat, flat, flat, flat), out_specs=deep, check_vma=False
    )
```
